32 devices in a mesh: sub: 16 (over z, y, core), rhs: 2 (over x).
Axes of the slice: x: 2, y: 2, z: 4, core: 2. Of those that a mesh axis runs over, the one named last changes fastest.
Arguments:
- right_side: float32 [64, 8192], P('rhs', 'sub'), may hold values from -6 to 6
- stiffness_blocks: float32 [128, 27, 4096], P('sub'), may hold values from -0.15625 to 0.15625
- block_columns: int32 [128, 27], P('sub'), may hold values from 0 to 15
- interface_rows: int32 [16, 2, 4], P('sub'), may hold values from 0 to 7, as said below
- corner_owner: int32 [16, 8], P('sub'), may hold values from 0 to 31, as said below
- corner_basis: float32 [8, 8192], P('rhs', 'sub'), may hold values from -0.25 to 0.25
- jacobi_scale: float32 [8192], P('sub'), may hold values from 0.5 to 2
- coarse_inverse: float32 [32, 32], replicated, as said below
Outputs:
- solution_field: float32 [64, 8192], P('rhs', 'sub')
- residual: float32 [64, 8192], P('rhs', 'sub')
The draws below stay inside these ranges and needn't reach their ends.
Inputs may be any that keep to these rules, and one draw needn't show every extreme that they name: `interface_rows`: the 8 block rows named for one subdomain are distinct. `corner_owner`: corner j of subdomain s names a coarse unknown between (s - 1) * 2 and (s + 2) * 2 - 1, within range; corner 0 names s * 2, corner 8 - 1 names s * 2 + 1. `coarse_inverse`: symmetric and positive definite.
All inputs are finite; a program needn't handle non-finite values.
Results may differ from the reference program's by a relative error of at most 0.0003.
Values sent between devices are 32-bit elements; how exact they have to be, the bound alone decides.
No kernel may reach another device: no remote copies, remote signals or barrier semaphores. Data moves between devices by JAX's collectives and lax.ppermute only.
A program may use at most 64 MiB of HBM per device.

```python
import math
import jax
import jax.numpy as jnp
from jax import lax

B = 64
KNZ = 27
NB = 8
IFB = 4
NCL = 8
NC_DEV = 2
ITERS = 2
NE = 16
NBT = 128
NTOT = 8192
CASES = 64
NCG = 32


def draw_interface_rows(key, part):
    count = NBT // NB
    scores = jax.random.randint(key, (count, NB), 0, 1048576)
    distinct = scores * NB + jnp.arange(NB, dtype=jnp.int32)[None, :]
    order = jnp.argsort(distinct, axis=1)[:, :2 * IFB]
    return order.reshape(count, 2, IFB).astype(jnp.int32)


def draw_corner_owner(key, part):
    count = NCG // NC_DEV
    base = (jnp.arange(count, dtype=jnp.int32) * NC_DEV)[:, None]
    offsets = jax.random.randint(key, (count, NCL), -NC_DEV, 2 * NC_DEV)
    owner = jnp.clip(base + offsets, 0, NCG - 1)
    owner = owner.at[:, 0].set(base[:, 0])
    owner = owner.at[:, NCL - 1].set(base[:, 0] + NC_DEV - 1)
    return owner.astype(jnp.int32)


def draw_coarse_inverse(key, part):
    key_off = jax.random.fold_in(key, 11)
    key_diag = jax.random.fold_in(key, 12)
    key_dense = jax.random.fold_in(key, 13)
    index = jnp.arange(NCG, dtype=jnp.int32)
    gap = jnp.abs(index[:, None] - index[None, :])
    band = ((gap <= 8) & (gap > 0)).astype(jnp.float32)
    raw = 0.06 * jnp.clip(jax.random.normal(key_off, (NCG, NCG), jnp.float32), -2.0, 2.0)
    factor = jnp.clip(jax.random.normal(key_dense, (NCG, NCG), jnp.float32), -3.0, 3.0)
    symmetric = 0.5 * (raw + raw.T) * band
    diagonal = jax.random.uniform(key_diag, (NCG,), jnp.float32, 2.0, 3.0)
    product = jnp.dot(factor, factor.T, precision=lax.Precision.HIGHEST) / NCG
    dense = 0.5 * (product + product.T)
    return symmetric + jnp.diag(diagonal) + dense


def with_ends(values, stream_key, low, largest):
    extent = values.shape
    index_at = [jax.random.randint(jax.random.fold_in(stream_key, axis), (), 0, extent[axis]) for axis in range(len(extent))]
    values = values.at[tuple(index_at)].set(low)
    longest = extent.index(max(extent))
    index_at[longest] = (index_at[longest] + 1) % extent[longest]
    return values.at[tuple(index_at)].set(largest)


def block_levels(stream_key, extent, cuts, low, largest):
    def one(dim, parts):
        draws = jax.random.uniform(jax.random.fold_in(jax.random.fold_in(stream_key, 6), dim), (parts,), jnp.float32, low / len(cuts), largest / len(cuts))
        return jnp.repeat(jnp.exp(draws), extent[dim] // parts).reshape((-1,) + (1,) * (len(extent) - dim - 1))

    factor_of = one(*cuts[0])
    for cut in cuts[1:]:
        factor_of = factor_of * one(*cut)
    return factor_of


def noise(stream_key, dims, deviation, limit, shards=(), kind=jnp.bfloat16):
    loudness = block_levels(stream_key, dims, shards, -0.22, 0.18) if shards else 1.0
    entries = jax.random.normal(stream_key, dims, jnp.float32) * deviation * loudness
    return jnp.minimum(jnp.maximum(entries, -limit), limit).astype(kind)


def setup_inputs(seed: int = 0) -> dict:
    key_of = jax.random.split(jax.random.key(seed), 9)
    right_side = noise(key_of[0], (CASES, NTOT), 1.0, 6.0, ((0, 2), (1, 16)), jnp.float32)
    stiffness_blocks = noise(key_of[1], (NBT, KNZ, B * B), (KNZ * B) ** -0.5, 0.15625, ((0, 16),), jnp.float32)
    block_columns = with_ends(jax.random.randint(key_of[2], (NBT, KNZ), 0, NE), jax.random.fold_in(key_of[2], 1), 0, NE - 1).astype(jnp.int32)
    interface_rows = draw_interface_rows(jax.random.fold_in(key_of[8], 71), 0)
    corner_owner = draw_corner_owner(jax.random.fold_in(key_of[8], 71), 0)
    corner_basis = noise(key_of[5], (NCL, NTOT), (NB * B) ** -0.5, 0.25, ((0, 2), (1, 16)), jnp.float32)
    jacobi_scale = jnp.clip(jnp.exp(math.log(2.0) - 1.3862944 * jax.random.uniform(key_of[6], (NTOT,), jnp.float32) ** block_levels(key_of[6], (NTOT,), ((0, 16),), -0.2, 0.2)), 0.5, 2.0)
    coarse_inverse = draw_coarse_inverse(jax.random.fold_in(key_of[8], 71), 0)
    return {"right_side": right_side, "stiffness_blocks": stiffness_blocks, "block_columns": block_columns, "interface_rows": interface_rows, "corner_owner": corner_owner, "corner_basis": corner_basis, "jacobi_scale": jacobi_scale, "coarse_inverse": coarse_inverse}


diag_shift = 1.0


def reference(right_side, stiffness_blocks, block_columns, interface_rows, corner_owner, corner_basis, jacobi_scale, coarse_inverse):
    highest = lax.Precision.HIGHEST
    nsub = NBT // NB
    nloc = NB * B
    rows = jnp.arange(NBT, dtype=jnp.int32)
    owner_sub = (rows // NB)[:, None]
    local = block_columns
    lower = jnp.clip(owner_sub - 1, 0, nsub - 1)
    upper = jnp.clip(owner_sub + 1, 0, nsub - 1)
    low_pos = jnp.clip(local - NB, 0, IFB - 1)
    up_pos = jnp.clip(local - NB - IFB, 0, IFB - 1)
    glob = jnp.where(local < NB, owner_sub * NB + local,
                     jnp.where(local < NB + IFB, lower * NB + interface_rows[lower, 1, low_pos],
                               upper * NB + interface_rows[upper, 0, up_pos])).astype(jnp.int32)
    live = ((local < NB) | ((local < NB + IFB) & (owner_sub > 0)) | ((local >= NB + IFB) & (owner_sub < nsub - 1))).astype(jnp.float32)
    blocks = stiffness_blocks.reshape(NBT, KNZ, B, B)

    def apply_operator(field):
        grid = field.reshape(CASES, NBT, B)

        def one_sub(acc, s):
            start = (s * NB).astype(jnp.int32)
            index = lax.dynamic_slice_in_dim(glob, start, NB, 0)
            weight = lax.dynamic_slice_in_dim(live, start, NB, 0)
            mats = lax.dynamic_slice_in_dim(blocks, start, NB, 0)
            picked = grid[:, index] * weight[None, :, :, None]
            strain = jnp.einsum('ikab,cikb->cia', mats, picked, precision=highest)
            back = jnp.einsum('ikab,cia->cikb', mats, strain, precision=highest) * weight[None, :, :, None]
            acc = acc.at[:, index.reshape(-1)].add(back.reshape(CASES, NB * KNZ, B))
            return acc, None

        acc, unused = lax.scan(one_sub, jnp.zeros((CASES, NBT, B), jnp.float32), jnp.arange(nsub, dtype=jnp.int32))
        return diag_shift * field + acc.reshape(CASES, NTOT)

    basis = corner_basis.reshape(NCL, nsub, nloc)
    hits = (corner_owner[:, :, None] == jnp.arange(NCG, dtype=jnp.int32)[None, None, :]).astype(jnp.float32)

    def precondition(resid):
        split = resid.reshape(CASES, nsub, nloc)
        corner = jnp.einsum('csn,jsn->csj', split, basis, precision=highest)
        coarse = jnp.einsum('csj,sju->cu', corner, hits, precision=highest)
        solved = jnp.dot(coarse, coarse_inverse, precision=highest)
        spread = jnp.einsum('cu,sju->csj', solved, hits, precision=highest)
        fine = jnp.einsum('csj,jsn->csn', spread, basis, precision=highest).reshape(CASES, NTOT)
        z = jacobi_scale[None, :] * resid + fine
        return z, jnp.sum(resid * z, axis=1)

    solution_field = jnp.zeros_like(right_side)
    residual = right_side
    z, rz = precondition(residual)
    direction = z
    for step in range(ITERS):
        image = apply_operator(direction)
        alpha = rz / jnp.sum(direction * image, axis=1)
        solution_field = solution_field + alpha[:, None] * direction
        residual = residual - alpha[:, None] * image
        if step + 1 < ITERS:
            z, rz_next = precondition(residual)
            direction = z + (rz_next / rz)[:, None] * direction
            rz = rz_next
    return solution_field, residual
```

```python
import functools

import jax
import jax.numpy as jnp
from jax import lax
from jax.experimental import pallas as pl
from jax.experimental.pallas import tpu as pltpu
from jax.sharding import PartitionSpec as P

B = 64
KNZ = 27
IFB = 4
NCL = 8
NB = 2 * IFB
NE = NB + 2 * IFB
EDGE = IFB * B
OWN = NB * B
EXT = NE * B
ROWS = NB * B
KPAD = 32
F32 = jnp.float32
BF16 = jnp.bfloat16
HIGHEST = lax.Precision.HIGHEST
NT = (((1,), (1,)), ((), ()))
NN = (((1,), (0,)), ((), ()))
VMEM_LIMIT = 48 * 1024 * 1024


def split(x):
    high = x.astype(BF16)
    return high, (x - high.astype(F32)).astype(BF16)


def times(x, high, low, dims):
    count = x.shape[0]
    xh, xl = split(x)
    both = lax.dot_general(
        jnp.concatenate([xh, xl], axis=0), high, dims, preferred_element_type=F32
    )
    return both[:count] + both[count:] + lax.dot_general(xh, low, dims, preferred_element_type=F32)


def exact(x, y, dims=NN):
    return lax.dot_general(x, y, dims, precision=HIGHEST, preferred_element_type=F32)


def call(kernel, outs, n_in, smem=(), scratch=()):
    def spec(space):
        return pl.BlockSpec(memory_space=space)

    return pl.pallas_call(
        kernel,
        out_shape=outs,
        in_specs=[spec(pltpu.SMEM if i in smem else pltpu.VMEM) for i in range(n_in)],
        out_specs=[spec(pltpu.VMEM) for _ in outs],
        scratch_shapes=list(scratch),
        compiler_params=pltpu.CompilerParams(vmem_limit_bytes=VMEM_LIMIT),
    )


def shape(*dims):
    return jax.ShapeDtypeStruct(dims, F32)


def place_of(rows_ref, odd, j):
    side = jnp.where(odd == 1, j // IFB, 1 - j // IFB)
    return rows_ref[0, side, j % IFB]


def assemble(rows_ref, columns_ref, blocks_ref, high_ref, low_ref, wh_ref, wl_ref):
    step = pl.program_id(0)
    odd = lax.axis_index("sub") % 2

    @pl.when(step == 0)
    def _():
        wh_ref[...] = jnp.zeros_like(wh_ref)
        wl_ref[...] = jnp.zeros_like(wl_ref)

    column = columns_ref[0]
    place = jnp.where(
        column < NB, -1, jnp.where((column < NB + IFB) == (odd == 1), column % IFB + NB, column % IFB + NB + IFB)
    )
    for j in range(NB):
        place = jnp.where(column == place_of(rows_ref, odd, j), j, place)
    place = jnp.where(column < 0, -1, place)
    r = lax.broadcasted_iota(jnp.int32, (NE * 8, 8 * KPAD), 0)
    q = lax.broadcasted_iota(jnp.int32, (NE * 8, 8 * KPAD), 1)
    hit = (r // 8 == place) & (r % 8 == q // KPAD)
    onehot = jnp.where(hit, 1.0, 0.0).astype(BF16)
    for g in range(8):
        wh, wl = split(blocks_ref[0, :, 512 * g : 512 * (g + 1)])
        wh_ref[g, :KNZ, :] = wh
        wl_ref[g, :KNZ, :] = wl
    dense = lax.dot_general(
        onehot, wh_ref[...].reshape(8 * KPAD, 512), NN, preferred_element_type=F32
    ) + lax.dot_general(onehot, wl_ref[...].reshape(8 * KPAD, 512), NN, preferred_element_type=F32)
    first = lax.broadcasted_iota(jnp.int32, (8, 128), 1) < B
    for m in range(NE // 2):
        for h in range(4):
            left = dense[16 * m : 16 * m + 8, 128 * h : 128 * (h + 1)]
            right = dense[16 * m + 8 : 16 * m + 16, 128 * h : 128 * (h + 1)]
            tile = jnp.concatenate(
                [
                    jnp.where(first, left, pltpu.roll(right, B, 1)),
                    jnp.where(first, pltpu.roll(left, B, 1), right),
                ],
                axis=0,
            )
            th, tl = split(tile)
            high_ref[16 * h : 16 * (h + 1), 128 * m : 128 * (m + 1)] = th
            low_ref[16 * h : 16 * (h + 1), 128 * m : 128 * (m + 1)] = tl


def prepare(rows_ref, owner_ref, right_ref, scale_ref, *rest, parts, ncoarse):
    basis_refs = rest[:parts]
    resid_ref, side_a_ref, side_b_ref, blk_ref = rest[parts:]
    odd = lax.axis_index("sub") % 2
    mine = lax.axis_index("rhs")
    cases = right_ref.shape[0]
    per = NCL // parts
    scale = jnp.broadcast_to(scale_ref[...], (8, OWN))
    unknown = lax.broadcasted_iota(jnp.int32, (ncoarse, OWN), 0)
    coarse = jnp.zeros((ncoarse, OWN), F32)
    for k in range(parts):
        for t in range(per):
            owner = owner_ref[0, ((mine + k) % parts) * per + t]
            coarse = coarse + jnp.where(unknown == owner, basis_refs[k][t : t + 1, :], 0.0)
    right = right_ref[...]
    total = 2 * cases + ncoarse + 8
    for n in range(NB):
        cut = slice(B * n, B * (n + 1))
        blk_ref[n, 0:cases, :] = right[:, cut] * scale[0:1, cut]
        blk_ref[n, cases : cases + ncoarse, :] = coarse[:, cut]
        blk_ref[n, cases + ncoarse : cases + ncoarse + 8, :] = scale[:, cut]
        blk_ref[n, cases + ncoarse + 8 : total, :] = right[:, cut]
    for j in range(0, NB, 2):
        pair = jnp.concatenate(
            [blk_ref[place_of(rows_ref, odd, j)], blk_ref[place_of(rows_ref, odd, j + 1)]], axis=1
        )
        target = side_a_ref if j < IFB else side_b_ref
        at = B * (j % IFB)
        target[:, at : at + 2 * B] = pair[: total - cases]
        resid_ref[:, B * j : B * (j + 2)] = pair[total - cases :]


def first_strain(
    resid_ref, a_ref, b_ref, ga_ref, gb_ref, high_ref, low_ref, strain_ref, pay_ref, *, cases, ncoarse
):
    count = cases + ncoarse
    field = jnp.concatenate(
        [a_ref[:count, :], b_ref[:count, :], ga_ref[:count, :], gb_ref[:count, :]], axis=1
    )
    strain = times(field, high_ref[...], low_ref[...], NT)
    strain_ref[...] = strain
    own = field[:, :OWN]
    resid = resid_ref[...]
    paired = jnp.concatenate([own, strain], axis=1)
    gram = exact(paired, paired[cases:], NT)
    restricted = exact(resid, own[cases:], NT)
    lead = paired[:cases]
    pay_ref[...] = jnp.zeros_like(pay_ref)
    pay_ref[:cases, 0:ncoarse] = restricted
    pay_ref[:cases, ncoarse : 2 * ncoarse] = gram[:cases]
    pay_ref[:ncoarse, 2 * ncoarse : 3 * ncoarse] = gram[cases:]
    pay_ref[:cases, 3 * ncoarse : 3 * ncoarse + 1] = jnp.sum(
        resid * own[:cases], axis=1, keepdims=True
    )
    pay_ref[:cases, 3 * ncoarse + 1 : 3 * ncoarse + 2] = jnp.sum(lead * lead, axis=1, keepdims=True)


def first_image(a_ref, b_ref, strain_ref, high_ref, low_ref, send_a_ref, send_b_ref):
    strain = strain_ref[...]
    count = strain.shape[0]
    back = times(strain, high_ref[...], low_ref[...], NN)
    send_a_ref[:count, :] = a_ref[:count, :] + back[:, :EDGE]
    send_a_ref[count:, :] = back[:, OWN : OWN + EDGE]
    send_b_ref[:count, :] = b_ref[:count, :] + back[:, EDGE:OWN]
    send_b_ref[count:, :] = back[:, OWN + EDGE :]


def second_strain(
    inverse_ref,
    resid_ref,
    a_ref,
    b_ref,
    ga_ref,
    gb_ref,
    own_a_ref,
    own_b_ref,
    got_a_ref,
    got_b_ref,
    high_ref,
    low_ref,
    *rest,
    cases,
    ncoarse,
    n_pay,
):
    pays = rest[:n_pay]
    strain_ref, pay_ref, resid1_ref, z0_ref, z1_ref, q0_ref, keep_ref = rest[n_pay:]
    count = cases + ncoarse
    pay = pays[0][...]
    for other in pays[1:]:
        pay = pay + other[...]
    u0 = pay[:cases, 0:ncoarse]
    ra = pay[:cases, ncoarse : 2 * ncoarse]
    rac = pay[:ncoarse, 2 * ncoarse : 3 * ncoarse]
    inverse = inverse_ref[...]
    y0 = exact(u0, inverse)
    ry = exact(y0, rac)
    rz0 = pay[:cases, 3 * ncoarse : 3 * ncoarse + 1] + jnp.sum(u0 * y0, axis=1, keepdims=True)
    pq0 = pay[:cases, 3 * ncoarse + 1 : 3 * ncoarse + 2] + jnp.sum(
        y0 * (2.0 * ra + ry), axis=1, keepdims=True
    )
    alpha = rz0 / pq0
    u1 = u0 - alpha * (ra + ry)
    y1 = exact(u1, inverse)
    image = jnp.concatenate(
        [
            own_a_ref[:count, :] + got_a_ref[count:, :],
            own_b_ref[:count, :] + got_b_ref[count:, :],
            own_a_ref[count:, :] + got_a_ref[:count, :],
            own_b_ref[count:, :] + got_b_ref[:count, :],
        ],
        axis=1,
    )
    parts = [a_ref, b_ref, ga_ref, gb_ref]
    scaled = jnp.concatenate([ref[:cases, :] for ref in parts], axis=1)
    coarse = jnp.concatenate([ref[cases:count, :] for ref in parts], axis=1)
    scale = jnp.concatenate([ref[count : count + 1, :] for ref in parts], axis=1)
    q0 = image[:cases] + exact(y0, image[cases:])
    z0 = scaled[:, :OWN] + exact(y0, coarse[:, :OWN])
    resid1 = resid_ref[...] - alpha * q0[:, :OWN]
    z1 = scaled - (alpha * scale) * q0 + exact(y1, coarse)
    strain = times(z1, high_ref[...], low_ref[...], NT)
    strain_ref[...] = strain
    own = z1[:, :OWN]
    resid1_ref[...] = resid1
    z0_ref[...] = z0
    z1_ref[...] = own
    q0_ref[...] = q0[:, :OWN]
    pay_ref[...] = jnp.zeros_like(pay_ref)
    pay_ref[:, 0:1] = jnp.sum(resid1 * resid1 * scale[:, :OWN], axis=1, keepdims=True)
    pay_ref[:, 1:2] = jnp.sum(own * own, axis=1, keepdims=True) + jnp.sum(
        strain * strain, axis=1, keepdims=True
    )
    pay_ref[:, 2:3] = jnp.sum(own * q0[:, :OWN], axis=1, keepdims=True)
    keep_ref[...] = jnp.zeros_like(keep_ref)
    keep_ref[:, 0:1] = rz0
    keep_ref[:, 1:2] = pq0
    keep_ref[:, 2:3] = alpha
    keep_ref[:, 3:4] = jnp.sum(u1 * y1, axis=1, keepdims=True)


def second_image(z1_ref, strain_ref, high_ref, low_ref, own_ref, send_a_ref, send_b_ref):
    back = times(strain_ref[...], high_ref[...], low_ref[...], NN)
    own_ref[...] = z1_ref[...] + back[:, :OWN]
    send_a_ref[...] = back[:, OWN : OWN + EDGE]
    send_b_ref[...] = back[:, OWN + EDGE :]


def finish(
    rows_ref, resid1_ref, z0_ref, z1_ref, q0_ref, keep_ref, own_ref, got_a_ref, got_b_ref, *rest, n_pay
):
    pays = rest[:n_pay]
    field_ref, resid2_ref, blk_ref = rest[n_pay:]
    odd = lax.axis_index("sub") % 2
    cases = own_ref.shape[0]
    pay = pays[0][...]
    for other in pays[1:]:
        pay = pay + other[...]
    keep = keep_ref[...]
    rz0, pq0, alpha0 = keep[:, 0:1], keep[:, 1:2], keep[:, 2:3]
    rz1 = pay[:, 0:1] + keep[:, 3:4]
    beta = rz1 / rz0
    pq1 = pay[:, 1:2] + beta * (2.0 * pay[:, 2:3] + beta * pq0)
    alpha1 = rz1 / pq1
    image = own_ref[...] + jnp.concatenate([got_a_ref[...], got_b_ref[...]], axis=1)
    z0 = z0_ref[...]
    field = alpha0 * z0 + alpha1 * (z1_ref[...] + beta * z0)
    resid2 = resid1_ref[...] - alpha1 * (image + beta * q0_ref[...])
    for j in range(NB):
        at = place_of(rows_ref, odd, j)
        blk_ref[at, :cases, :] = field[:, B * j : B * (j + 1)]
        blk_ref[at, cases:, :] = resid2[:, B * j : B * (j + 1)]
    for n in range(0, NB, 2):
        pair = jnp.concatenate([blk_ref[n], blk_ref[n + 1]], axis=1)
        field_ref[:, B * n : B * (n + 2)] = pair[:cases]
        resid2_ref[:, B * n : B * (n + 2)] = pair[cases:]


def swap(x, steps, count):
    return [lax.ppermute(x, "sub", [(i, i ^ k) for i in range(count)]) for k in steps]


def rounds_of(count):
    rounds = []
    base = 1
    while base < count:
        if base * 4 <= count:
            rounds.append((base, 2 * base, 3 * base))
            base *= 4
        else:
            rounds.append((base,))
            base *= 2
    return rounds


def across(a, b, count):
    low = lax.ppermute(a, "sub", [(i, i ^ 1) for i in range(count)])
    inner = [(i, i + 1) for i in range(1, count - 1, 2)]
    return low, lax.ppermute(b, "sub", inner + [(j, i) for i, j in inner])


def body(
    right_side,
    stiffness_blocks,
    block_columns,
    interface_rows,
    corner_owner,
    corner_basis,
    jacobi_scale,
    coarse_inverse,
):
    cases = right_side.shape[0]
    ncoarse = coarse_inverse.shape[0]
    count = lax.axis_size("sub")
    parts = lax.axis_size("rhs")
    live = cases + ncoarse
    rounds = rounds_of(count)

    bases = [corner_basis] + [
        lax.ppermute(corner_basis, "rhs", [((i + k) % parts, i) for i in range(parts)])
        for k in range(1, parts)
    ]
    padded = jnp.pad(block_columns, ((0, 0), (0, KPAD - KNZ)), constant_values=-1)
    tiled = jnp.tile(padded, (1, 8)).reshape(NB, 1, 8 * KPAD)
    high, low = pl.pallas_call(
        assemble,
        out_shape=[jax.ShapeDtypeStruct((ROWS, EXT), BF16)] * 2,
        grid=(NB,),
        in_specs=[
            pl.BlockSpec(memory_space=pltpu.SMEM),
            pl.BlockSpec((1, 1, 8 * KPAD), lambda i: (i, 0, 0)),
            pl.BlockSpec((1, KNZ, B * B), lambda i: (i, 0, 0)),
        ],
        out_specs=[pl.BlockSpec((B, EXT), lambda i: (i, 0))] * 2,
        scratch_shapes=[pltpu.VMEM((8, KPAD, 512), BF16)] * 2,
        compiler_params=pltpu.CompilerParams(vmem_limit_bytes=VMEM_LIMIT),
    )(interface_rows, tiled, stiffness_blocks)

    resid, side_a, side_b = call(
        functools.partial(prepare, parts=parts, ncoarse=ncoarse),
        [shape(cases, OWN), shape(live + 8, EDGE), shape(live + 8, EDGE)],
        4 + parts,
        smem=(0, 1),
        scratch=[pltpu.VMEM((NB, live + 8 + cases, B), F32)],
    )(interface_rows, corner_owner, right_side, jacobi_scale.reshape(1, OWN), *bases)
    ghost_a, ghost_b = across(side_a, side_b, count)

    lanes = -(-(3 * ncoarse + 2) // 128) * 128
    strain, pay = call(
        functools.partial(first_strain, cases=cases, ncoarse=ncoarse),
        [shape(live, ROWS), shape(max(cases, ncoarse), lanes)],
        7,
    )(resid, side_a, side_b, ghost_a, ghost_b, high, low)
    for steps in rounds[:-1]:
        pay = sum(swap(pay, steps, count), pay)
    pays = [pay] + swap(pay, rounds[-1], count)
    own_a, own_b = call(first_image, [shape(2 * live, EDGE)] * 2, 5)(side_a, side_b, strain, high, low)
    got_a, got_b = across(own_a, own_b, count)

    strain, pay, resid1, z0, z1, q0, keep = call(
        functools.partial(second_strain, cases=cases, ncoarse=ncoarse, n_pay=len(pays)),
        [shape(cases, ROWS), shape(cases, 128)] + [shape(cases, OWN)] * 4 + [shape(cases, 128)],
        12 + len(pays),
    )(
        coarse_inverse, resid, side_a, side_b, ghost_a, ghost_b, own_a, own_b, got_a, got_b, high, low, *pays
    )
    for steps in rounds[:-1]:
        pay = sum(swap(pay, steps, count), pay)
    pays = [pay] + swap(pay, rounds[-1], count)
    own, back_a, back_b = call(
        second_image, [shape(cases, OWN), shape(cases, EDGE), shape(cases, EDGE)], 4
    )(z1, strain, high, low)
    got_a, got_b = across(back_a, back_b, count)
    return tuple(
        call(
            functools.partial(finish, n_pay=len(pays)),
            [shape(cases, OWN)] * 2,
            9 + len(pays),
            smem=(0,),
            scratch=[pltpu.VMEM((NB, 2 * cases, B), F32)],
        )(interface_rows, resid1, z0, z1, q0, keep, own, got_a, got_b, *pays)
    )


def solution(mesh):
    placed = (
        P("rhs", "sub"),
        P("sub", None, None),
        P("sub", None),
        P("sub", None, None),
        P("sub", None),
        P("rhs", "sub"),
        P("sub"),
        P(),
    )
    return jax.shard_map(
        body,
        mesh=mesh,
        in_specs=placed,
        out_specs=(P("rhs", "sub"), P("rhs", "sub")),
        check_vma=False,
    )
```

```python
import functools

import jax
import jax.numpy as jnp
from jax import lax
from jax.experimental import pallas as pl
from jax.experimental.pallas import tpu as pltpu
from jax.sharding import PartitionSpec as P

B = 64
KNZ = 27
IFB = 4
NCL = 8
NB = 2 * IFB
NE = NB + 2 * IFB
EDGE = IFB * B
OWN = NB * B
EXT = NE * B
ROWS = NB * B
KPAD = 32
F32 = jnp.float32
BF16 = jnp.bfloat16
HIGHEST = lax.Precision.HIGHEST
NT = (((1,), (1,)), ((), ()))
NN = (((1,), (0,)), ((), ()))
VMEM_LIMIT = 48 * 1024 * 1024
CHUNK = 512


def split(x):
    high = x.astype(BF16)
    return high, (x - high.astype(F32)).astype(BF16)


def times(x, high, low, dims):
    count = x.shape[0]
    xh, xl = split(x)
    both = lax.dot_general(
        jnp.concatenate([xh, xl], axis=0), high, dims, preferred_element_type=F32
    )
    return both[:count] + both[count:] + lax.dot_general(xh, low, dims, preferred_element_type=F32)


def apply(x, halves):
    return jnp.concatenate([times(x, h[...], l[...], NT) for h, l in halves], axis=1)


def apply_back(x, halves):
    cut = ROWS // 2
    (h0, l0), (h1, l1) = halves
    return times(x[:, :cut], h0[...], l0[...], NN) + times(x[:, cut:], h1[...], l1[...], NN)


def exact(x, y, dims=NN):
    return lax.dot_general(x, y, dims, precision=HIGHEST, preferred_element_type=F32)


def call(kernel, outs, n_in, smem=(), raw=(), raw_out=False, scratch=()):
    def spec(i):
        if i in raw:
            return pl.BlockSpec(memory_space=pl.ANY)
        return pl.BlockSpec(memory_space=pltpu.SMEM if i in smem else pltpu.VMEM)

    return pl.pallas_call(
        kernel,
        out_shape=outs,
        in_specs=[spec(i) for i in range(n_in)],
        out_specs=[
            pl.BlockSpec(memory_space=pl.ANY if raw_out else pltpu.VMEM) for _ in outs
        ],
        scratch_shapes=list(scratch),
        compiler_params=pltpu.CompilerParams(vmem_limit_bytes=VMEM_LIMIT),
    )


def shape(*dims):
    return jax.ShapeDtypeStruct(dims, F32)


def place_of(rows_ref, odd, j):
    side = jnp.where(odd == 1, j // IFB, 1 - j // IFB)
    return rows_ref[0, side, j % IFB]


def spread(onehot, raw, high_ref, low_ref, at):
    width = raw.shape[-1]
    padded = jnp.concatenate([raw, jnp.zeros((1, NB, width), F32)], axis=0)
    rest = jnp.zeros((NB * (KPAD - KNZ - 1), width), BF16)
    wh, wl = split(padded.reshape(NB * (KNZ + 1), width))
    dense = lax.dot_general(
        onehot, jnp.concatenate([wh, rest], axis=0), NN, preferred_element_type=F32
    ) + lax.dot_general(onehot, jnp.concatenate([wl, rest], axis=0), NN, preferred_element_type=F32)
    first = lax.broadcasted_iota(jnp.int32, (NB, 128), 1) < B
    for m in range(NE // 2):
        for h in range(width // 128):
            cut = slice(128 * h, 128 * (h + 1))
            left = dense[16 * m : 16 * m + 8, cut]
            right = dense[16 * m + 8 : 16 * m + 16, cut]
            tile = jnp.concatenate(
                [
                    jnp.where(first, left, pltpu.roll(right, B, 1)),
                    jnp.where(first, pltpu.roll(left, B, 1), right),
                ],
                axis=0,
            )
            th, tl = split(tile)
            row = slice(at + 16 * h, at + 16 * (h + 1))
            high_ref[row, 128 * m : 128 * (m + 1)] = th
            low_ref[row, 128 * m : 128 * (m + 1)] = tl


def open_up(
    rows_hbm,
    right_hbm,
    scale_hbm,
    columns_hbm,
    blocks_hbm,
    resid_ref,
    fine_ref,
    onehot_ref,
    raw_ref,
    high_ref,
    low_ref,
    rows_ref,
    right_ref,
    scale_ref,
    columns_ref,
    chunk_ref,
    blk_ref,
    sems,
):
    odd = lax.axis_index("sub") % 2
    cases = right_ref.shape[0]
    half = B * B // 2
    small = [
        pltpu.make_async_copy(rows_hbm, rows_ref, sems.at[0]),
        pltpu.make_async_copy(columns_hbm, columns_ref, sems.at[1]),
        pltpu.make_async_copy(right_hbm, right_ref, sems.at[2]),
        pltpu.make_async_copy(scale_hbm, scale_ref, sems.at[3]),
    ]
    chunks = [
        pltpu.make_async_copy(
            blocks_hbm.at[:, :, pl.ds(CHUNK * t, CHUNK)], chunk_ref.at[t], sems.at[4 + t]
        )
        for t in range(half // CHUNK)
    ]
    tail = pltpu.make_async_copy(
        blocks_hbm.at[:, :, pl.ds(half, half)], raw_ref, sems.at[4 + len(chunks)]
    )
    for copy in small + chunks + [tail]:
        copy.start()
    for copy in small:
        copy.wait()
    column = columns_ref[...]
    place = jnp.where(
        (column < NB + IFB) == (odd == 1), column % IFB + NB, column % IFB + NB + IFB
    )
    for j in range(NB):
        place = jnp.where(column == place_of(rows_ref, odd, j), j, place)
    slot = lax.broadcasted_iota(jnp.int32, (KNZ, NB * KPAD), 0)
    entry = lax.broadcasted_iota(jnp.int32, (KNZ, NB * KPAD), 1)
    widen = jnp.where(entry // NB == slot, 1.0, 0.0).astype(BF16)
    wide = lax.dot_general(place.astype(F32).astype(BF16), widen, NN, preferred_element_type=F32)
    r = lax.broadcasted_iota(jnp.int32, (NE * NB, NB * KPAD), 0)
    q = lax.broadcasted_iota(jnp.int32, (NE * NB, NB * KPAD), 1)
    hit = (jnp.concatenate([wide] * NE, axis=0) == (r // NB).astype(F32)) & (r % NB == q % NB)
    onehot = jnp.where(hit, 1.0, 0.0).astype(BF16)
    onehot_ref[...] = onehot
    right = right_ref[...]
    scale = jnp.broadcast_to(scale_ref[...], (8, OWN))
    for n in range(NB):
        cut = slice(B * n, B * (n + 1))
        blk_ref[n, 0:cases, :] = right[:, cut]
        blk_ref[n, cases : 2 * cases, :] = right[:, cut] * scale[0:1, cut]
        blk_ref[n, 2 * cases :, :] = scale[:, cut]
    for j in range(0, NB, 2):
        pair = jnp.concatenate(
            [blk_ref[place_of(rows_ref, odd, j)], blk_ref[place_of(rows_ref, odd, j + 1)]], axis=1
        )
        resid_ref[:, B * j : B * (j + 2)] = pair[:cases]
        fine_ref[:, B * j : B * (j + 2)] = pair[cases:]
    for t, copy in enumerate(chunks):
        copy.wait()
        spread(onehot, chunk_ref[t], high_ref, low_ref, NB * CHUNK // B * t)
    tail.wait()


def open_rest(onehot_ref, raw_ref, after_ref, high_ref, low_ref):
    onehot = onehot_ref[...]
    for t in range(B * B // 2 // CHUNK):
        spread(
            onehot, raw_ref[:, :, CHUNK * t : CHUNK * (t + 1)], high_ref, low_ref, NB * CHUNK // B * t
        )


def sides(rows_ref, owner_ref, fine_ref, *rest, parts, ncoarse):
    basis_refs = rest[:parts]
    side_a_ref, side_b_ref, blk_ref = rest[parts:]
    odd = lax.axis_index("sub") % 2
    mine = lax.axis_index("rhs")
    cases = fine_ref.shape[0] - 8
    per = NCL // parts
    unknown = lax.broadcasted_iota(jnp.int32, (ncoarse, OWN), 0)
    coarse = jnp.zeros((ncoarse, OWN), F32)
    for k in range(parts):
        for t in range(per):
            owner = owner_ref[0, ((mine + k) % parts) * per + t]
            coarse = coarse + jnp.where(unknown == owner, basis_refs[k][t : t + 1, :], 0.0)
    for n in range(NB):
        blk_ref[n] = coarse[:, B * n : B * (n + 1)]
    for ref, first in ((side_a_ref, 0), (side_b_ref, IFB)):
        part = slice(B * first, B * (first + IFB))
        ref[:cases, :] = fine_ref[:cases, part]
        ref[cases + ncoarse :, :] = fine_ref[cases:, part]
        for j in range(0, IFB, 2):
            ref[cases : cases + ncoarse, B * j : B * (j + 2)] = jnp.concatenate(
                [
                    blk_ref[place_of(rows_ref, odd, first + j)],
                    blk_ref[place_of(rows_ref, odd, first + j + 1)],
                ],
                axis=1,
            )


def first_strain(
    resid_ref, a_ref, b_ref, ga_ref, gb_ref, h0, l0, h1, l1, strain_ref, pay_ref, *, cases, ncoarse
):
    count = cases + ncoarse
    field = jnp.concatenate(
        [a_ref[:count, :], b_ref[:count, :], ga_ref[:count, :], gb_ref[:count, :]], axis=1
    )
    strain = apply(field, ((h0, l0), (h1, l1)))
    strain_ref[...] = strain
    own = field[:, :OWN]
    resid = resid_ref[...]
    paired = jnp.concatenate([own, strain], axis=1)
    gram = exact(paired, paired[cases:], NT)
    restricted = exact(resid, own[cases:], NT)
    lead = paired[:cases]
    pay_ref[...] = jnp.zeros_like(pay_ref)
    pay_ref[:cases, 0:ncoarse] = restricted
    pay_ref[:cases, ncoarse : 2 * ncoarse] = gram[:cases]
    pay_ref[:ncoarse, 2 * ncoarse : 3 * ncoarse] = gram[cases:]
    pay_ref[:cases, 3 * ncoarse : 3 * ncoarse + 1] = jnp.sum(
        resid * own[:cases], axis=1, keepdims=True
    )
    pay_ref[:cases, 3 * ncoarse + 1 : 3 * ncoarse + 2] = jnp.sum(lead * lead, axis=1, keepdims=True)


def first_image(a_ref, b_ref, strain_ref, h0, l0, h1, l1, send_a_ref, send_b_ref):
    strain = strain_ref[...]
    count = strain.shape[0]
    back = apply_back(strain, ((h0, l0), (h1, l1)))
    send_a_ref[:count, :] = a_ref[:count, :] + back[:, :EDGE]
    send_a_ref[count:, :] = back[:, OWN : OWN + EDGE]
    send_b_ref[:count, :] = b_ref[:count, :] + back[:, EDGE:OWN]
    send_b_ref[count:, :] = back[:, OWN + EDGE :]


def second_strain(
    inverse_ref,
    resid_ref,
    a_ref,
    b_ref,
    ga_ref,
    gb_ref,
    own_a_ref,
    own_b_ref,
    got_a_ref,
    got_b_ref,
    h0,
    l0,
    h1,
    l1,
    *rest,
    cases,
    ncoarse,
    n_pay,
):
    pays = rest[:n_pay]
    strain_ref, pay_ref, resid1_ref, z0_ref, z1_ref, q0_ref, keep_ref = rest[n_pay:]
    count = cases + ncoarse
    pay = pays[0][...]
    for other in pays[1:]:
        pay = pay + other[...]
    u0 = pay[:cases, 0:ncoarse]
    ra = pay[:cases, ncoarse : 2 * ncoarse]
    rac = pay[:ncoarse, 2 * ncoarse : 3 * ncoarse]
    inverse = inverse_ref[...]
    y0 = exact(u0, inverse)
    ry = exact(y0, rac)
    rz0 = pay[:cases, 3 * ncoarse : 3 * ncoarse + 1] + jnp.sum(u0 * y0, axis=1, keepdims=True)
    pq0 = pay[:cases, 3 * ncoarse + 1 : 3 * ncoarse + 2] + jnp.sum(
        y0 * (2.0 * ra + ry), axis=1, keepdims=True
    )
    alpha = rz0 / pq0
    u1 = u0 - alpha * (ra + ry)
    y1 = exact(u1, inverse)
    image = jnp.concatenate(
        [
            own_a_ref[:count, :] + got_a_ref[count:, :],
            own_b_ref[:count, :] + got_b_ref[count:, :],
            own_a_ref[count:, :] + got_a_ref[:count, :],
            own_b_ref[count:, :] + got_b_ref[:count, :],
        ],
        axis=1,
    )
    parts = [a_ref, b_ref, ga_ref, gb_ref]
    scaled = jnp.concatenate([ref[:cases, :] for ref in parts], axis=1)
    coarse = jnp.concatenate([ref[cases:count, :] for ref in parts], axis=1)
    scale = jnp.concatenate([ref[count : count + 1, :] for ref in parts], axis=1)
    q0 = image[:cases] + exact(y0, image[cases:])
    z0 = scaled[:, :OWN] + exact(y0, coarse[:, :OWN])
    resid1 = resid_ref[...] - alpha * q0[:, :OWN]
    z1 = scaled - (alpha * scale) * q0 + exact(y1, coarse)
    strain = apply(z1, ((h0, l0), (h1, l1)))
    strain_ref[...] = strain
    own = z1[:, :OWN]
    resid1_ref[...] = resid1
    z0_ref[...] = z0
    z1_ref[...] = own
    q0_ref[...] = q0[:, :OWN]
    pay_ref[...] = jnp.zeros_like(pay_ref)
    pay_ref[:, 0:1] = jnp.sum(resid1 * resid1 * scale[:, :OWN], axis=1, keepdims=True)
    pay_ref[:, 1:2] = jnp.sum(own * own, axis=1, keepdims=True) + jnp.sum(
        strain * strain, axis=1, keepdims=True
    )
    pay_ref[:, 2:3] = jnp.sum(own * q0[:, :OWN], axis=1, keepdims=True)
    keep_ref[...] = jnp.zeros_like(keep_ref)
    keep_ref[:, 0:1] = rz0
    keep_ref[:, 1:2] = pq0
    keep_ref[:, 2:3] = alpha
    keep_ref[:, 3:4] = jnp.sum(u1 * y1, axis=1, keepdims=True)


def second_image(z1_ref, strain_ref, h0, l0, h1, l1, own_ref, send_a_ref, send_b_ref):
    back = apply_back(strain_ref[...], ((h0, l0), (h1, l1)))
    own_ref[...] = z1_ref[...] + back[:, :OWN]
    send_a_ref[...] = back[:, OWN : OWN + EDGE]
    send_b_ref[...] = back[:, OWN + EDGE :]


def finish(
    rows_ref, resid1_ref, z0_ref, z1_ref, q0_ref, keep_ref, own_ref, got_a_ref, got_b_ref, *rest, n_pay
):
    pays = rest[:n_pay]
    field_hbm, resid2_hbm, field_ref, resid2_ref, blk_ref, sems = rest[n_pay:]
    odd = lax.axis_index("sub") % 2
    cases = own_ref.shape[0]
    pay = pays[0][...]
    for other in pays[1:]:
        pay = pay + other[...]
    keep = keep_ref[...]
    rz0, pq0, alpha0 = keep[:, 0:1], keep[:, 1:2], keep[:, 2:3]
    rz1 = pay[:, 0:1] + keep[:, 3:4]
    beta = rz1 / rz0
    pq1 = pay[:, 1:2] + beta * (2.0 * pay[:, 2:3] + beta * pq0)
    alpha1 = rz1 / pq1
    image = own_ref[...] + jnp.concatenate([got_a_ref[...], got_b_ref[...]], axis=1)
    z0 = z0_ref[...]
    field = alpha0 * z0 + alpha1 * (z1_ref[...] + beta * z0)
    resid2 = resid1_ref[...] - alpha1 * (image + beta * q0_ref[...])
    copies = []
    for k, (value, out, buf) in enumerate(
        ((field, field_hbm, field_ref), (resid2, resid2_hbm, resid2_ref))
    ):
        for j in range(NB):
            blk_ref[k, place_of(rows_ref, odd, j)] = value[:, B * j : B * (j + 1)]
        for n in range(0, NB, 2):
            buf[:, B * n : B * (n + 2)] = jnp.concatenate([blk_ref[k, n], blk_ref[k, n + 1]], axis=1)
        copies.append(pltpu.make_async_copy(buf, out, sems.at[k]))
        copies[-1].start()
    for copy in copies:
        copy.wait()


def swap(x, steps, count):
    return [lax.ppermute(x, "sub", [(i, i ^ k) for i in range(count)]) for k in steps]


def rounds_of(count):
    rounds = []
    base = 1
    while base < count:
        if base * 4 <= count:
            rounds.append((base, 2 * base, 3 * base))
            base *= 4
        else:
            rounds.append((base,))
            base *= 2
    return rounds


def across(a, b, count):
    low = lax.ppermute(a, "sub", [(i, i ^ 1) for i in range(count)])
    inner = [(i, i + 1) for i in range(1, count - 1, 2)]
    return low, lax.ppermute(b, "sub", inner + [(j, i) for i, j in inner])


def body(
    right_side,
    stiffness_blocks,
    block_columns,
    interface_rows,
    corner_owner,
    corner_basis,
    jacobi_scale,
    coarse_inverse,
):
    cases = right_side.shape[0]
    ncoarse = coarse_inverse.shape[0]
    count = lax.axis_size("sub")
    parts = lax.axis_size("rhs")
    live = cases + ncoarse
    rounds = rounds_of(count)

    bases = [corner_basis] + [
        lax.ppermute(corner_basis, "rhs", [((i + k) % parts, i) for i in range(parts)])
        for k in range(1, parts)
    ]
    half = B * B // 2
    g_half = jax.ShapeDtypeStruct((ROWS // 2, EXT), BF16)
    resid, fine, onehot, raw, h0, l0 = call(
        open_up,
        [
            shape(cases, OWN),
            shape(cases + 8, OWN),
            jax.ShapeDtypeStruct((NE * NB, NB * KPAD), BF16),
            shape(KNZ, NB, half),
            g_half,
            g_half,
        ],
        5,
        raw=range(5),
        scratch=[
            pltpu.SMEM((1, 2, IFB), jnp.int32),
            pltpu.VMEM((cases, OWN), F32),
            pltpu.VMEM((1, OWN), F32),
            pltpu.VMEM((NB, KNZ), jnp.int32),
            pltpu.VMEM((half // CHUNK, KNZ, NB, CHUNK), F32),
            pltpu.VMEM((NB, 2 * cases + 8, B), F32),
            pltpu.SemaphoreType.DMA((half // CHUNK + 5,)),
        ],
    )(
        interface_rows,
        right_side,
        jacobi_scale.reshape(1, OWN),
        block_columns,
        jnp.transpose(stiffness_blocks, (1, 0, 2)),
    )
    side_a, side_b = call(
        functools.partial(sides, parts=parts, ncoarse=ncoarse),
        [shape(live + 8, EDGE), shape(live + 8, EDGE)],
        3 + parts,
        smem=(0, 1),
        scratch=[pltpu.VMEM((NB, ncoarse, B), F32)],
    )(interface_rows, corner_owner, fine, *bases)
    h1, l1 = call(open_rest, [g_half, g_half], 3)(onehot, raw, side_a)
    dense = (h0, l0, h1, l1)
    ghost_a, ghost_b = across(side_a, side_b, count)

    lanes = -(-(3 * ncoarse + 2) // 128) * 128
    strain, pay = call(
        functools.partial(first_strain, cases=cases, ncoarse=ncoarse),
        [shape(live, ROWS), shape(max(cases, ncoarse), lanes)],
        9,
    )(resid, side_a, side_b, ghost_a, ghost_b, *dense)
    for steps in rounds[:-1]:
        pay = sum(swap(pay, steps, count), pay)
    pays = [pay] + swap(pay, rounds[-1], count)
    own_a, own_b = call(first_image, [shape(2 * live, EDGE)] * 2, 7)(side_a, side_b, strain, *dense)
    got_a, got_b = across(own_a, own_b, count)

    strain, pay, resid1, z0, z1, q0, keep = call(
        functools.partial(second_strain, cases=cases, ncoarse=ncoarse, n_pay=len(pays)),
        [shape(cases, ROWS), shape(cases, 128)] + [shape(cases, OWN)] * 4 + [shape(cases, 128)],
        14 + len(pays),
    )(
        coarse_inverse, resid, side_a, side_b, ghost_a, ghost_b, own_a, own_b, got_a, got_b, *dense, *pays
    )
    for steps in rounds[:-1]:
        pay = sum(swap(pay, steps, count), pay)
    pays = [pay] + swap(pay, rounds[-1], count)
    own, back_a, back_b = call(
        second_image, [shape(cases, OWN), shape(cases, EDGE), shape(cases, EDGE)], 6
    )(z1, strain, *dense)
    got_a, got_b = across(back_a, back_b, count)
    return tuple(
        call(
            functools.partial(finish, n_pay=len(pays)),
            [shape(cases, OWN)] * 2,
            9 + len(pays),
            smem=(0,),
            raw_out=True,
            scratch=[
                pltpu.VMEM((cases, OWN), F32),
                pltpu.VMEM((cases, OWN), F32),
                pltpu.VMEM((2, NB, cases, B), F32),
                pltpu.SemaphoreType.DMA((2,)),
            ],
        )(interface_rows, resid1, z0, z1, q0, keep, own, got_a, got_b, *pays)
    )


def solution(mesh):
    placed = (
        P("rhs", "sub"),
        P("sub", None, None),
        P("sub", None),
        P("sub", None, None),
        P("sub", None),
        P("rhs", "sub"),
        P("sub"),
        P(),
    )
    return jax.shard_map(
        body,
        mesh=mesh,
        in_specs=placed,
        out_specs=(P("rhs", "sub"), P("rhs", "sub")),
        check_vma=False,
    )
```

```python
import functools

import jax
import jax.numpy as jnp
from jax import lax
from jax.experimental import pallas as pl
from jax.experimental.pallas import tpu as pltpu
from jax.sharding import PartitionSpec as P

B = 64
KNZ = 27
IFB = 4
NCL = 8
NB = 2 * IFB
NE = NB + 2 * IFB
EDGE = IFB * B
OWN = NB * B
EXT = NE * B
ROWS = NB * B
KPAD = 32
F32 = jnp.float32
BF16 = jnp.bfloat16
HIGHEST = lax.Precision.HIGHEST
NT = (((1,), (1,)), ((), ()))
NN = (((1,), (0,)), ((), ()))
VMEM_SMALL = 16 * 1024 * 1024
VMEM_LARGE = 48 * 1024 * 1024
CHUNK = 512


def split(x):
    high = x.astype(BF16)
    return high, (x - high.astype(F32)).astype(BF16)


def times(x, high, low, dims):
    count = x.shape[0]
    xh, xl = split(x)
    both = lax.dot_general(
        jnp.concatenate([xh, xl], axis=0), high, dims, preferred_element_type=F32
    )
    return both[:count] + both[count:] + lax.dot_general(xh, low, dims, preferred_element_type=F32)


def exact(x, y, dims=NN):
    return lax.dot_general(x, y, dims, precision=HIGHEST, preferred_element_type=F32)


def call(kernel, outs, n_in, smem=(), raw=(), raw_out=False, scratch=(), bytes_moved=None, large=False):
    def spec(i):
        if i in raw:
            return pl.BlockSpec(memory_space=pltpu.HBM)
        return pl.BlockSpec(memory_space=pltpu.SMEM if i in smem else pltpu.VMEM)

    return pl.pallas_call(
        kernel,
        out_shape=outs,
        in_specs=[spec(i) for i in range(n_in)],
        out_specs=[
            pl.BlockSpec(memory_space=pltpu.HBM if raw_out else pltpu.VMEM) for _ in outs
        ],
        scratch_shapes=list(scratch),
        cost_estimate=bytes_moved
        and pl.CostEstimate(flops=0, transcendentals=0, bytes_accessed=bytes_moved),
        compiler_params=pltpu.CompilerParams(vmem_limit_bytes=VMEM_LARGE if large else VMEM_SMALL),
    )


def shape(*dims):
    return jax.ShapeDtypeStruct(dims, F32)


def place_of(rows_ref, odd, j):
    side = jnp.where(odd == 1, j // IFB, 1 - j // IFB)
    return rows_ref[0, side, j % IFB]


def load_blocks(blocks_hbm, high_ref, low_ref, chunk_ref, sems):
    chunks = [
        pltpu.make_async_copy(
            blocks_hbm.at[:, :, pl.ds(CHUNK * t, CHUNK)], chunk_ref.at[t], sems.at[t]
        )
        for t in range(B * B // CHUNK)
    ]
    for copy in chunks:
        copy.start()
    filler = jnp.zeros((NB * KPAD - NB * (KNZ + 1), B * B), BF16)
    high_ref[NB * (KNZ + 1) :, :] = filler
    low_ref[NB * (KNZ + 1) :, :] = filler
    for t, copy in enumerate(chunks):
        copy.wait()
        padded = jnp.concatenate([chunk_ref[t], jnp.zeros((1, NB, CHUNK), F32)], axis=0)
        wh, wl = split(padded.reshape(NB * (KNZ + 1), CHUNK))
        cut = slice(CHUNK * t, CHUNK * (t + 1))
        high_ref[: NB * (KNZ + 1), cut] = wh
        low_ref[: NB * (KNZ + 1), cut] = wl


def assemble(rows_ref, columns_ref, wh_ref, wl_ref, after_ref, high_ref, low_ref):
    odd = lax.axis_index("sub") % 2
    column = columns_ref[...]
    place = jnp.where(
        (column < NB + IFB) == (odd == 1), column % IFB + NB, column % IFB + NB + IFB
    )
    for j in range(NB):
        place = jnp.where(column == place_of(rows_ref, odd, j), j, place)
    slot = lax.broadcasted_iota(jnp.int32, (KNZ, NB * KPAD), 0)
    entry = lax.broadcasted_iota(jnp.int32, (KNZ, NB * KPAD), 1)
    widen = jnp.where(entry // NB == slot, 1.0, 0.0).astype(BF16)
    wide = lax.dot_general(place.astype(F32).astype(BF16), widen, NN, preferred_element_type=F32)
    r = lax.broadcasted_iota(jnp.int32, (NE * NB, NB * KPAD), 0)
    q = lax.broadcasted_iota(jnp.int32, (NE * NB, NB * KPAD), 1)
    hit = (jnp.concatenate([wide] * NE, axis=0) == (r // NB).astype(F32)) & (r % NB == q % NB)
    onehot = jnp.where(hit, 1.0, 0.0).astype(BF16)
    first = lax.broadcasted_iota(jnp.int32, (NB, 128), 1) < B
    for t in range(B * B // CHUNK):
        cut = slice(CHUNK * t, CHUNK * (t + 1))
        dense = lax.dot_general(
            onehot, wh_ref[:, cut], NN, preferred_element_type=F32
        ) + lax.dot_general(onehot, wl_ref[:, cut], NN, preferred_element_type=F32)
        for m in range(NE // 2):
            for h in range(CHUNK // 128):
                lane = slice(128 * h, 128 * (h + 1))
                left = dense[16 * m : 16 * m + 8, lane]
                right = dense[16 * m + 8 : 16 * m + 16, lane]
                tile = jnp.concatenate(
                    [
                        jnp.where(first, left, pltpu.roll(right, B, 1)),
                        jnp.where(first, pltpu.roll(left, B, 1), right),
                    ],
                    axis=0,
                )
                th, tl = split(tile)
                at = NB * CHUNK // B * t + 16 * h
                high_ref[at : at + 16, 128 * m : 128 * (m + 1)] = th
                low_ref[at : at + 16, 128 * m : 128 * (m + 1)] = tl


def sides(rows_ref, owner_ref, right_ref, scale_ref, after_ref, *rest, parts, ncoarse):
    basis_refs = rest[:parts]
    resid_ref, side_a_ref, side_b_ref, blk_ref = rest[parts:]
    odd = lax.axis_index("sub") % 2
    mine = lax.axis_index("rhs")
    cases = right_ref.shape[0]
    per = NCL // parts
    scale = jnp.broadcast_to(scale_ref[...], (8, OWN))
    unknown = lax.broadcasted_iota(jnp.int32, (ncoarse, OWN), 0)
    coarse = jnp.zeros((ncoarse, OWN), F32)
    for k in range(parts):
        for t in range(per):
            owner = owner_ref[0, ((mine + k) % parts) * per + t]
            coarse = coarse + jnp.where(unknown == owner, basis_refs[k][t : t + 1, :], 0.0)
    right = right_ref[...]
    fine = right * scale[0:1]
    live = cases + ncoarse
    for n in range(NB):
        cut = slice(B * n, B * (n + 1))
        blk_ref[n, 0:cases, :] = fine[:, cut]
        blk_ref[n, cases:live, :] = coarse[:, cut]
        blk_ref[n, live : live + 8, :] = scale[:, cut]
        blk_ref[n, live + 8 :, :] = right[:, cut]
    for j in range(0, NB, 2):
        pair = jnp.concatenate(
            [blk_ref[place_of(rows_ref, odd, j)], blk_ref[place_of(rows_ref, odd, j + 1)]], axis=1
        )
        target = side_a_ref if j < IFB else side_b_ref
        at = B * (j % IFB)
        target[:, at : at + 2 * B] = pair[: live + 8]
        resid_ref[:, B * j : B * (j + 2)] = pair[live + 8 :]


def first_apply(a_ref, b_ref, ga_ref, gb_ref, high_ref, low_ref, strain_ref, send_a_ref, send_b_ref):
    live = strain_ref.shape[0]
    field = jnp.concatenate([ref[:live, :] for ref in (a_ref, b_ref, ga_ref, gb_ref)], axis=1)
    strain = times(field, high_ref[...], low_ref[...], NT)
    strain_ref[...] = strain
    back = times(strain, high_ref[...], low_ref[...], NN)
    send_a_ref[:live, :] = field[:, :EDGE] + back[:, :EDGE]
    send_a_ref[live:, :] = back[:, OWN : OWN + EDGE]
    send_b_ref[:live, :] = field[:, EDGE:OWN] + back[:, EDGE:OWN]
    send_b_ref[live:, :] = back[:, OWN + EDGE :]


def first_sums(resid_ref, a_ref, b_ref, strain_ref, fixed_ref, *, cases, ncoarse):
    live = cases + ncoarse
    own = jnp.concatenate([a_ref[:live, :], b_ref[:live, :]], axis=1)
    paired = jnp.concatenate([own, strain_ref[...]], axis=1)
    gram = exact(paired, paired[cases:], NT)
    resid = resid_ref[...]
    lead = paired[:cases]
    fixed_ref[...] = jnp.zeros_like(fixed_ref)
    fixed_ref[:cases, 0:ncoarse] = exact(resid, own[cases:], NT)
    fixed_ref[:cases, ncoarse : 2 * ncoarse] = gram[:cases]
    fixed_ref[:ncoarse, 2 * ncoarse : 3 * ncoarse] = gram[cases:]
    at = 3 * ncoarse
    fixed_ref[:cases, at : at + 1] = jnp.sum(resid * own[:cases], axis=1, keepdims=True)
    fixed_ref[:cases, at + 1 : at + 2] = jnp.sum(lead * lead, axis=1, keepdims=True)


def second_apply(
    a_ref,
    b_ref,
    ga_ref,
    gb_ref,
    own_a_ref,
    own_b_ref,
    got_a_ref,
    got_b_ref,
    high_ref,
    low_ref,
    fixed_ref,
    strain_ref,
    image_ref,
    scaled_ref,
    pay_ref,
    *,
    cases,
    ncoarse,
):
    live = cases + ncoarse
    image = jnp.concatenate(
        [
            own_a_ref[:live, :] + got_a_ref[live:, :],
            own_b_ref[:live, :] + got_b_ref[live:, :],
            own_a_ref[live:, :] + got_a_ref[:live, :],
            own_b_ref[live:, :] + got_b_ref[:live, :],
        ],
        axis=1,
    )
    scale = jnp.concatenate(
        [ref[live : live + 1, :] for ref in (a_ref, b_ref, ga_ref, gb_ref)], axis=1
    )
    field = scale * image
    strain = times(field, high_ref[...], low_ref[...], NT)
    own = field[:, :OWN]
    first = image[:, :OWN]
    strain_ref[...] = strain
    image_ref[...] = first
    scaled_ref[...] = own
    paired = jnp.concatenate([own, strain], axis=1)
    gram = exact(paired, paired[cases:], NT)
    cross = exact(own, first[cases:], NT)
    lead = paired[:cases]
    pay_ref[...] = jnp.zeros_like(pay_ref)
    n = ncoarse
    pay_ref[:, 0 : 3 * n] = fixed_ref[:, 0 : 3 * n]
    pay_ref[:cases, 3 * n : 4 * n] = cross[:cases]
    pay_ref[:n, 4 * n : 5 * n] = cross[cases:]
    pay_ref[:cases, 5 * n : 6 * n] = gram[:cases]
    pay_ref[:n, 6 * n : 7 * n] = gram[cases:]
    at = 7 * n
    pay_ref[:, at : at + 2] = fixed_ref[:, 3 * n : 3 * n + 2]
    pay_ref[:cases, at + 2 : at + 3] = jnp.sum(own[:cases] * first[:cases], axis=1, keepdims=True)
    pay_ref[:cases, at + 3 : at + 4] = jnp.sum(lead * lead, axis=1, keepdims=True)


def second_image(scaled_ref, strain_ref, high_ref, low_ref, own_ref, send_a_ref, send_b_ref):
    back = times(strain_ref[...], high_ref[...], low_ref[...], NN)
    own_ref[...] = scaled_ref[...] + back[:, :OWN]
    send_a_ref[...] = back[:, OWN : OWN + EDGE]
    send_b_ref[...] = back[:, OWN + EDGE :]


def finish(
    rows_ref,
    inverse_ref,
    resid_ref,
    a_ref,
    b_ref,
    image_ref,
    scaled_ref,
    own_ref,
    got_a_ref,
    got_b_ref,
    *rest,
    cases,
    ncoarse,
    n_pay,
):
    pays = rest[:n_pay]
    field_hbm, resid2_hbm, field_ref, resid2_ref, blk_ref, sems = rest[n_pay:]
    odd = lax.axis_index("sub") % 2
    n = ncoarse
    live = cases + n
    pay = pays[0][...]
    for other in pays[1:]:
        pay = pay + other[...]

    def total(value):
        return jnp.sum(value, axis=1, keepdims=True)

    u0 = pay[:cases, 0:n]
    g12 = pay[:cases, n : 2 * n]
    g22 = pay[:n, 2 * n : 3 * n]
    g14 = pay[:cases, 3 * n : 4 * n]
    g34 = pay[:cases, 5 * n : 6 * n]
    at = 7 * n
    r0d, g11, g13, g33 = (pay[:cases, at + k : at + k + 1] for k in range(4))
    inverse = inverse_ref[...]
    y0 = exact(u0, inverse)
    y22 = exact(y0, g22)
    y24 = exact(y0, pay[:n, 4 * n : 5 * n])
    y44 = exact(y0, pay[:n, 6 * n : 7 * n])
    rz0 = r0d + total(u0 * y0)
    pq0 = g11 + total(y0 * (2.0 * g12 + y22))
    alpha = rz0 / pq0
    u1 = u0 - alpha * (g12 + y22)
    y1 = exact(u1, inverse)
    cross = g13 + total(y0 * g14)
    rz1 = (
        r0d
        - 2.0 * alpha * (g11 + total(y0 * g12))
        + alpha * alpha * (cross + total(y0 * (g14 + y24)))
        + total(u1 * y1)
    )
    beta = rz1 / rz0
    lead = 1.0 + beta
    coarse = y1 + beta * y0
    c22 = exact(y1, g22) + beta * y22
    pq1 = (
        lead * (lead * g11 + 2.0 * total(coarse * g12) - 2.0 * alpha * cross)
        + total(coarse * (c22 - 2.0 * alpha * (g14 + y24)))
        + alpha * alpha * (g33 + total(y0 * (2.0 * g34 + y44)))
    )
    alpha1 = rz1 / pq1
    lower = alpha1 * alpha
    upper = alpha + alpha1 * lead
    weights = jnp.concatenate([alpha * y0 + alpha1 * coarse, -lower * y0], axis=1)
    start = jnp.concatenate([a_ref[:live, :], b_ref[:live, :]], axis=1)
    scaled = scaled_ref[...]
    image = image_ref[...]
    image2 = own_ref[...] + jnp.concatenate([got_a_ref[...], got_b_ref[...]], axis=1)
    field = (
        upper * start[:cases]
        - lower * scaled[:cases]
        + exact(weights, jnp.concatenate([start[cases:], scaled[cases:]], axis=0))
    )
    resid2 = (
        resid_ref[...]
        - upper * image[:cases]
        + lower * image2[:cases]
        - exact(weights, jnp.concatenate([image[cases:], image2[cases:]], axis=0))
    )
    copies = []
    for k, (value, out, buf) in enumerate(
        ((field, field_hbm, field_ref), (resid2, resid2_hbm, resid2_ref))
    ):
        for j in range(NB):
            blk_ref[k, place_of(rows_ref, odd, j)] = value[:, B * j : B * (j + 1)]
        for m in range(0, NB, 2):
            buf[:, B * m : B * (m + 2)] = jnp.concatenate([blk_ref[k, m], blk_ref[k, m + 1]], axis=1)
        copies.append(pltpu.make_async_copy(buf, out, sems.at[k]))
        copies[-1].start()
    for copy in copies:
        copy.wait()


def lanes_for(width):
    return -(-width // 128) * 128


def swap(x, steps, count):
    return [lax.ppermute(x, "sub", [(i, i ^ k) for i in range(count)]) for k in steps]


def rounds_of(count):
    rounds = []
    base = 1
    while base < count:
        if base * 4 <= count:
            rounds.append((base, 2 * base, 3 * base))
            base *= 4
        else:
            rounds.append((base,))
            base *= 2
    return rounds


def across(a, b, count):
    low = lax.ppermute(a, "sub", [(i, i ^ 1) for i in range(count)])
    inner = [(i, i + 1) for i in range(1, count - 1, 2)]
    return low, lax.ppermute(b, "sub", inner + [(j, i) for i, j in inner])


def body(
    right_side,
    stiffness_blocks,
    block_columns,
    interface_rows,
    corner_owner,
    corner_basis,
    jacobi_scale,
    coarse_inverse,
):
    cases = right_side.shape[0]
    ncoarse = coarse_inverse.shape[0]
    count = lax.axis_size("sub")
    parts = lax.axis_size("rhs")
    live = cases + ncoarse
    rounds = rounds_of(count)
    run = functools.partial(call, large=live > 128)

    bases = [corner_basis] + [
        lax.ppermute(corner_basis, "rhs", [((i + k) % parts, i) for i in range(parts)])
        for k in range(1, parts)
    ]
    packed = jax.ShapeDtypeStruct((NB * KPAD, B * B), BF16)
    wh, wl = call(
        load_blocks,
        [packed, packed],
        1,
        raw=(0,),
        scratch=[
            pltpu.VMEM((B * B // CHUNK, KNZ, NB, CHUNK), F32),
            pltpu.SemaphoreType.DMA((B * B // CHUNK,)),
        ],
        bytes_moved=16 * 1024 * 1024,
        large=True,
    )(jnp.transpose(stiffness_blocks, (1, 0, 2)))
    resid, side_a, side_b = run(
        functools.partial(sides, parts=parts, ncoarse=ncoarse),
        [shape(cases, OWN), shape(live + 8, EDGE), shape(live + 8, EDGE)],
        5 + parts,
        smem=(0, 1),
        scratch=[pltpu.VMEM((NB, live + 8 + cases, B), F32)],
    )(interface_rows, corner_owner, right_side, jacobi_scale.reshape(1, OWN), wh, *bases)
    dense = jax.ShapeDtypeStruct((ROWS, EXT), BF16)
    high, low = run(assemble, [dense, dense], 5, smem=(0,))(
        interface_rows, block_columns, wh, wl, side_a
    )
    ghost_a, ghost_b = across(side_a, side_b, count)
    ends = (side_a, side_b, ghost_a, ghost_b)

    rows = max(cases, ncoarse)
    strain, own_a, own_b = run(
        first_apply, [shape(live, ROWS), shape(2 * live, EDGE), shape(2 * live, EDGE)], 6
    )(*ends, high, low)
    got_a, got_b = across(own_a, own_b, count)
    (fixed,) = run(
        functools.partial(first_sums, cases=cases, ncoarse=ncoarse),
        [shape(rows, lanes_for(3 * ncoarse + 2))],
        4,
    )(resid, side_a, side_b, strain)
    strain, image, scaled, pay = run(
        functools.partial(second_apply, cases=cases, ncoarse=ncoarse),
        [shape(live, ROWS), shape(live, OWN), shape(live, OWN), shape(rows, lanes_for(7 * ncoarse + 4))],
        11,
    )(*ends, own_a, own_b, got_a, got_b, high, low, fixed)
    for steps in rounds[:-1]:
        pay = sum(swap(pay, steps, count), pay)
    pays = [pay] + swap(pay, rounds[-1], count)
    own, back_a, back_b = run(
        second_image, [shape(live, OWN), shape(live, EDGE), shape(live, EDGE)], 4
    )(scaled, strain, high, low)
    got_a, got_b = across(back_a, back_b, count)
    return tuple(
        run(
            functools.partial(finish, cases=cases, ncoarse=ncoarse, n_pay=len(pays)),
            [shape(cases, OWN)] * 2,
            10 + len(pays),
            smem=(0,),
            raw_out=True,
            scratch=[
                pltpu.VMEM((cases, OWN), F32),
                pltpu.VMEM((cases, OWN), F32),
                pltpu.VMEM((2, NB, cases, B), F32),
                pltpu.SemaphoreType.DMA((2,)),
            ],
        )(
            interface_rows,
            coarse_inverse,
            resid,
            side_a,
            side_b,
            image,
            scaled,
            own,
            got_a,
            got_b,
            *pays,
        )
    )


def solution(mesh):
    placed = (
        P("rhs", "sub"),
        P("sub", None, None),
        P("sub", None),
        P("sub", None, None),
        P("sub", None),
        P("rhs", "sub"),
        P("sub"),
        P(),
    )
    return jax.shard_map(
        body,
        mesh=mesh,
        in_specs=placed,
        out_specs=(P("rhs", "sub"), P("rhs", "sub")),
        check_vma=False,
    )
```

```python
import functools

import jax
import jax.numpy as jnp
from jax import lax
from jax.experimental import pallas as pl
from jax.experimental.pallas import tpu as pltpu
from jax.sharding import PartitionSpec as P

B = 64
KNZ = 27
IFB = 4
NCL = 8
NB = 2 * IFB
NE = NB + 2 * IFB
EDGE = IFB * B
OWN = NB * B
EXT = NE * B
ROWS = NB * B
KPAD = 32
F32 = jnp.float32
BF16 = jnp.bfloat16
HIGHEST = lax.Precision.HIGHEST
NT = (((1,), (1,)), ((), ()))
NN = (((1,), (0,)), ((), ()))
VMEM_SMALL = 16 * 1024 * 1024
VMEM_LARGE = 48 * 1024 * 1024
CHUNK = 512


def split(x):
    high = x.astype(BF16)
    return high, (x - high.astype(F32)).astype(BF16)


def times(x, high, low, dims):
    count = x.shape[0]
    xh, xl = split(x)
    both = lax.dot_general(
        jnp.concatenate([xh, xl], axis=0), high, dims, preferred_element_type=F32
    )
    return both[:count] + both[count:] + lax.dot_general(xh, low, dims, preferred_element_type=F32)


def exact(x, y, dims=NN):
    return lax.dot_general(x, y, dims, precision=HIGHEST, preferred_element_type=F32)


def call(kernel, outs, n_in, smem=(), raw=(), raw_out=False, scratch=(), bytes_moved=None, large=False):
    def spec(i):
        if i in raw:
            return pl.BlockSpec(memory_space=pltpu.HBM)
        return pl.BlockSpec(memory_space=pltpu.SMEM if i in smem else pltpu.VMEM)

    return pl.pallas_call(
        kernel,
        out_shape=outs,
        in_specs=[spec(i) for i in range(n_in)],
        out_specs=[
            pl.BlockSpec(memory_space=pltpu.HBM if raw_out else pltpu.VMEM) for _ in outs
        ],
        scratch_shapes=list(scratch),
        cost_estimate=bytes_moved
        and pl.CostEstimate(flops=0, transcendentals=0, bytes_accessed=bytes_moved),
        compiler_params=pltpu.CompilerParams(vmem_limit_bytes=VMEM_LARGE if large else VMEM_SMALL),
    )


def shape(*dims):
    return jax.ShapeDtypeStruct(dims, F32)


def place_of(rows_ref, odd, j):
    side = jnp.where(odd == 1, j // IFB, 1 - j // IFB)
    return rows_ref[0, side, j % IFB]


def load_blocks(blocks_hbm, high_ref, low_ref, chunk_ref, sems):
    chunks = [
        pltpu.make_async_copy(
            blocks_hbm.at[:, :, pl.ds(CHUNK * t, CHUNK)], chunk_ref.at[t], sems.at[t]
        )
        for t in range(B * B // CHUNK)
    ]
    for copy in chunks:
        copy.start()
    filler = jnp.zeros((NB * KPAD - NB * (KNZ + 1), B * B), BF16)
    high_ref[NB * (KNZ + 1) :, :] = filler
    low_ref[NB * (KNZ + 1) :, :] = filler
    for t, copy in enumerate(chunks):
        copy.wait()
        padded = jnp.concatenate([chunk_ref[t], jnp.zeros((1, NB, CHUNK), F32)], axis=0)
        wh, wl = split(padded.reshape(NB * (KNZ + 1), CHUNK))
        cut = slice(CHUNK * t, CHUNK * (t + 1))
        high_ref[: NB * (KNZ + 1), cut] = wh
        low_ref[: NB * (KNZ + 1), cut] = wl


def assemble(rows_ref, columns_ref, wh_ref, wl_ref, after_ref, high_ref, low_ref):
    odd = lax.axis_index("sub") % 2
    column = columns_ref[...]
    place = jnp.where(
        (column < NB + IFB) == (odd == 1), column % IFB + NB, column % IFB + NB + IFB
    )
    for j in range(NB):
        place = jnp.where(column == place_of(rows_ref, odd, j), j, place)
    slot = lax.broadcasted_iota(jnp.int32, (KNZ, NB * KPAD), 0)
    entry = lax.broadcasted_iota(jnp.int32, (KNZ, NB * KPAD), 1)
    widen = jnp.where(entry // NB == slot, 1.0, 0.0).astype(BF16)
    wide = lax.dot_general(place.astype(F32).astype(BF16), widen, NN, preferred_element_type=F32)
    r = lax.broadcasted_iota(jnp.int32, (NE * NB, NB * KPAD), 0)
    q = lax.broadcasted_iota(jnp.int32, (NE * NB, NB * KPAD), 1)
    hit = (jnp.concatenate([wide] * NE, axis=0) == (r // NB).astype(F32)) & (r % NB == q % NB)
    onehot = jnp.where(hit, 1.0, 0.0).astype(BF16)
    first = lax.broadcasted_iota(jnp.int32, (NB, 128), 1) < B
    for t in range(B * B // CHUNK):
        cut = slice(CHUNK * t, CHUNK * (t + 1))
        dense = lax.dot_general(
            onehot, wh_ref[:, cut], NN, preferred_element_type=F32
        ) + lax.dot_general(onehot, wl_ref[:, cut], NN, preferred_element_type=F32)
        for m in range(NE // 2):
            for h in range(CHUNK // 128):
                lane = slice(128 * h, 128 * (h + 1))
                left = dense[16 * m : 16 * m + 8, lane]
                right = dense[16 * m + 8 : 16 * m + 16, lane]
                tile = jnp.concatenate(
                    [
                        jnp.where(first, left, pltpu.roll(right, B, 1)),
                        jnp.where(first, pltpu.roll(left, B, 1), right),
                    ],
                    axis=0,
                )
                th, tl = split(tile)
                at = NB * CHUNK // B * t + 16 * h
                high_ref[at : at + 16, 128 * m : 128 * (m + 1)] = th
                low_ref[at : at + 16, 128 * m : 128 * (m + 1)] = tl


def sides(rows_ref, owner_ref, right_ref, scale_ref, after_ref, *rest, parts, ncoarse):
    basis_refs = rest[:parts]
    resid_ref, side_a_ref, side_b_ref, blk_ref = rest[parts:]
    odd = lax.axis_index("sub") % 2
    mine = lax.axis_index("rhs")
    cases = right_ref.shape[0]
    per = NCL // parts
    scale = jnp.broadcast_to(scale_ref[...], (8, OWN))
    unknown = lax.broadcasted_iota(jnp.int32, (ncoarse, OWN), 0)
    coarse = jnp.zeros((ncoarse, OWN), F32)
    for k in range(parts):
        for t in range(per):
            owner = owner_ref[0, ((mine + k) % parts) * per + t]
            coarse = coarse + jnp.where(unknown == owner, basis_refs[k][t : t + 1, :], 0.0)
    right = right_ref[...]
    fine = right * scale[0:1]
    live = cases + ncoarse
    for n in range(NB):
        cut = slice(B * n, B * (n + 1))
        blk_ref[n, 0:cases, :] = fine[:, cut]
        blk_ref[n, cases:live, :] = coarse[:, cut]
        blk_ref[n, live : live + 8, :] = scale[:, cut]
        blk_ref[n, live + 8 :, :] = right[:, cut]
    for j in range(0, NB, 2):
        pair = jnp.concatenate(
            [blk_ref[place_of(rows_ref, odd, j)], blk_ref[place_of(rows_ref, odd, j + 1)]], axis=1
        )
        target = side_a_ref if j < IFB else side_b_ref
        at = B * (j % IFB)
        target[:, at : at + 2 * B] = pair[: live + 8]
        resid_ref[:, B * j : B * (j + 2)] = pair[live + 8 :]


def first_apply(a_ref, b_ref, ga_ref, gb_ref, high_ref, low_ref, strain_ref, send_a_ref, send_b_ref):
    live = strain_ref.shape[0]
    field = jnp.concatenate(
        [a_ref[:live, :], b_ref[:live, :], ga_ref[:live, :], inside() * gb_ref[:live, :]], axis=1
    )
    strain = times(field, high_ref[...], low_ref[...], NT)
    strain_ref[...] = strain
    back = times(strain, high_ref[...], low_ref[...], NN)
    send_a_ref[:live, :] = field[:, :EDGE] + back[:, :EDGE]
    send_a_ref[live:, :] = back[:, OWN : OWN + EDGE]
    send_b_ref[:live, :] = field[:, EDGE:OWN] + back[:, EDGE:OWN]
    send_b_ref[live:, :] = back[:, OWN + EDGE :]


def first_sums(resid_ref, a_ref, b_ref, strain_ref, fixed_ref, *, cases, ncoarse):
    live = cases + ncoarse
    own = jnp.concatenate([a_ref[:live, :], b_ref[:live, :]], axis=1)
    paired = jnp.concatenate([own, strain_ref[...]], axis=1)
    gram = exact(paired, paired[cases:], NT)
    resid = resid_ref[...]
    lead = paired[:cases]
    fixed_ref[...] = jnp.zeros_like(fixed_ref)
    fixed_ref[:cases, 0:ncoarse] = exact(resid, own[cases:], NT)
    fixed_ref[:cases, ncoarse : 2 * ncoarse] = gram[:cases]
    fixed_ref[:ncoarse, 2 * ncoarse : 3 * ncoarse] = gram[cases:]
    at = 3 * ncoarse
    fixed_ref[:cases, at : at + 1] = jnp.sum(resid * own[:cases], axis=1, keepdims=True)
    fixed_ref[:cases, at + 1 : at + 2] = jnp.sum(lead * lead, axis=1, keepdims=True)


def second_apply(
    a_ref,
    b_ref,
    ga_ref,
    gb_ref,
    own_a_ref,
    own_b_ref,
    got_a_ref,
    got_b_ref,
    high_ref,
    low_ref,
    fixed_ref,
    strain_ref,
    image_ref,
    scaled_ref,
    pay_ref,
    *,
    cases,
    ncoarse,
):
    live = cases + ncoarse
    inner = inside()
    image = jnp.concatenate(
        [
            own_a_ref[:live, :] + got_a_ref[live:, :],
            own_b_ref[:live, :] + inner * got_b_ref[live:, :],
            own_a_ref[live:, :] + got_a_ref[:live, :],
            own_b_ref[live:, :] + got_b_ref[:live, :],
        ],
        axis=1,
    )
    end = slice(live, live + 1)
    scale = jnp.concatenate(
        [a_ref[end, :], b_ref[end, :], ga_ref[end, :], inner * gb_ref[end, :]], axis=1
    )
    field = scale * image
    strain = times(field, high_ref[...], low_ref[...], NT)
    own = field[:, :OWN]
    first = image[:, :OWN]
    strain_ref[...] = strain
    image_ref[...] = first
    scaled_ref[...] = own
    paired = jnp.concatenate([own, strain], axis=1)
    gram = exact(paired, paired[cases:], NT)
    cross = exact(own, first[cases:], NT)
    lead = paired[:cases]
    pay_ref[...] = jnp.zeros_like(pay_ref)
    n = ncoarse
    pay_ref[:, 0 : 3 * n] = fixed_ref[:, 0 : 3 * n]
    pay_ref[:cases, 3 * n : 4 * n] = cross[:cases]
    pay_ref[:n, 4 * n : 5 * n] = cross[cases:]
    pay_ref[:cases, 5 * n : 6 * n] = gram[:cases]
    pay_ref[:n, 6 * n : 7 * n] = gram[cases:]
    at = 7 * n
    pay_ref[:, at : at + 2] = fixed_ref[:, 3 * n : 3 * n + 2]
    pay_ref[:cases, at + 2 : at + 3] = jnp.sum(own[:cases] * first[:cases], axis=1, keepdims=True)
    pay_ref[:cases, at + 3 : at + 4] = jnp.sum(lead * lead, axis=1, keepdims=True)


def second_image(scaled_ref, strain_ref, high_ref, low_ref, own_ref, send_a_ref, send_b_ref):
    back = times(strain_ref[...], high_ref[...], low_ref[...], NN)
    own_ref[...] = scaled_ref[...] + back[:, :OWN]
    send_a_ref[...] = back[:, OWN : OWN + EDGE]
    send_b_ref[...] = back[:, OWN + EDGE :]


def finish(
    rows_ref,
    inverse_ref,
    resid_ref,
    a_ref,
    b_ref,
    image_ref,
    scaled_ref,
    own_ref,
    got_a_ref,
    got_b_ref,
    *rest,
    cases,
    ncoarse,
    n_pay,
):
    pays = rest[:n_pay]
    field_hbm, resid2_hbm, field_ref, resid2_ref, blk_ref, sems = rest[n_pay:]
    odd = lax.axis_index("sub") % 2
    n = ncoarse
    live = cases + n
    pay = pays[0][...]
    for other in pays[1:]:
        pay = pay + other[...]

    def total(value):
        return jnp.sum(value, axis=1, keepdims=True)

    u0 = pay[:cases, 0:n]
    g12 = pay[:cases, n : 2 * n]
    g22 = pay[:n, 2 * n : 3 * n]
    g14 = pay[:cases, 3 * n : 4 * n]
    g34 = pay[:cases, 5 * n : 6 * n]
    at = 7 * n
    r0d, g11, g13, g33 = (pay[:cases, at + k : at + k + 1] for k in range(4))
    inverse = inverse_ref[...]
    y0 = exact(u0, inverse)
    y22 = exact(y0, g22)
    y24 = exact(y0, pay[:n, 4 * n : 5 * n])
    y44 = exact(y0, pay[:n, 6 * n : 7 * n])
    rz0 = r0d + total(u0 * y0)
    pq0 = g11 + total(y0 * (2.0 * g12 + y22))
    alpha = rz0 / pq0
    u1 = u0 - alpha * (g12 + y22)
    y1 = exact(u1, inverse)
    cross = g13 + total(y0 * g14)
    rz1 = (
        r0d
        - 2.0 * alpha * (g11 + total(y0 * g12))
        + alpha * alpha * (cross + total(y0 * (g14 + y24)))
        + total(u1 * y1)
    )
    beta = rz1 / rz0
    lead = 1.0 + beta
    coarse = y1 + beta * y0
    c22 = exact(y1, g22) + beta * y22
    pq1 = (
        lead * (lead * g11 + 2.0 * total(coarse * g12) - 2.0 * alpha * cross)
        + total(coarse * (c22 - 2.0 * alpha * (g14 + y24)))
        + alpha * alpha * (g33 + total(y0 * (2.0 * g34 + y44)))
    )
    alpha1 = rz1 / pq1
    lower = alpha1 * alpha
    upper = alpha + alpha1 * lead
    weights = jnp.concatenate([alpha * y0 + alpha1 * coarse, -lower * y0], axis=1)
    start = jnp.concatenate([a_ref[:live, :], b_ref[:live, :]], axis=1)
    scaled = scaled_ref[...]
    image = image_ref[...]
    image2 = own_ref[...] + jnp.concatenate([got_a_ref[...], inside() * got_b_ref[...]], axis=1)
    field = (
        upper * start[:cases]
        - lower * scaled[:cases]
        + exact(weights, jnp.concatenate([start[cases:], scaled[cases:]], axis=0))
    )
    resid2 = (
        resid_ref[...]
        - upper * image[:cases]
        + lower * image2[:cases]
        - exact(weights, jnp.concatenate([image[cases:], image2[cases:]], axis=0))
    )
    copies = []
    for k, (value, out, buf) in enumerate(
        ((field, field_hbm, field_ref), (resid2, resid2_hbm, resid2_ref))
    ):
        for j in range(NB):
            blk_ref[k, place_of(rows_ref, odd, j)] = value[:, B * j : B * (j + 1)]
        for m in range(0, NB, 2):
            buf[:, B * m : B * (m + 2)] = jnp.concatenate([blk_ref[k, m], blk_ref[k, m + 1]], axis=1)
        copies.append(pltpu.make_async_copy(buf, out, sems.at[k]))
        copies[-1].start()
    for copy in copies:
        copy.wait()


def lanes_for(width):
    return -(-width // 128) * 128


def swap(x, steps, count):
    return [lax.ppermute(x, "sub", [(i, i ^ k) for i in range(count)]) for k in steps]


def rounds_of(count):
    rounds = []
    base = 1
    while base < count:
        turn = 1 if base > 1 else 0
        if base * 4 <= count:
            rounds.append((base, 2 * base + turn, 3 * base + turn))
            base *= 4
        else:
            rounds.append((base,))
            base *= 2
    return rounds


def across(a, b, count, parts):
    low = lax.ppermute(a, "sub", [(i, i ^ 1) for i in range(count)])
    inner = [(i, i + 1) for i in range(1, count - 1, 2)]
    pairs = [(i * parts + x, j * parts + x) for i, j in inner for x in range(parts)]
    ends = [(i * parts + x, i * parts + x + 1) for i in (0, count - 1) for x in range(0, parts - 1, 2)]
    pairs += ends
    return low, lax.ppermute(b, ("sub", "rhs"), pairs + [(j, i) for i, j in pairs])


def inside():
    place = lax.axis_index("sub")
    return jnp.where((place == 0) | (place == lax.axis_size("sub") - 1), 0.0, 1.0)


def body(
    right_side,
    stiffness_blocks,
    block_columns,
    interface_rows,
    corner_owner,
    corner_basis,
    jacobi_scale,
    coarse_inverse,
):
    cases = right_side.shape[0]
    ncoarse = coarse_inverse.shape[0]
    count = lax.axis_size("sub")
    parts = lax.axis_size("rhs")
    live = cases + ncoarse
    rounds = rounds_of(count)
    run = functools.partial(call, large=live > 128)

    bases = [corner_basis] + [
        lax.ppermute(corner_basis, "rhs", [((i + k) % parts, i) for i in range(parts)])
        for k in range(1, parts)
    ]
    packed = jax.ShapeDtypeStruct((NB * KPAD, B * B), BF16)
    wh, wl = call(
        load_blocks,
        [packed, packed],
        1,
        raw=(0,),
        scratch=[
            pltpu.VMEM((B * B // CHUNK, KNZ, NB, CHUNK), F32),
            pltpu.SemaphoreType.DMA((B * B // CHUNK,)),
        ],
        bytes_moved=16 * 1024 * 1024,
        large=True,
    )(jnp.transpose(stiffness_blocks, (1, 0, 2)))
    resid, side_a, side_b = run(
        functools.partial(sides, parts=parts, ncoarse=ncoarse),
        [shape(cases, OWN), shape(live + 8, EDGE), shape(live + 8, EDGE)],
        5 + parts,
        smem=(0, 1),
        scratch=[pltpu.VMEM((NB, live + 8 + cases, B), F32)],
    )(interface_rows, corner_owner, right_side, jacobi_scale.reshape(1, OWN), wh, *bases)
    dense = jax.ShapeDtypeStruct((ROWS, EXT), BF16)
    high, low = run(assemble, [dense, dense], 5, smem=(0,))(
        interface_rows, block_columns, wh, wl, side_a
    )
    ghost_a, ghost_b = across(side_a, side_b, count, parts)
    ends = (side_a, side_b, ghost_a, ghost_b)

    rows = max(cases, ncoarse)
    strain, own_a, own_b = run(
        first_apply, [shape(live, ROWS), shape(2 * live, EDGE), shape(2 * live, EDGE)], 6
    )(*ends, high, low)
    got_a, got_b = across(own_a, own_b, count, parts)
    (fixed,) = run(
        functools.partial(first_sums, cases=cases, ncoarse=ncoarse),
        [shape(rows, lanes_for(3 * ncoarse + 2))],
        4,
    )(resid, side_a, side_b, strain)
    strain, image, scaled, pay = run(
        functools.partial(second_apply, cases=cases, ncoarse=ncoarse),
        [shape(live, ROWS), shape(live, OWN), shape(live, OWN), shape(rows, lanes_for(7 * ncoarse + 4))],
        11,
    )(*ends, own_a, own_b, got_a, got_b, high, low, fixed)
    for steps in rounds[:-1]:
        pay = sum(swap(pay, steps, count), pay)
    pays = [pay] + swap(pay, rounds[-1], count)
    own, back_a, back_b = run(
        second_image, [shape(live, OWN), shape(live, EDGE), shape(live, EDGE)], 4
    )(scaled, strain, high, low)
    got_a, got_b = across(back_a, back_b, count, parts)
    return tuple(
        run(
            functools.partial(finish, cases=cases, ncoarse=ncoarse, n_pay=len(pays)),
            [shape(cases, OWN)] * 2,
            10 + len(pays),
            smem=(0,),
            raw_out=True,
            scratch=[
                pltpu.VMEM((cases, OWN), F32),
                pltpu.VMEM((cases, OWN), F32),
                pltpu.VMEM((2, NB, cases, B), F32),
                pltpu.SemaphoreType.DMA((2,)),
            ],
        )(
            interface_rows,
            coarse_inverse,
            resid,
            side_a,
            side_b,
            image,
            scaled,
            own,
            got_a,
            got_b,
            *pays,
        )
    )


def solution(mesh):
    placed = (
        P("rhs", "sub"),
        P("sub", None, None),
        P("sub", None),
        P("sub", None, None),
        P("sub", None),
        P("rhs", "sub"),
        P("sub"),
        P(),
    )
    return jax.shard_map(
        body,
        mesh=mesh,
        in_specs=placed,
        out_specs=(P("rhs", "sub"), P("rhs", "sub")),
        check_vma=False,
    )
```

```python
import functools

import jax
import jax.numpy as jnp
from jax import lax
from jax.experimental import pallas as pl
from jax.experimental.pallas import tpu as pltpu
from jax.sharding import PartitionSpec as P

B = 64
KNZ = 27
IFB = 4
NCL = 8
NB = 2 * IFB
NE = NB + 2 * IFB
EDGE = IFB * B
OWN = NB * B
EXT = NE * B
ROWS = NB * B
KPAD = 32
F32 = jnp.float32
BF16 = jnp.bfloat16
HIGHEST = lax.Precision.HIGHEST
NT = (((1,), (1,)), ((), ()))
NN = (((1,), (0,)), ((), ()))
VMEM_SMALL = 16 * 1024 * 1024
VMEM_LARGE = 48 * 1024 * 1024
CHUNK = 512
STEP = 2
FRAME = 16
WIDE = 24
TN = (((0,), (0,)), ((), ()))


def split(x):
    high = x.astype(BF16)
    return high, (x - high.astype(F32)).astype(BF16)


def times(x, high, low, dims):
    count = x.shape[0]
    xh, xl = split(x)
    both = lax.dot_general(
        jnp.concatenate([xh, xl], axis=0), high, dims, preferred_element_type=F32
    )
    return both[:count] + both[count:] + lax.dot_general(xh, low, dims, preferred_element_type=F32)


def exact(x, y, dims=NN):
    return lax.dot_general(x, y, dims, precision=HIGHEST, preferred_element_type=F32)


def call(kernel, outs, n_in, smem=(), raw=(), raw_out=False, scratch=(), bytes_moved=None, large=False):
    def spec(i):
        if i in raw:
            return pl.BlockSpec(memory_space=pltpu.HBM)
        return pl.BlockSpec(memory_space=pltpu.SMEM if i in smem else pltpu.VMEM)

    return pl.pallas_call(
        kernel,
        out_shape=outs,
        in_specs=[spec(i) for i in range(n_in)],
        out_specs=[
            pl.BlockSpec(memory_space=pltpu.HBM if raw_out else pltpu.VMEM) for _ in outs
        ],
        scratch_shapes=list(scratch),
        cost_estimate=bytes_moved
        and pl.CostEstimate(flops=0, transcendentals=0, bytes_accessed=bytes_moved),
        compiler_params=pltpu.CompilerParams(vmem_limit_bytes=VMEM_LARGE if large else VMEM_SMALL),
    )


def shape(*dims):
    return jax.ShapeDtypeStruct(dims, F32)


def place_of(rows_ref, odd, j):
    side = jnp.where(odd == 1, j // IFB, 1 - j // IFB)
    return rows_ref[0, side, j % IFB]


def load_blocks(blocks_hbm, high_ref, low_ref, chunk_ref, sems):
    chunks = [
        pltpu.make_async_copy(
            blocks_hbm.at[:, :, pl.ds(CHUNK * t, CHUNK)], chunk_ref.at[t], sems.at[t]
        )
        for t in range(B * B // CHUNK)
    ]
    for copy in chunks:
        copy.start()
    filler = jnp.zeros((NB * KPAD - NB * (KNZ + 1), B * B), BF16)
    high_ref[NB * (KNZ + 1) :, :] = filler
    low_ref[NB * (KNZ + 1) :, :] = filler
    for t, copy in enumerate(chunks):
        copy.wait()
        padded = jnp.concatenate([chunk_ref[t], jnp.zeros((1, NB, CHUNK), F32)], axis=0)
        wh, wl = split(padded.reshape(NB * (KNZ + 1), CHUNK))
        cut = slice(CHUNK * t, CHUNK * (t + 1))
        high_ref[: NB * (KNZ + 1), cut] = wh
        low_ref[: NB * (KNZ + 1), cut] = wl


def assemble(rows_ref, columns_ref, wh_ref, wl_ref, after_ref, high_ref, low_ref):
    odd = lax.axis_index("sub") % 2
    column = columns_ref[...]
    place = jnp.where(
        (column < NB + IFB) == (odd == 1), column % IFB + NB, column % IFB + NB + IFB
    )
    for j in range(NB):
        place = jnp.where(column == place_of(rows_ref, odd, j), j, place)
    slot = lax.broadcasted_iota(jnp.int32, (KNZ, NB * KPAD), 0)
    entry = lax.broadcasted_iota(jnp.int32, (KNZ, NB * KPAD), 1)
    widen = jnp.where(entry // NB == slot, 1.0, 0.0).astype(BF16)
    wide = lax.dot_general(place.astype(F32).astype(BF16), widen, NN, preferred_element_type=F32)
    r = lax.broadcasted_iota(jnp.int32, (NE * NB, NB * KPAD), 0)
    q = lax.broadcasted_iota(jnp.int32, (NE * NB, NB * KPAD), 1)
    hit = (jnp.concatenate([wide] * NE, axis=0) == (r // NB).astype(F32)) & (r % NB == q % NB)
    onehot = jnp.where(hit, 1.0, 0.0).astype(BF16)
    first = lax.broadcasted_iota(jnp.int32, (NB, 128), 1) < B
    for t in range(B * B // CHUNK):
        cut = slice(CHUNK * t, CHUNK * (t + 1))
        dense = lax.dot_general(
            onehot, wh_ref[:, cut], NN, preferred_element_type=F32
        ) + lax.dot_general(onehot, wl_ref[:, cut], NN, preferred_element_type=F32)
        for m in range(NE // 2):
            for h in range(CHUNK // 128):
                lane = slice(128 * h, 128 * (h + 1))
                left = dense[16 * m : 16 * m + 8, lane]
                right = dense[16 * m + 8 : 16 * m + 16, lane]
                tile = jnp.concatenate(
                    [
                        jnp.where(first, left, pltpu.roll(right, B, 1)),
                        jnp.where(first, pltpu.roll(left, B, 1), right),
                    ],
                    axis=0,
                )
                th, tl = split(tile)
                at = NB * CHUNK // B * t + 16 * h
                high_ref[at : at + 16, 128 * m : 128 * (m + 1)] = th
                low_ref[at : at + 16, 128 * m : 128 * (m + 1)] = tl


def sides(rows_ref, owner_ref, right_ref, scale_ref, after_ref, *rest, parts):
    basis_refs = rest[:parts]
    resid_ref, side_a_ref, side_b_ref, blk_ref = rest[parts:]
    odd = lax.axis_index("sub") % 2
    mine = lax.axis_index("rhs")
    cases = right_ref.shape[0]
    per = NCL // parts
    scale = jnp.broadcast_to(scale_ref[...], (8, OWN))
    unknown = lax.broadcasted_iota(jnp.int32, (FRAME, OWN), 0) + frame_start()
    coarse = jnp.zeros((FRAME, OWN), F32)
    for k in range(parts):
        for t in range(per):
            owner = owner_ref[0, ((mine + k) % parts) * per + t]
            coarse = coarse + jnp.where(unknown == owner, basis_refs[k][t : t + 1, :], 0.0)
    right = right_ref[...]
    fine = right * scale[0:1]
    live = cases + FRAME
    for n in range(NB):
        cut = slice(B * n, B * (n + 1))
        blk_ref[n, 0:cases, :] = fine[:, cut]
        blk_ref[n, cases:live, :] = coarse[:, cut]
        blk_ref[n, live : live + 8, :] = scale[:, cut]
        blk_ref[n, live + 8 :, :] = right[:, cut]
    for j in range(0, NB, 2):
        pair = jnp.concatenate(
            [blk_ref[place_of(rows_ref, odd, j)], blk_ref[place_of(rows_ref, odd, j + 1)]], axis=1
        )
        target = side_a_ref if j < IFB else side_b_ref
        at = B * (j % IFB)
        target[:, at : at + 2 * B] = pair[: live + 8]
        resid_ref[:, B * j : B * (j + 2)] = pair[live + 8 :]


def frame_start():
    return STEP * lax.axis_index("sub") - 6


def turned(rows, upper):
    up = pltpu.roll(rows, STEP, 0)
    down = pltpu.roll(rows, rows.shape[0] - STEP, 0)
    return jnp.where(upper, up, down)


def arrived(rows, upper):
    cases = rows.shape[0] - FRAME
    return jnp.concatenate([rows[:cases], turned(rows[cases:], upper)], axis=0)


def first_apply(a_ref, b_ref, ga_ref, gb_ref, high_ref, low_ref, strain_ref, send_a_ref, send_b_ref):
    live = strain_ref.shape[0]
    odd = lax.axis_index("sub") % 2 == 1
    field = jnp.concatenate(
        [
            a_ref[:live, :],
            b_ref[:live, :],
            arrived(ga_ref[:live, :], jnp.logical_not(odd)),
            arrived(inside() * gb_ref[:live, :], odd),
        ],
        axis=1,
    )
    strain = times(field, high_ref[...], low_ref[...], NT)
    strain_ref[...] = strain
    back = times(strain, high_ref[...], low_ref[...], NN)
    send_a_ref[:live, :] = field[:, :EDGE] + back[:, :EDGE]
    send_a_ref[live:, :] = back[:, OWN : OWN + EDGE]
    send_b_ref[:live, :] = field[:, EDGE:OWN] + back[:, EDGE:OWN]
    send_b_ref[live:, :] = back[:, OWN + EDGE :]


def to_lanes(block, wide_ref):
    width = wide_ref.shape[1]
    wide_ref[...] = jnp.zeros_like(wide_ref)
    wide_ref[:, :FRAME] = block
    return pltpu.roll(wide_ref[...], (frame_start() + width) % width, 1)


def row_sums(value):
    return exact(jnp.ones((8, value.shape[1]), F32), value, NT)[0:1]


def first_sums(resid_ref, a_ref, b_ref, strain_ref, frame_ref, scalar_ref, wide_ref, *, ncoarse):
    live = strain_ref.shape[0]
    cases = live - FRAME
    own = jnp.concatenate([a_ref[:live, :], b_ref[:live, :]], axis=1)
    paired = jnp.concatenate([own, strain_ref[...]], axis=1)
    gram = exact(paired[cases:], paired, NT)
    resid = resid_ref[...]
    lead = paired[:cases]
    width = cases + ncoarse
    frame_ref[...] = jnp.zeros_like(frame_ref)
    frame_ref[:, 0:cases] = gram[:, :cases]
    frame_ref[:, cases:width] = to_lanes(gram[:, cases:], wide_ref)[:, :ncoarse]
    frame_ref[:, 3 * width : 3 * width + cases] = exact(own[cases:], resid, NT)
    scalar_ref[...] = jnp.zeros_like(scalar_ref)
    scalar_ref[0:1, :] = row_sums(resid * own[:cases])
    scalar_ref[1:2, :] = row_sums(lead * lead)


def second_apply(
    a_ref,
    b_ref,
    ga_ref,
    gb_ref,
    own_a_ref,
    own_b_ref,
    got_a_ref,
    got_b_ref,
    high_ref,
    low_ref,
    frame_ref,
    scalar_ref,
    strain_ref,
    image_ref,
    scaled_ref,
    pay_ref,
    wide_ref,
    tall_ref,
    *,
    ncoarse,
):
    live = strain_ref.shape[0]
    cases = live - FRAME
    odd = lax.axis_index("sub") % 2 == 1
    even = jnp.logical_not(odd)
    inner = inside()
    image = jnp.concatenate(
        [
            own_a_ref[:live, :] + arrived(got_a_ref[live:, :], even),
            own_b_ref[:live, :] + inner * arrived(got_b_ref[live:, :], odd),
            own_a_ref[live:, :] + arrived(got_a_ref[:live, :], even),
            own_b_ref[live:, :] + arrived(got_b_ref[:live, :], odd),
        ],
        axis=1,
    )
    end = slice(live, live + 1)
    scale = jnp.concatenate(
        [a_ref[end, :], b_ref[end, :], ga_ref[end, :], inner * gb_ref[end, :]], axis=1
    )
    field = scale * image
    strain = times(field, high_ref[...], low_ref[...], NT)
    own = field[:, :OWN]
    first = image[:, :OWN]
    strain_ref[...] = strain
    image_ref[...] = first
    scaled_ref[...] = own
    paired = jnp.concatenate([own, strain], axis=1)
    gram = exact(paired[cases:], paired, NT)
    cross = exact(first[cases:], own, NT)
    lead = paired[:cases]
    width = cases + ncoarse
    tall_ref[...] = jnp.zeros_like(tall_ref)
    tall_ref[:FRAME, :] = frame_ref[...]
    for at, block in ((width, cross), (2 * width, gram)):
        tall_ref[:FRAME, at : at + cases] = block[:, :cases]
        tall_ref[:FRAME, at + cases : at + width] = to_lanes(block[:, cases:], wide_ref)[:, :ncoarse]
    pay_ref[...] = pltpu.roll(tall_ref[...], (frame_start() + ncoarse) % ncoarse, 0)
    at = 3 * width + cases
    pay_ref[0:8, at : at + cases] = scalar_ref[...]
    pay_ref[2:3, at : at + cases] = row_sums(own[:cases] * first[:cases])
    pay_ref[3:4, at : at + cases] = row_sums(lead * lead)


def second_image(scaled_ref, strain_ref, high_ref, low_ref, own_ref, send_a_ref, send_b_ref):
    back = times(strain_ref[...], high_ref[...], low_ref[...], NN)
    own_ref[...] = scaled_ref[...] + back[:, :OWN]
    send_a_ref[...] = back[:, OWN : OWN + EDGE]
    send_b_ref[...] = back[:, OWN + EDGE :]


def window(value, start, count):
    rows = value.shape[0] + 32
    longer = jnp.concatenate([value, jnp.zeros((32, value.shape[1]), F32)], axis=0)
    return pltpu.roll(longer, (rows - start) % rows, 0)[:count]


def widened(own, got_a, got_b, even):
    gap = WIDE - FRAME

    def placed(rows, upper):
        none = jnp.zeros((gap, rows.shape[1]), F32)
        low = jnp.concatenate([rows, none], axis=0)
        return jnp.where(upper, pltpu.roll(low, 2 * STEP, 0), low)

    none = jnp.zeros((gap, own.shape[1]), F32)
    middle = pltpu.roll(jnp.concatenate([own, none], axis=0), STEP, 0)
    return middle + jnp.concatenate(
        [placed(got_a, even), placed(got_b, jnp.logical_not(even))], axis=1
    )


def finish(
    rows_ref,
    inverse_ref,
    resid_ref,
    a_ref,
    b_ref,
    image_ref,
    scaled_ref,
    own_ref,
    got_a_ref,
    got_b_ref,
    *rest,
    ncoarse,
    n_pay,
):
    pays = rest[:n_pay]
    field_hbm, resid2_hbm, field_ref, resid2_ref, blk_ref, sems = rest[n_pay:]
    odd = lax.axis_index("sub") % 2
    live = own_ref.shape[0]
    cases = live - FRAME
    width = cases + ncoarse
    pay = pays[0][...]
    for other in pays[1:]:
        pay = pay + other[...]

    def total(value):
        return jnp.sum(value, axis=0, keepdims=True)

    def piece(k):
        at = (k // 2) * width + (k % 2) * cases
        return pay[:, at : at + (ncoarse if k % 2 and k < 6 else cases)]

    g12, g22, g14, g24, g34, g44, u0, scalars = (piece(k) for k in range(8))
    r0d, g11, g13, g33 = (scalars[k : k + 1] for k in range(4))
    inverse = inverse_ref[...]
    y0 = exact(inverse, u0)
    stacked = exact(jnp.concatenate([g22, g24, g44], axis=0), y0)
    y22, y24, y44 = (stacked[k * ncoarse : (k + 1) * ncoarse] for k in range(3))
    rz0 = r0d + total(u0 * y0)
    pq0 = g11 + total(y0 * (2.0 * g12 + y22))
    alpha = rz0 / pq0
    u1 = u0 - alpha * (g12 + y22)
    y1 = exact(inverse, u1)
    cross = g13 + total(y0 * g14)
    rz1 = (
        r0d
        - 2.0 * alpha * (g11 + total(y0 * g12))
        + alpha * alpha * (cross + total(y0 * (g14 + y24)))
        + total(u1 * y1)
    )
    beta = rz1 / rz0
    lead = 1.0 + beta
    coarse = y1 + beta * y0
    c22 = exact(g22, y1) + beta * y22
    pq1 = (
        lead * (lead * g11 + 2.0 * total(coarse * g12) - 2.0 * alpha * cross)
        + total(coarse * (c22 - 2.0 * alpha * (g14 + y24)))
        + alpha * alpha * (g33 + total(y0 * (2.0 * g34 + y44)))
    )
    alpha1 = rz1 / pq1
    lower = alpha1 * alpha
    upper = alpha + alpha1 * lead
    first = alpha * y0 + alpha1 * coarse
    second = -lower * y0
    begin = frame_start()
    first16 = window(first, begin, FRAME)
    weights = jnp.concatenate([first16, window(second, begin, FRAME)], axis=0)
    weights2 = jnp.concatenate([first16, window(second, begin - STEP, WIDE)], axis=0)
    row = lax.broadcasted_iota(jnp.int32, (8, 256), 0)
    half = lax.broadcasted_iota(jnp.int32, (8, 256), 1) // 128
    pair = jnp.concatenate([upper, lower, jnp.zeros((6, cases), F32)], axis=0)
    columns = exact(pair, jnp.where(row == half, 1.0, 0.0), TN)
    upper = jnp.concatenate([columns[:, :128]] * (OWN // 128), axis=1)
    lower = jnp.concatenate([columns[:, 128:]] * (OWN // 128), axis=1)
    start = jnp.concatenate([a_ref[:live, :], b_ref[:live, :]], axis=1)
    scaled = scaled_ref[...]
    image = image_ref[...]
    own = own_ref[...]
    got_a = got_a_ref[...]
    got_b = inside() * got_b_ref[...]
    image2 = own[:cases] + jnp.concatenate([got_a[:cases], got_b[:cases]], axis=1)
    coarse2 = widened(own[cases:], got_a[cases:], got_b[cases:], odd == 0)
    field = (
        upper * start[:cases]
        - lower * scaled[:cases]
        + exact(weights, jnp.concatenate([start[cases:], scaled[cases:]], axis=0), TN)
    )
    resid2 = (
        resid_ref[...]
        - upper * image[:cases]
        + lower * image2
        - exact(weights2, jnp.concatenate([image[cases:], coarse2], axis=0), TN)
    )
    copies = []
    for k, (value, out, buf) in enumerate(
        ((field, field_hbm, field_ref), (resid2, resid2_hbm, resid2_ref))
    ):
        for j in range(NB):
            blk_ref[k, place_of(rows_ref, odd, j)] = value[:, B * j : B * (j + 1)]
        for m in range(0, NB, 2):
            buf[:, B * m : B * (m + 2)] = jnp.concatenate([blk_ref[k, m], blk_ref[k, m + 1]], axis=1)
        copies.append(pltpu.make_async_copy(buf, out, sems.at[k]))
        copies[-1].start()
    for copy in copies:
        copy.wait()


def lanes_for(width):
    return -(-width // 128) * 128


def swap(x, steps, count):
    return [lax.ppermute(x, "sub", [(i, i ^ k) for i in range(count)]) for k in steps]


def rounds_of(count):
    rounds = []
    base = 1
    while base < count:
        turn = 1 if base > 1 else 0
        if base * 4 <= count:
            rounds.append((base, 2 * base + turn, 3 * base + turn))
            base *= 4
        else:
            rounds.append((base,))
            base *= 2
    return rounds


def across(a, b, count, parts):
    low = lax.ppermute(a, "sub", [(i, i ^ 1) for i in range(count)])
    inner = [(i, i + 1) for i in range(1, count - 1, 2)]
    pairs = [(i * parts + x, j * parts + x) for i, j in inner for x in range(parts)]
    ends = [(i * parts + x, i * parts + x + 1) for i in (0, count - 1) for x in range(0, parts - 1, 2)]
    pairs += ends
    return low, lax.ppermute(b, ("sub", "rhs"), pairs + [(j, i) for i, j in pairs])


def inside():
    place = lax.axis_index("sub")
    return jnp.where((place == 0) | (place == lax.axis_size("sub") - 1), 0.0, 1.0)


def body(
    right_side,
    stiffness_blocks,
    block_columns,
    interface_rows,
    corner_owner,
    corner_basis,
    jacobi_scale,
    coarse_inverse,
):
    cases = right_side.shape[0]
    ncoarse = coarse_inverse.shape[0]
    count = lax.axis_size("sub")
    parts = lax.axis_size("rhs")
    live = cases + FRAME
    rounds = rounds_of(count)
    run = functools.partial(call, large=ncoarse > 128)

    bases = [corner_basis] + [
        lax.ppermute(corner_basis, "rhs", [((i + k) % parts, i) for i in range(parts)])
        for k in range(1, parts)
    ]
    packed = jax.ShapeDtypeStruct((NB * KPAD, B * B), BF16)
    wh, wl = call(
        load_blocks,
        [packed, packed],
        1,
        raw=(0,),
        scratch=[
            pltpu.VMEM((B * B // CHUNK, KNZ, NB, CHUNK), F32),
            pltpu.SemaphoreType.DMA((B * B // CHUNK,)),
        ],
        bytes_moved=16 * 1024 * 1024,
        large=True,
    )(jnp.transpose(stiffness_blocks, (1, 0, 2)))
    resid, side_a, side_b = run(
        functools.partial(sides, parts=parts),
        [shape(cases, OWN), shape(live + 8, EDGE), shape(live + 8, EDGE)],
        5 + parts,
        smem=(0, 1),
        scratch=[pltpu.VMEM((NB, live + 8 + cases, B), F32)],
    )(interface_rows, corner_owner, right_side, jacobi_scale.reshape(1, OWN), wh, *bases)
    dense = jax.ShapeDtypeStruct((ROWS, EXT), BF16)
    high, low = run(assemble, [dense, dense], 5, smem=(0,))(
        interface_rows, block_columns, wh, wl, side_a
    )
    ghost_a, ghost_b = across(side_a, side_b, count, parts)
    ends = (side_a, side_b, ghost_a, ghost_b)

    lanes = lanes_for(3 * (cases + ncoarse) + 2 * cases)
    wide = pltpu.VMEM((FRAME, lanes_for(ncoarse)), F32)
    strain, own_a, own_b = run(
        first_apply, [shape(live, ROWS), shape(2 * live, EDGE), shape(2 * live, EDGE)], 6
    )(*ends, high, low)
    got_a, got_b = across(own_a, own_b, count, parts)
    frame, scalars = run(
        functools.partial(first_sums, ncoarse=ncoarse),
        [shape(FRAME, lanes), shape(8, cases)],
        4,
        scratch=[wide],
    )(resid, side_a, side_b, strain)
    strain, image, scaled, pay = run(
        functools.partial(second_apply, ncoarse=ncoarse),
        [shape(live, ROWS), shape(live, OWN), shape(live, OWN), shape(ncoarse, lanes)],
        12,
        scratch=[wide, pltpu.VMEM((ncoarse, lanes), F32)],
    )(*ends, own_a, own_b, got_a, got_b, high, low, frame, scalars)
    for steps in rounds[:-1]:
        pay = sum(swap(pay, steps, count), pay)
    pays = [pay] + swap(pay, rounds[-1], count)
    own, back_a, back_b = run(
        second_image, [shape(live, OWN), shape(live, EDGE), shape(live, EDGE)], 4
    )(scaled, strain, high, low)
    got_a, got_b = across(back_a, back_b, count, parts)
    return tuple(
        run(
            functools.partial(finish, ncoarse=ncoarse, n_pay=len(pays)),
            [shape(cases, OWN)] * 2,
            10 + len(pays),
            smem=(0,),
            raw_out=True,
            scratch=[
                pltpu.VMEM((cases, OWN), F32),
                pltpu.VMEM((cases, OWN), F32),
                pltpu.VMEM((2, NB, cases, B), F32),
                pltpu.SemaphoreType.DMA((2,)),
            ],
        )(
            interface_rows,
            coarse_inverse,
            resid,
            side_a,
            side_b,
            image,
            scaled,
            own,
            got_a,
            got_b,
            *pays,
        )
    )


def solution(mesh):
    placed = (
        P("rhs", "sub"),
        P("sub", None, None),
        P("sub", None),
        P("sub", None, None),
        P("sub", None),
        P("rhs", "sub"),
        P("sub"),
        P(),
    )
    return jax.shard_map(
        body,
        mesh=mesh,
        in_specs=placed,
        out_specs=(P("rhs", "sub"), P("rhs", "sub")),
        check_vma=False,
    )
```

```python
import functools

import jax
import jax.numpy as jnp
from jax import lax
from jax.experimental import pallas as pl
from jax.experimental.pallas import tpu as pltpu
from jax.sharding import PartitionSpec as P

B = 64
KNZ = 27
IFB = 4
NCL = 8
NB = 2 * IFB
NE = NB + 2 * IFB
EDGE = IFB * B
OWN = NB * B
EXT = NE * B
ROWS = NB * B
KPAD = 32
F32 = jnp.float32
BF16 = jnp.bfloat16
HIGHEST = lax.Precision.HIGHEST
NT = (((1,), (1,)), ((), ()))
NN = (((1,), (0,)), ((), ()))
VMEM_SMALL = 16 * 1024 * 1024
VMEM_LARGE = 48 * 1024 * 1024
CHUNK = 512
STEP = 2
FRAME = 16
WIDE = 24
TN = (((0,), (0,)), ((), ()))


def split(x):
    high = x.astype(BF16)
    return high, (x - high.astype(F32)).astype(BF16)


def times(x, high, low, dims):
    count = x.shape[0]
    xh, xl = split(x)
    both = lax.dot_general(
        jnp.concatenate([xh, xl], axis=0), high, dims, preferred_element_type=F32
    )
    return both[:count] + both[count:] + lax.dot_general(xh, low, dims, preferred_element_type=F32)


def exact(x, y, dims=NN):
    return lax.dot_general(x, y, dims, precision=HIGHEST, preferred_element_type=F32)


def near(x, y, dims=NN):
    xh, xl = split(x)
    yh, yl = split(y)
    (left,), (right,) = dims[0]
    return lax.dot_general(
        jnp.concatenate([xh, xh, xl], axis=left),
        jnp.concatenate([yh, yl, yh], axis=right),
        dims,
        preferred_element_type=F32,
    )


def call(kernel, outs, n_in, smem=(), raw=(), raw_out=False, scratch=(), bytes_moved=None, large=False):
    def spec(i):
        if i in raw:
            return pl.BlockSpec(memory_space=pltpu.HBM)
        return pl.BlockSpec(memory_space=pltpu.SMEM if i in smem else pltpu.VMEM)

    return pl.pallas_call(
        kernel,
        out_shape=outs,
        in_specs=[spec(i) for i in range(n_in)],
        out_specs=[
            pl.BlockSpec(memory_space=pltpu.HBM if raw_out else pltpu.VMEM) for _ in outs
        ],
        scratch_shapes=list(scratch),
        cost_estimate=bytes_moved
        and pl.CostEstimate(flops=0, transcendentals=0, bytes_accessed=bytes_moved),
        compiler_params=pltpu.CompilerParams(vmem_limit_bytes=VMEM_LARGE if large else VMEM_SMALL),
    )


def shape(*dims):
    return jax.ShapeDtypeStruct(dims, F32)


def place_of(rows_ref, odd, j):
    side = jnp.where(odd == 1, j // IFB, 1 - j // IFB)
    return rows_ref[0, side, j % IFB]


def load_blocks(blocks_hbm, high_ref, low_ref, chunk_ref, sems):
    chunks = [
        pltpu.make_async_copy(
            blocks_hbm.at[:, :, pl.ds(CHUNK * t, CHUNK)], chunk_ref.at[t], sems.at[t]
        )
        for t in range(B * B // CHUNK)
    ]
    for copy in chunks:
        copy.start()
    filler = jnp.zeros((NB * KPAD - NB * (KNZ + 1), B * B), BF16)
    high_ref[NB * (KNZ + 1) :, :] = filler
    low_ref[NB * (KNZ + 1) :, :] = filler
    for t, copy in enumerate(chunks):
        copy.wait()
        padded = jnp.concatenate([chunk_ref[t], jnp.zeros((1, NB, CHUNK), F32)], axis=0)
        wh, wl = split(padded.reshape(NB * (KNZ + 1), CHUNK))
        cut = slice(CHUNK * t, CHUNK * (t + 1))
        high_ref[: NB * (KNZ + 1), cut] = wh
        low_ref[: NB * (KNZ + 1), cut] = wl


def assemble(rows_ref, columns_ref, wh_ref, wl_ref, after_ref, high_ref, low_ref):
    odd = lax.axis_index("sub") % 2
    column = columns_ref[...]
    place = jnp.where(
        (column < NB + IFB) == (odd == 1), column % IFB + NB, column % IFB + NB + IFB
    )
    for j in range(NB):
        place = jnp.where(column == place_of(rows_ref, odd, j), j, place)
    slot = lax.broadcasted_iota(jnp.int32, (KNZ, NB * KPAD), 0)
    entry = lax.broadcasted_iota(jnp.int32, (KNZ, NB * KPAD), 1)
    widen = jnp.where(entry // NB == slot, 1.0, 0.0).astype(BF16)
    wide = lax.dot_general(place.astype(F32).astype(BF16), widen, NN, preferred_element_type=F32)
    r = lax.broadcasted_iota(jnp.int32, (NE * NB, NB * KPAD), 0)
    q = lax.broadcasted_iota(jnp.int32, (NE * NB, NB * KPAD), 1)
    hit = (jnp.concatenate([wide] * NE, axis=0) == (r // NB).astype(F32)) & (r % NB == q % NB)
    onehot = jnp.where(hit, 1.0, 0.0).astype(BF16)
    first = lax.broadcasted_iota(jnp.int32, (NB, 128), 1) < B
    for t in range(B * B // CHUNK):
        cut = slice(CHUNK * t, CHUNK * (t + 1))
        dense = lax.dot_general(
            onehot, wh_ref[:, cut], NN, preferred_element_type=F32
        ) + lax.dot_general(onehot, wl_ref[:, cut], NN, preferred_element_type=F32)
        for m in range(NE // 2):
            for h in range(CHUNK // 128):
                lane = slice(128 * h, 128 * (h + 1))
                left = dense[16 * m : 16 * m + 8, lane]
                right = dense[16 * m + 8 : 16 * m + 16, lane]
                tile = jnp.concatenate(
                    [
                        jnp.where(first, left, pltpu.roll(right, B, 1)),
                        jnp.where(first, pltpu.roll(left, B, 1), right),
                    ],
                    axis=0,
                )
                th, tl = split(tile)
                at = NB * CHUNK // B * t + 16 * h
                high_ref[at : at + 16, 128 * m : 128 * (m + 1)] = th
                low_ref[at : at + 16, 128 * m : 128 * (m + 1)] = tl


def sides(rows_ref, owner_ref, right_ref, scale_ref, after_ref, *rest, parts):
    basis_refs = rest[:parts]
    resid_ref, side_a_ref, side_b_ref, blk_ref = rest[parts:]
    odd = lax.axis_index("sub") % 2
    mine = lax.axis_index("rhs")
    cases = right_ref.shape[0]
    per = NCL // parts
    scale = jnp.broadcast_to(scale_ref[...], (8, OWN))
    unknown = lax.broadcasted_iota(jnp.int32, (FRAME, OWN), 0) + frame_start()
    coarse = jnp.zeros((FRAME, OWN), F32)
    for k in range(parts):
        for t in range(per):
            owner = owner_ref[0, ((mine + k) % parts) * per + t]
            coarse = coarse + jnp.where(unknown == owner, basis_refs[k][t : t + 1, :], 0.0)
    right = right_ref[...]
    fine = right * scale[0:1]
    live = cases + FRAME
    for n in range(NB):
        cut = slice(B * n, B * (n + 1))
        blk_ref[n, 0:cases, :] = fine[:, cut]
        blk_ref[n, cases:live, :] = coarse[:, cut]
        blk_ref[n, live : live + 8, :] = scale[:, cut]
        blk_ref[n, live + 8 :, :] = right[:, cut]
    for j in range(0, NB, 2):
        pair = jnp.concatenate(
            [blk_ref[place_of(rows_ref, odd, j)], blk_ref[place_of(rows_ref, odd, j + 1)]], axis=1
        )
        target = side_a_ref if j < IFB else side_b_ref
        at = B * (j % IFB)
        target[:, at : at + 2 * B] = pair[: live + 8]
        resid_ref[:, B * j : B * (j + 2)] = pair[live + 8 :]


def frame_start():
    return STEP * lax.axis_index("sub") - 6


def turned(rows, upper):
    up = pltpu.roll(rows, STEP, 0)
    down = pltpu.roll(rows, rows.shape[0] - STEP, 0)
    return jnp.where(upper, up, down)


def arrived(rows, upper):
    cases = rows.shape[0] - FRAME
    return jnp.concatenate([rows[:cases], turned(rows[cases:], upper)], axis=0)


def first_apply(a_ref, b_ref, ga_ref, gb_ref, high_ref, low_ref, strain_ref, send_a_ref, send_b_ref):
    live = strain_ref.shape[0]
    odd = lax.axis_index("sub") % 2 == 1
    field = jnp.concatenate(
        [
            a_ref[:live, :],
            b_ref[:live, :],
            arrived(ga_ref[:live, :], jnp.logical_not(odd)),
            arrived(inside() * gb_ref[:live, :], odd),
        ],
        axis=1,
    )
    strain = times(field, high_ref[...], low_ref[...], NT)
    strain_ref[...] = strain
    back = times(strain, high_ref[...], low_ref[...], NN)
    send_a_ref[:live, :] = field[:, :EDGE] + back[:, :EDGE]
    send_a_ref[live:, :] = back[:, OWN : OWN + EDGE]
    send_b_ref[:live, :] = field[:, EDGE:OWN] + back[:, EDGE:OWN]
    send_b_ref[live:, :] = back[:, OWN + EDGE :]


def to_lanes(block, wide_ref):
    width = wide_ref.shape[1]
    wide_ref[...] = jnp.zeros_like(wide_ref)
    wide_ref[:, :FRAME] = block
    return pltpu.roll(wide_ref[...], (frame_start() + width) % width, 1)


def row_sums(value):
    return exact(jnp.ones((8, value.shape[1]), F32), value, NT)[0:1]


def first_sums(resid_ref, a_ref, b_ref, strain_ref, frame_ref, scalar_ref, wide_ref, *, ncoarse):
    live = strain_ref.shape[0]
    cases = live - FRAME
    own = jnp.concatenate([a_ref[:live, :], b_ref[:live, :]], axis=1)
    paired = jnp.concatenate([own, strain_ref[...]], axis=1)
    gram = exact(paired[cases:], paired, NT)
    resid = resid_ref[...]
    lead = paired[:cases]
    second = places(cases, ncoarse)[0]
    frame_ref[...] = jnp.zeros_like(frame_ref)
    frame_ref[:, 0:cases] = exact(own[cases:], resid, NT)
    frame_ref[:, cases : cases + ncoarse] = to_lanes(gram[:, cases:], wide_ref)[:, :ncoarse]
    frame_ref[:, second : second + cases] = gram[:, :cases]
    scalar_ref[...] = jnp.zeros_like(scalar_ref)
    scalar_ref[0:1, :] = row_sums(resid * own[:cases])
    scalar_ref[1:2, :] = row_sums(lead * lead)


def second_apply(
    a_ref,
    b_ref,
    ga_ref,
    gb_ref,
    own_a_ref,
    own_b_ref,
    got_a_ref,
    got_b_ref,
    high_ref,
    low_ref,
    frame_ref,
    scalar_ref,
    strain_ref,
    image_ref,
    scaled_ref,
    pay_ref,
    wide_ref,
    tall_ref,
    *,
    ncoarse,
):
    live = strain_ref.shape[0]
    cases = live - FRAME
    odd = lax.axis_index("sub") % 2 == 1
    even = jnp.logical_not(odd)
    inner = inside()
    image = jnp.concatenate(
        [
            own_a_ref[:live, :] + arrived(got_a_ref[live:, :], even),
            own_b_ref[:live, :] + inner * arrived(got_b_ref[live:, :], odd),
            own_a_ref[live:, :] + arrived(got_a_ref[:live, :], even),
            own_b_ref[live:, :] + arrived(got_b_ref[:live, :], odd),
        ],
        axis=1,
    )
    end = slice(live, live + 1)
    scale = jnp.concatenate(
        [a_ref[end, :], b_ref[end, :], ga_ref[end, :], inner * gb_ref[end, :]], axis=1
    )
    field = scale * image
    strain = times(field, high_ref[...], low_ref[...], NT)
    own = field[:, :OWN]
    first = image[:, :OWN]
    strain_ref[...] = strain
    image_ref[...] = first
    scaled_ref[...] = own
    paired = jnp.concatenate([own, strain], axis=1)
    gram = exact(paired[cases:], paired, NT)
    cross = exact(first[cases:], own, NT)
    lead = paired[:cases]
    width = cases + ncoarse
    tall_ref[...] = jnp.zeros_like(tall_ref)
    tall_ref[:FRAME, :] = frame_ref[...]
    second = places(cases, ncoarse)[0]
    for block, at, far in (
        (cross, width, width + cases),
        (gram, second + width, second + cases),
    ):
        tall_ref[:FRAME, at : at + cases] = block[:, :cases]
        tall_ref[:FRAME, far : far + ncoarse] = to_lanes(block[:, cases:], wide_ref)[:, :ncoarse]
    pay_ref[...] = pltpu.roll(tall_ref[...], (frame_start() + ncoarse) % ncoarse, 0)
    at = second + width + cases
    pay_ref[0:8, at : at + cases] = scalar_ref[...]
    pay_ref[2:3, at : at + cases] = row_sums(own[:cases] * first[:cases])
    pay_ref[3:4, at : at + cases] = row_sums(lead * lead)


def second_image(scaled_ref, strain_ref, high_ref, low_ref, own_ref, send_a_ref, send_b_ref):
    back = times(strain_ref[...], high_ref[...], low_ref[...], NN)
    own_ref[...] = scaled_ref[...] + back[:, :OWN]
    send_a_ref[...] = back[:, OWN : OWN + EDGE]
    send_b_ref[...] = back[:, OWN + EDGE :]


def window(value, start, count):
    rows = value.shape[0] + 32
    longer = jnp.concatenate([value, jnp.zeros((32, value.shape[1]), F32)], axis=0)
    return pltpu.roll(longer, (rows - start) % rows, 0)[:count]


def widened(own, got_a, got_b, even):
    gap = WIDE - FRAME

    def placed(rows, upper):
        none = jnp.zeros((gap, rows.shape[1]), F32)
        low = jnp.concatenate([rows, none], axis=0)
        return jnp.where(upper, pltpu.roll(low, 2 * STEP, 0), low)

    none = jnp.zeros((gap, own.shape[1]), F32)
    middle = pltpu.roll(jnp.concatenate([own, none], axis=0), STEP, 0)
    return middle + jnp.concatenate(
        [placed(got_a, even), placed(got_b, jnp.logical_not(even))], axis=1
    )


def finish(
    rows_ref,
    inverse_ref,
    resid_ref,
    a_ref,
    b_ref,
    image_ref,
    scaled_ref,
    own_ref,
    got_a_ref,
    got_b_ref,
    *rest,
    ncoarse,
    n_pay,
):
    pays = rest[:n_pay]
    field_hbm, resid2_hbm, field_ref, resid2_ref, blk_ref, sems = rest[n_pay:]
    odd = lax.axis_index("sub") % 2
    live = own_ref.shape[0]
    cases = live - FRAME
    width = cases + ncoarse
    pay = pays[0][...]
    for other in pays[1:]:
        pay = pay + other[...]

    def total(value):
        return jnp.sum(value, axis=0, keepdims=True)

    lead, full = places(cases, ncoarse)
    one, two = pay[:, :lead], pay[:, lead:]
    tile = slice(0, 128)
    u0, g12 = one[:, tile], two[:, tile]
    g14 = pltpu.roll(one, lead - width, 1)[:, tile]
    g34 = pltpu.roll(two, full - lead - width, 1)[:, tile]
    scalars = pltpu.roll(two[0:8], full - lead - width - cases, 1)[:, tile]
    r0d, g11, g13, g33 = (scalars[k : k + 1] for k in range(4))
    inverse = inverse_ref[...]
    y0 = near(inverse, u0)

    def picked(left, at, y):
        def none(rows):
            return [jnp.zeros((rows, 128), F32)] if rows else []

        rest = left.shape[1] - at - ncoarse
        return near(left, jnp.concatenate(none(at) + [y] + none(rest), axis=0))

    y22 = picked(one, cases, y0)
    y24 = picked(one, width + cases, y0)
    y44 = picked(two, cases, y0)
    rz0 = r0d + total(u0 * y0)
    pq0 = g11 + total(y0 * (2.0 * g12 + y22))
    alpha = rz0 / pq0
    u1 = u0 - alpha * (g12 + y22)
    y1 = near(inverse, u1)
    cross = g13 + total(y0 * g14)
    rz1 = (
        r0d
        - 2.0 * alpha * (g11 + total(y0 * g12))
        + alpha * alpha * (cross + total(y0 * (g14 + y24)))
        + total(u1 * y1)
    )
    beta = rz1 / rz0
    ahead = 1.0 + beta
    coarse = y1 + beta * y0
    c22 = picked(one, cases, y1) + beta * y22
    pq1 = (
        ahead * (ahead * g11 + 2.0 * total(coarse * g12) - 2.0 * alpha * cross)
        + total(coarse * (c22 - 2.0 * alpha * (g14 + y24)))
        + alpha * alpha * (g33 + total(y0 * (2.0 * g34 + y44)))
    )
    alpha1 = rz1 / pq1
    lower = alpha1 * alpha
    upper = alpha + alpha1 * ahead
    first = alpha * y0 + alpha1 * coarse
    second = -lower * y0
    begin = frame_start()
    first16 = window(first, begin, FRAME)
    weights = jnp.concatenate([first16, window(second, begin, FRAME)], axis=0)[:, :cases]
    weights2 = jnp.concatenate([first16, window(second, begin - STEP, WIDE)], axis=0)[:, :cases]
    row = lax.broadcasted_iota(jnp.int32, (8, 256), 0)
    half = lax.broadcasted_iota(jnp.int32, (8, 256), 1) // 128
    pair = jnp.concatenate([upper, lower, jnp.zeros((6, 128), F32)], axis=0)[:, :cases]
    columns = exact(pair, jnp.where(row == half, 1.0, 0.0), TN)
    upper = jnp.concatenate([columns[:, :128]] * (OWN // 128), axis=1)
    lower = jnp.concatenate([columns[:, 128:]] * (OWN // 128), axis=1)
    start = jnp.concatenate([a_ref[:live, :], b_ref[:live, :]], axis=1)
    scaled = scaled_ref[...]
    image = image_ref[...]
    own = own_ref[...]
    got_a = got_a_ref[...]
    got_b = inside() * got_b_ref[...]
    image2 = own[:cases] + jnp.concatenate([got_a[:cases], got_b[:cases]], axis=1)
    coarse2 = widened(own[cases:], got_a[cases:], got_b[cases:], odd == 0)
    field = (
        upper * start[:cases]
        - lower * scaled[:cases]
        + near(weights, jnp.concatenate([start[cases:], scaled[cases:]], axis=0), TN)
    )
    resid2 = (
        resid_ref[...]
        - upper * image[:cases]
        + lower * image2
        - near(weights2, jnp.concatenate([image[cases:], coarse2], axis=0), TN)
    )
    copies = []
    for k, (value, out, buf) in enumerate(
        ((field, field_hbm, field_ref), (resid2, resid2_hbm, resid2_ref))
    ):
        for j in range(NB):
            blk_ref[k, place_of(rows_ref, odd, j)] = value[:, B * j : B * (j + 1)]
        for m in range(0, NB, 2):
            buf[:, B * m : B * (m + 2)] = jnp.concatenate([blk_ref[k, m], blk_ref[k, m + 1]], axis=1)
        copies.append(pltpu.make_async_copy(buf, out, sems.at[k]))
        copies[-1].start()
    for copy in copies:
        copy.wait()


def places(cases, ncoarse):
    both = cases + ncoarse
    lead = lanes_for(2 * both)
    return lead, lead + lanes_for(2 * cases + both)


def lanes_for(width):
    return -(-width // 128) * 128


def swap(x, steps, count):
    return [lax.ppermute(x, "sub", [(i, i ^ k) for i in range(count)]) for k in steps]


def rounds_of(count):
    rounds = []
    base = 1
    while base < count:
        turn = 1 if base > 1 else 0
        if base * 4 <= count:
            rounds.append((base, 2 * base + turn, 3 * base + turn))
            base *= 4
        else:
            rounds.append((base,))
            base *= 2
    return rounds


def across(a, b, count, parts):
    low = lax.ppermute(a, "sub", [(i, i ^ 1) for i in range(count)])
    inner = [(i, i + 1) for i in range(1, count - 1, 2)]
    pairs = [(i * parts + x, j * parts + x) for i, j in inner for x in range(parts)]
    ends = [(i * parts + x, i * parts + x + 1) for i in (0, count - 1) for x in range(0, parts - 1, 2)]
    pairs += ends
    return low, lax.ppermute(b, ("sub", "rhs"), pairs + [(j, i) for i, j in pairs])


def inside():
    place = lax.axis_index("sub")
    return jnp.where((place == 0) | (place == lax.axis_size("sub") - 1), 0.0, 1.0)


def body(
    right_side,
    stiffness_blocks,
    block_columns,
    interface_rows,
    corner_owner,
    corner_basis,
    jacobi_scale,
    coarse_inverse,
):
    cases = right_side.shape[0]
    ncoarse = coarse_inverse.shape[0]
    count = lax.axis_size("sub")
    parts = lax.axis_size("rhs")
    live = cases + FRAME
    rounds = rounds_of(count)
    run = functools.partial(call, large=ncoarse > 128)

    bases = [corner_basis] + [
        lax.ppermute(corner_basis, "rhs", [((i + k) % parts, i) for i in range(parts)])
        for k in range(1, parts)
    ]
    packed = jax.ShapeDtypeStruct((NB * KPAD, B * B), BF16)
    wh, wl = call(
        load_blocks,
        [packed, packed],
        1,
        raw=(0,),
        scratch=[
            pltpu.VMEM((B * B // CHUNK, KNZ, NB, CHUNK), F32),
            pltpu.SemaphoreType.DMA((B * B // CHUNK,)),
        ],
        bytes_moved=16 * 1024 * 1024,
        large=True,
    )(jnp.transpose(stiffness_blocks, (1, 0, 2)))
    resid, side_a, side_b = run(
        functools.partial(sides, parts=parts),
        [shape(cases, OWN), shape(live + 8, EDGE), shape(live + 8, EDGE)],
        5 + parts,
        smem=(0, 1),
        scratch=[pltpu.VMEM((NB, live + 8 + cases, B), F32)],
    )(interface_rows, corner_owner, right_side, jacobi_scale.reshape(1, OWN), wh, *bases)
    dense = jax.ShapeDtypeStruct((ROWS, EXT), BF16)
    high, low = run(assemble, [dense, dense], 5, smem=(0,))(
        interface_rows, block_columns, wh, wl, side_a
    )
    ghost_a, ghost_b = across(side_a, side_b, count, parts)
    ends = (side_a, side_b, ghost_a, ghost_b)

    lanes = places(cases, ncoarse)[1]
    wide = pltpu.VMEM((FRAME, lanes_for(ncoarse)), F32)
    strain, own_a, own_b = run(
        first_apply, [shape(live, ROWS), shape(2 * live, EDGE), shape(2 * live, EDGE)], 6
    )(*ends, high, low)
    got_a, got_b = across(own_a, own_b, count, parts)
    frame, scalars = run(
        functools.partial(first_sums, ncoarse=ncoarse),
        [shape(FRAME, lanes), shape(8, cases)],
        4,
        scratch=[wide],
    )(resid, side_a, side_b, strain)
    strain, image, scaled, pay = run(
        functools.partial(second_apply, ncoarse=ncoarse),
        [shape(live, ROWS), shape(live, OWN), shape(live, OWN), shape(ncoarse, lanes)],
        12,
        scratch=[wide, pltpu.VMEM((ncoarse, lanes), F32)],
    )(*ends, own_a, own_b, got_a, got_b, high, low, frame, scalars)
    for steps in rounds[:-1]:
        pay = sum(swap(pay, steps, count), pay)
    pays = [pay] + swap(pay, rounds[-1], count)
    own, back_a, back_b = run(
        second_image, [shape(live, OWN), shape(live, EDGE), shape(live, EDGE)], 4
    )(scaled, strain, high, low)
    got_a, got_b = across(back_a, back_b, count, parts)
    return tuple(
        run(
            functools.partial(finish, ncoarse=ncoarse, n_pay=len(pays)),
            [shape(cases, OWN)] * 2,
            10 + len(pays),
            smem=(0,),
            raw_out=True,
            scratch=[
                pltpu.VMEM((cases, OWN), F32),
                pltpu.VMEM((cases, OWN), F32),
                pltpu.VMEM((2, NB, cases, B), F32),
                pltpu.SemaphoreType.DMA((2,)),
            ],
        )(
            interface_rows,
            coarse_inverse,
            resid,
            side_a,
            side_b,
            image,
            scaled,
            own,
            got_a,
            got_b,
            *pays,
        )
    )


def solution(mesh):
    placed = (
        P("rhs", "sub"),
        P("sub", None, None),
        P("sub", None),
        P("sub", None, None),
        P("sub", None),
        P("rhs", "sub"),
        P("sub"),
        P(),
    )
    return jax.shard_map(
        body,
        mesh=mesh,
        in_specs=placed,
        out_specs=(P("rhs", "sub"), P("rhs", "sub")),
        check_vma=False,
    )
```

```python
import functools

import jax
import jax.numpy as jnp
from jax import lax
from jax.experimental import pallas as pl
from jax.experimental.pallas import tpu as pltpu
from jax.sharding import PartitionSpec as P

B = 64
KNZ = 27
IFB = 4
NCL = 8
NB = 2 * IFB
NE = NB + 2 * IFB
EDGE = IFB * B
OWN = NB * B
EXT = NE * B
ROWS = NB * B
KPAD = 32
F32 = jnp.float32
BF16 = jnp.bfloat16
HIGHEST = lax.Precision.HIGHEST
NT = (((1,), (1,)), ((), ()))
NN = (((1,), (0,)), ((), ()))
VMEM_SMALL = 16 * 1024 * 1024
VMEM_LARGE = 48 * 1024 * 1024
CHUNK = 512
STEP = 2
FRAME = 16
WIDE = 24
TN = (((0,), (0,)), ((), ()))


def split(x):
    high = x.astype(BF16)
    return high, (x - high.astype(F32)).astype(BF16)


def times(x, high, low, dims):
    count = x.shape[0]
    xh, xl = split(x)
    both = lax.dot_general(
        jnp.concatenate([xh, xl], axis=0), high, dims, preferred_element_type=F32
    )
    return both[:count] + both[count:] + lax.dot_general(xh, low, dims, preferred_element_type=F32)


def exact(x, y, dims=NN):
    return lax.dot_general(x, y, dims, precision=HIGHEST, preferred_element_type=F32)


def near(x, y, dims=NN):
    xh, xl = split(x)
    yh, yl = split(y)
    (left,), (right,) = dims[0]
    return lax.dot_general(
        jnp.concatenate([xh, xh, xl], axis=left),
        jnp.concatenate([yh, yl, yh], axis=right),
        dims,
        preferred_element_type=F32,
    )


def call(kernel, outs, n_in, smem=(), raw=(), raw_out=False, scratch=(), bytes_moved=None, large=False):
    def spec(i):
        if i in raw:
            return pl.BlockSpec(memory_space=pltpu.HBM)
        return pl.BlockSpec(memory_space=pltpu.SMEM if i in smem else pltpu.VMEM)

    return pl.pallas_call(
        kernel,
        out_shape=outs,
        in_specs=[spec(i) for i in range(n_in)],
        out_specs=[
            pl.BlockSpec(memory_space=pltpu.HBM if raw_out else pltpu.VMEM) for _ in outs
        ],
        scratch_shapes=list(scratch),
        cost_estimate=bytes_moved
        and pl.CostEstimate(flops=0, transcendentals=0, bytes_accessed=bytes_moved),
        compiler_params=pltpu.CompilerParams(vmem_limit_bytes=VMEM_LARGE if large else VMEM_SMALL),
    )


def shape(*dims):
    return jax.ShapeDtypeStruct(dims, F32)


def place_of(rows_ref, odd, j):
    side = jnp.where(odd == 1, j // IFB, 1 - j // IFB)
    return rows_ref[0, side, j % IFB]


def load_blocks(blocks_hbm, high_ref, low_ref, chunk_ref, sems):
    chunks = [
        pltpu.make_async_copy(
            blocks_hbm.at[:, :, pl.ds(CHUNK * t, CHUNK)], chunk_ref.at[t], sems.at[t]
        )
        for t in range(B * B // CHUNK)
    ]
    for copy in chunks:
        copy.start()
    filler = jnp.zeros((NB * KPAD - NB * (KNZ + 1), B * B), BF16)
    high_ref[NB * (KNZ + 1) :, :] = filler
    low_ref[NB * (KNZ + 1) :, :] = filler
    for t, copy in enumerate(chunks):
        copy.wait()
        padded = jnp.concatenate([chunk_ref[t], jnp.zeros((1, NB, CHUNK), F32)], axis=0)
        wh, wl = split(padded.reshape(NB * (KNZ + 1), CHUNK))
        cut = slice(CHUNK * t, CHUNK * (t + 1))
        high_ref[: NB * (KNZ + 1), cut] = wh
        low_ref[: NB * (KNZ + 1), cut] = wl


def assemble(rows_ref, columns_ref, wh_ref, wl_ref, after_ref, high_ref, low_ref):
    odd = lax.axis_index("sub") % 2
    column = columns_ref[...]
    place = jnp.where(
        (column < NB + IFB) == (odd == 1), column % IFB + NB, column % IFB + NB + IFB
    )
    for j in range(NB):
        place = jnp.where(column == place_of(rows_ref, odd, j), j, place)
    slot = lax.broadcasted_iota(jnp.int32, (KNZ, NB * KPAD), 0)
    entry = lax.broadcasted_iota(jnp.int32, (KNZ, NB * KPAD), 1)
    widen = jnp.where(entry // NB == slot, 1.0, 0.0).astype(BF16)
    wide = lax.dot_general(place.astype(F32).astype(BF16), widen, NN, preferred_element_type=F32)
    r = lax.broadcasted_iota(jnp.int32, (NE * NB, NB * KPAD), 0)
    q = lax.broadcasted_iota(jnp.int32, (NE * NB, NB * KPAD), 1)
    hit = (jnp.concatenate([wide] * NE, axis=0) == (r // NB).astype(F32)) & (r % NB == q % NB)
    onehot = jnp.where(hit, 1.0, 0.0).astype(BF16)
    first = lax.broadcasted_iota(jnp.int32, (NB, 128), 1) < B
    for t in range(B * B // CHUNK):
        cut = slice(CHUNK * t, CHUNK * (t + 1))
        dense = lax.dot_general(
            onehot, wh_ref[:, cut], NN, preferred_element_type=F32
        ) + lax.dot_general(onehot, wl_ref[:, cut], NN, preferred_element_type=F32)
        for m in range(NE // 2):
            for h in range(CHUNK // 128):
                lane = slice(128 * h, 128 * (h + 1))
                left = dense[16 * m : 16 * m + 8, lane]
                right = dense[16 * m + 8 : 16 * m + 16, lane]
                tile = jnp.concatenate(
                    [
                        jnp.where(first, left, pltpu.roll(right, B, 1)),
                        jnp.where(first, pltpu.roll(left, B, 1), right),
                    ],
                    axis=0,
                )
                th, tl = split(tile)
                at = NB * CHUNK // B * t + 16 * h
                high_ref[at : at + 16, 128 * m : 128 * (m + 1)] = th
                low_ref[at : at + 16, 128 * m : 128 * (m + 1)] = tl


def turn(high_ref, low_ref, high_t_ref, low_t_ref):
    high_t_ref[...] = high_ref[...].T
    low_t_ref[...] = low_ref[...].T


def sides(rows_ref, owner_ref, right_ref, scale_ref, after_ref, *rest, parts):
    basis_refs = rest[:parts]
    resid_ref, side_a_ref, side_b_ref, blk_ref = rest[parts:]
    odd = lax.axis_index("sub") % 2
    mine = lax.axis_index("rhs")
    cases = right_ref.shape[0]
    per = NCL // parts
    scale = jnp.broadcast_to(scale_ref[...], (8, OWN))
    unknown = lax.broadcasted_iota(jnp.int32, (FRAME, OWN), 0) + frame_start()
    coarse = jnp.zeros((FRAME, OWN), F32)
    for k in range(parts):
        for t in range(per):
            owner = owner_ref[0, ((mine + k) % parts) * per + t]
            coarse = coarse + jnp.where(unknown == owner, basis_refs[k][t : t + 1, :], 0.0)
    right = right_ref[...]
    fine = right * scale[0:1]
    live = cases + FRAME
    for n in range(NB):
        cut = slice(B * n, B * (n + 1))
        blk_ref[n, 0:cases, :] = fine[:, cut]
        blk_ref[n, cases:live, :] = coarse[:, cut]
        blk_ref[n, live : live + 8, :] = scale[:, cut]
        blk_ref[n, live + 8 :, :] = right[:, cut]
    for j in range(0, NB, 2):
        pair = jnp.concatenate(
            [blk_ref[place_of(rows_ref, odd, j)], blk_ref[place_of(rows_ref, odd, j + 1)]], axis=1
        )
        target = side_a_ref if j < IFB else side_b_ref
        at = B * (j % IFB)
        target[:, at : at + 2 * B] = pair[: live + 8]
        resid_ref[:, B * j : B * (j + 2)] = pair[live + 8 :]


def frame_start():
    return STEP * lax.axis_index("sub") - 6


def turned(rows, upper):
    up = pltpu.roll(rows, STEP, 0)
    down = pltpu.roll(rows, rows.shape[0] - STEP, 0)
    return jnp.where(upper, up, down)


def arrived(rows, upper):
    cases = rows.shape[0] - FRAME
    return jnp.concatenate([rows[:cases], turned(rows[cases:], upper)], axis=0)


def first_apply(
    a_ref, b_ref, ga_ref, gb_ref, high_ref, low_ref, high_t, low_t, strain_ref, send_a_ref, send_b_ref
):
    live = strain_ref.shape[0]
    odd = lax.axis_index("sub") % 2 == 1
    field = jnp.concatenate(
        [
            a_ref[:live, :],
            b_ref[:live, :],
            arrived(ga_ref[:live, :], jnp.logical_not(odd)),
            arrived(inside() * gb_ref[:live, :], odd),
        ],
        axis=1,
    )
    strain = times(field, high_t[...], low_t[...], NN)
    strain_ref[...] = strain
    back = times(strain, high_ref[...], low_ref[...], NN)
    send_a_ref[:live, :] = field[:, :EDGE] + back[:, :EDGE]
    send_a_ref[live:, :] = back[:, OWN : OWN + EDGE]
    send_b_ref[:live, :] = field[:, EDGE:OWN] + back[:, EDGE:OWN]
    send_b_ref[live:, :] = back[:, OWN + EDGE :]


def to_lanes(block, wide_ref):
    width = wide_ref.shape[1]
    wide_ref[...] = jnp.zeros_like(wide_ref)
    wide_ref[:, :FRAME] = block
    return pltpu.roll(wide_ref[...], (frame_start() + width) % width, 1)


def row_sums(value):
    return exact(jnp.ones((8, value.shape[1]), F32), value, NT)[0:1]


def first_sums(resid_ref, a_ref, b_ref, strain_ref, frame_ref, scalar_ref, wide_ref, *, ncoarse):
    live = strain_ref.shape[0]
    cases = live - FRAME
    own = jnp.concatenate([a_ref[:live, :], b_ref[:live, :]], axis=1)
    paired = jnp.concatenate([own, strain_ref[...]], axis=1)
    gram = exact(paired[cases:], paired, NT)
    resid = resid_ref[...]
    lead = paired[:cases]
    second = places(cases, ncoarse)[0]
    frame_ref[...] = jnp.zeros_like(frame_ref)
    frame_ref[:, 0:cases] = exact(own[cases:], resid, NT)
    frame_ref[:, cases : cases + ncoarse] = to_lanes(gram[:, cases:], wide_ref)[:, :ncoarse]
    frame_ref[:, second : second + cases] = gram[:, :cases]
    scalar_ref[...] = jnp.zeros_like(scalar_ref)
    scalar_ref[0:1, :] = row_sums(resid * own[:cases])
    scalar_ref[1:2, :] = row_sums(lead * lead)


def second_apply(
    a_ref,
    b_ref,
    ga_ref,
    gb_ref,
    own_a_ref,
    own_b_ref,
    got_a_ref,
    got_b_ref,
    high_t,
    low_t,
    frame_ref,
    scalar_ref,
    strain_ref,
    image_ref,
    scaled_ref,
    pay_ref,
    wide_ref,
    tall_ref,
    *,
    ncoarse,
):
    live = strain_ref.shape[0]
    cases = live - FRAME
    odd = lax.axis_index("sub") % 2 == 1
    even = jnp.logical_not(odd)
    inner = inside()
    image = jnp.concatenate(
        [
            own_a_ref[:live, :] + arrived(got_a_ref[live:, :], even),
            own_b_ref[:live, :] + inner * arrived(got_b_ref[live:, :], odd),
            own_a_ref[live:, :] + arrived(got_a_ref[:live, :], even),
            own_b_ref[live:, :] + arrived(got_b_ref[:live, :], odd),
        ],
        axis=1,
    )
    end = slice(live, live + 1)
    scale = jnp.concatenate(
        [a_ref[end, :], b_ref[end, :], ga_ref[end, :], inner * gb_ref[end, :]], axis=1
    )
    field = scale * image
    strain = times(field, high_t[...], low_t[...], NN)
    own = field[:, :OWN]
    first = image[:, :OWN]
    strain_ref[...] = strain
    image_ref[...] = first
    scaled_ref[...] = own
    paired = jnp.concatenate([own, strain], axis=1)
    gram = exact(paired[cases:], paired, NT)
    cross = exact(first[cases:], own, NT)
    lead = paired[:cases]
    width = cases + ncoarse
    tall_ref[...] = jnp.zeros_like(tall_ref)
    tall_ref[:FRAME, :] = frame_ref[...]
    second = places(cases, ncoarse)[0]
    for block, at, far in (
        (cross, width, width + cases),
        (gram, second + width, second + cases),
    ):
        tall_ref[:FRAME, at : at + cases] = block[:, :cases]
        tall_ref[:FRAME, far : far + ncoarse] = to_lanes(block[:, cases:], wide_ref)[:, :ncoarse]
    pay_ref[...] = pltpu.roll(tall_ref[...], (frame_start() + ncoarse) % ncoarse, 0)
    at = second + width + cases
    pay_ref[0:8, at : at + cases] = scalar_ref[...]
    pay_ref[2:3, at : at + cases] = row_sums(own[:cases] * first[:cases])
    pay_ref[3:4, at : at + cases] = row_sums(lead * lead)


def second_image(scaled_ref, strain_ref, high_ref, low_ref, own_ref, send_a_ref, send_b_ref):
    back = times(strain_ref[...], high_ref[...], low_ref[...], NN)
    own_ref[...] = scaled_ref[...] + back[:, :OWN]
    send_a_ref[...] = back[:, OWN : OWN + EDGE]
    send_b_ref[...] = back[:, OWN + EDGE :]


def window(value, start, count):
    rows = value.shape[0] + 32
    longer = jnp.concatenate([value, jnp.zeros((32, value.shape[1]), F32)], axis=0)
    return pltpu.roll(longer, (rows - start) % rows, 0)[:count]


def widened(own, got_a, got_b, even):
    gap = WIDE - FRAME

    def placed(rows, upper):
        none = jnp.zeros((gap, rows.shape[1]), F32)
        low = jnp.concatenate([rows, none], axis=0)
        return jnp.where(upper, pltpu.roll(low, 2 * STEP, 0), low)

    none = jnp.zeros((gap, own.shape[1]), F32)
    middle = pltpu.roll(jnp.concatenate([own, none], axis=0), STEP, 0)
    return middle + jnp.concatenate(
        [placed(got_a, even), placed(got_b, jnp.logical_not(even))], axis=1
    )


def finish(
    rows_ref,
    inverse_ref,
    resid_ref,
    a_ref,
    b_ref,
    image_ref,
    scaled_ref,
    own_ref,
    got_a_ref,
    got_b_ref,
    *rest,
    ncoarse,
    n_pay,
):
    pays = rest[:n_pay]
    field_hbm, resid2_hbm, field_ref, resid2_ref, blk_ref, sems = rest[n_pay:]
    odd = lax.axis_index("sub") % 2
    live = own_ref.shape[0]
    cases = live - FRAME
    width = cases + ncoarse
    pay = pays[0][...]
    for other in pays[1:]:
        pay = pay + other[...]

    def total(value):
        return jnp.sum(value, axis=0, keepdims=True)

    lead, full = places(cases, ncoarse)
    one, two = pay[:, :lead], pay[:, lead:]
    tile = slice(0, 128)
    u0, g12 = one[:, tile], two[:, tile]
    g14 = pltpu.roll(one, lead - width, 1)[:, tile]
    g34 = pltpu.roll(two, full - lead - width, 1)[:, tile]
    scalars = pltpu.roll(two[0:8], full - lead - width - cases, 1)[:, tile]
    r0d, g11, g13, g33 = (scalars[k : k + 1] for k in range(4))
    inverse = inverse_ref[...]
    y0 = near(inverse, u0)

    def picked(left, at, y):
        def none(rows):
            return [jnp.zeros((rows, 128), F32)] if rows else []

        rest = left.shape[1] - at - ncoarse
        return near(left, jnp.concatenate(none(at) + [y] + none(rest), axis=0))

    y22 = picked(one, cases, y0)
    y24 = picked(one, width + cases, y0)
    y44 = picked(two, cases, y0)
    rz0 = r0d + total(u0 * y0)
    pq0 = g11 + total(y0 * (2.0 * g12 + y22))
    alpha = rz0 / pq0
    u1 = u0 - alpha * (g12 + y22)
    y1 = near(inverse, u1)
    cross = g13 + total(y0 * g14)
    rz1 = (
        r0d
        - 2.0 * alpha * (g11 + total(y0 * g12))
        + alpha * alpha * (cross + total(y0 * (g14 + y24)))
        + total(u1 * y1)
    )
    beta = rz1 / rz0
    ahead = 1.0 + beta
    coarse = y1 + beta * y0
    c22 = picked(one, cases, y1) + beta * y22
    pq1 = (
        ahead * (ahead * g11 + 2.0 * total(coarse * g12) - 2.0 * alpha * cross)
        + total(coarse * (c22 - 2.0 * alpha * (g14 + y24)))
        + alpha * alpha * (g33 + total(y0 * (2.0 * g34 + y44)))
    )
    alpha1 = rz1 / pq1
    lower = alpha1 * alpha
    upper = alpha + alpha1 * ahead
    first = alpha * y0 + alpha1 * coarse
    second = -lower * y0
    begin = frame_start()
    first16 = window(first, begin, FRAME)
    weights = jnp.concatenate([first16, window(second, begin, FRAME)], axis=0)[:, :cases]
    weights2 = jnp.concatenate([first16, window(second, begin - STEP, WIDE)], axis=0)[:, :cases]
    row = lax.broadcasted_iota(jnp.int32, (8, 256), 0)
    half = lax.broadcasted_iota(jnp.int32, (8, 256), 1) // 128
    pair = jnp.concatenate([upper, lower, jnp.zeros((6, 128), F32)], axis=0)[:, :cases]
    columns = exact(pair, jnp.where(row == half, 1.0, 0.0), TN)
    upper = jnp.concatenate([columns[:, :128]] * (OWN // 128), axis=1)
    lower = jnp.concatenate([columns[:, 128:]] * (OWN // 128), axis=1)
    start = jnp.concatenate([a_ref[:live, :], b_ref[:live, :]], axis=1)
    scaled = scaled_ref[...]
    image = image_ref[...]
    own = own_ref[...]
    got_a = got_a_ref[...]
    got_b = inside() * got_b_ref[...]
    image2 = own[:cases] + jnp.concatenate([got_a[:cases], got_b[:cases]], axis=1)
    coarse2 = widened(own[cases:], got_a[cases:], got_b[cases:], odd == 0)
    field = (
        upper * start[:cases]
        - lower * scaled[:cases]
        + near(weights, jnp.concatenate([start[cases:], scaled[cases:]], axis=0), TN)
    )
    resid2 = (
        resid_ref[...]
        - upper * image[:cases]
        + lower * image2
        - near(weights2, jnp.concatenate([image[cases:], coarse2], axis=0), TN)
    )
    copies = []
    for k, (value, out, buf) in enumerate(
        ((field, field_hbm, field_ref), (resid2, resid2_hbm, resid2_ref))
    ):
        for j in range(NB):
            blk_ref[k, place_of(rows_ref, odd, j)] = value[:, B * j : B * (j + 1)]
        for m in range(0, NB, 2):
            buf[:, B * m : B * (m + 2)] = jnp.concatenate([blk_ref[k, m], blk_ref[k, m + 1]], axis=1)
        copies.append(pltpu.make_async_copy(buf, out, sems.at[k]))
        copies[-1].start()
    for copy in copies:
        copy.wait()


def places(cases, ncoarse):
    both = cases + ncoarse
    lead = lanes_for(2 * both)
    return lead, lead + lanes_for(2 * cases + both)


def lanes_for(width):
    return -(-width // 128) * 128


def swap(x, steps, count):
    return [lax.ppermute(x, "sub", [(i, i ^ k) for i in range(count)]) for k in steps]


def rounds_of(count):
    rounds = []
    base = 1
    while base < count:
        turn = 1 if base > 1 else 0
        if base * 4 <= count:
            rounds.append((base, 2 * base + turn, 3 * base + turn))
            base *= 4
        else:
            rounds.append((base,))
            base *= 2
    return rounds


def across(a, b, count, parts):
    low = lax.ppermute(a, "sub", [(i, i ^ 1) for i in range(count)])
    inner = [(i, i + 1) for i in range(1, count - 1, 2)]
    pairs = [(i * parts + x, j * parts + x) for i, j in inner for x in range(parts)]
    ends = [(i * parts + x, i * parts + x + 1) for i in (0, count - 1) for x in range(0, parts - 1, 2)]
    pairs += ends
    return low, lax.ppermute(b, ("sub", "rhs"), pairs + [(j, i) for i, j in pairs])


def inside():
    place = lax.axis_index("sub")
    return jnp.where((place == 0) | (place == lax.axis_size("sub") - 1), 0.0, 1.0)


def body(
    right_side,
    stiffness_blocks,
    block_columns,
    interface_rows,
    corner_owner,
    corner_basis,
    jacobi_scale,
    coarse_inverse,
):
    cases = right_side.shape[0]
    ncoarse = coarse_inverse.shape[0]
    count = lax.axis_size("sub")
    parts = lax.axis_size("rhs")
    live = cases + FRAME
    rounds = rounds_of(count)
    run = functools.partial(call, large=ncoarse > 128)

    bases = [corner_basis] + [
        lax.ppermute(corner_basis, "rhs", [((i + k) % parts, i) for i in range(parts)])
        for k in range(1, parts)
    ]
    packed = jax.ShapeDtypeStruct((NB * KPAD, B * B), BF16)
    wh, wl = call(
        load_blocks,
        [packed, packed],
        1,
        raw=(0,),
        scratch=[
            pltpu.VMEM((B * B // CHUNK, KNZ, NB, CHUNK), F32),
            pltpu.SemaphoreType.DMA((B * B // CHUNK,)),
        ],
        bytes_moved=16 * 1024 * 1024,
        large=True,
    )(jnp.transpose(stiffness_blocks, (1, 0, 2)))
    resid, side_a, side_b = run(
        functools.partial(sides, parts=parts),
        [shape(cases, OWN), shape(live + 8, EDGE), shape(live + 8, EDGE)],
        5 + parts,
        smem=(0, 1),
        scratch=[pltpu.VMEM((NB, live + 8 + cases, B), F32)],
    )(interface_rows, corner_owner, right_side, jacobi_scale.reshape(1, OWN), wh, *bases)
    dense = jax.ShapeDtypeStruct((ROWS, EXT), BF16)
    high, low = run(assemble, [dense, dense], 5, smem=(0,))(
        interface_rows, block_columns, wh, wl, side_a
    )
    turned_g = jax.ShapeDtypeStruct((EXT, ROWS), BF16)
    high_t, low_t = run(turn, [turned_g, turned_g], 2)(high, low)
    ghost_a, ghost_b = across(side_a, side_b, count, parts)
    ends = (side_a, side_b, ghost_a, ghost_b)

    lanes = places(cases, ncoarse)[1]
    wide = pltpu.VMEM((FRAME, lanes_for(ncoarse)), F32)
    strain, own_a, own_b = run(
        first_apply, [shape(live, ROWS), shape(2 * live, EDGE), shape(2 * live, EDGE)], 8
    )(*ends, high, low, high_t, low_t)
    got_a, got_b = across(own_a, own_b, count, parts)
    frame, scalars = run(
        functools.partial(first_sums, ncoarse=ncoarse),
        [shape(FRAME, lanes), shape(8, cases)],
        4,
        scratch=[wide],
    )(resid, side_a, side_b, strain)
    strain, image, scaled, pay = run(
        functools.partial(second_apply, ncoarse=ncoarse),
        [shape(live, ROWS), shape(live, OWN), shape(live, OWN), shape(ncoarse, lanes)],
        12,
        scratch=[wide, pltpu.VMEM((ncoarse, lanes), F32)],
    )(*ends, own_a, own_b, got_a, got_b, high_t, low_t, frame, scalars)
    for steps in rounds[:-1]:
        pay = sum(swap(pay, steps, count), pay)
    pays = [pay] + swap(pay, rounds[-1], count)
    own, back_a, back_b = run(
        second_image, [shape(live, OWN), shape(live, EDGE), shape(live, EDGE)], 4
    )(scaled, strain, high, low)
    got_a, got_b = across(back_a, back_b, count, parts)
    return tuple(
        run(
            functools.partial(finish, ncoarse=ncoarse, n_pay=len(pays)),
            [shape(cases, OWN)] * 2,
            10 + len(pays),
            smem=(0,),
            raw_out=True,
            scratch=[
                pltpu.VMEM((cases, OWN), F32),
                pltpu.VMEM((cases, OWN), F32),
                pltpu.VMEM((2, NB, cases, B), F32),
                pltpu.SemaphoreType.DMA((2,)),
            ],
        )(
            interface_rows,
            coarse_inverse,
            resid,
            side_a,
            side_b,
            image,
            scaled,
            own,
            got_a,
            got_b,
            *pays,
        )
    )


def solution(mesh):
    placed = (
        P("rhs", "sub"),
        P("sub", None, None),
        P("sub", None),
        P("sub", None, None),
        P("sub", None),
        P("rhs", "sub"),
        P("sub"),
        P(),
    )
    return jax.shard_map(
        body,
        mesh=mesh,
        in_specs=placed,
        out_specs=(P("rhs", "sub"), P("rhs", "sub")),
        check_vma=False,
    )
```

```python
import functools

import jax
import jax.numpy as jnp
from jax import lax
from jax.experimental import pallas as pl
from jax.experimental.pallas import tpu as pltpu
from jax.sharding import PartitionSpec as P

B = 64
KNZ = 27
IFB = 4
NCL = 8
NB = 2 * IFB
NE = NB + 2 * IFB
EDGE = IFB * B
OWN = NB * B
EXT = NE * B
ROWS = NB * B
KPAD = 32
F32 = jnp.float32
BF16 = jnp.bfloat16
HIGHEST = lax.Precision.HIGHEST
NT = (((1,), (1,)), ((), ()))
NN = (((1,), (0,)), ((), ()))
VMEM_SMALL = 16 * 1024 * 1024
VMEM_LARGE = 48 * 1024 * 1024
CHUNK = 512
STEP = 2
FRAME = 16
WIDE = 24
TN = (((0,), (0,)), ((), ()))


def split(x):
    high = x.astype(BF16)
    return high, (x - high.astype(F32)).astype(BF16)


def times(x, high, low, dims):
    count = x.shape[0]
    xh, xl = split(x)
    both = lax.dot_general(
        jnp.concatenate([xh, xl], axis=0), high, dims, preferred_element_type=F32
    )
    return both[:count] + both[count:] + lax.dot_general(xh, low, dims, preferred_element_type=F32)


def exact(x, y, dims=NN):
    return lax.dot_general(x, y, dims, precision=HIGHEST, preferred_element_type=F32)


def near(x, y, dims=NN):
    xh, xl = split(x)
    yh, yl = split(y)
    (left,), (right,) = dims[0]
    return lax.dot_general(
        jnp.concatenate([xh, xh, xl], axis=left),
        jnp.concatenate([yh, yl, yh], axis=right),
        dims,
        preferred_element_type=F32,
    )


def call(kernel, outs, n_in, smem=(), raw=(), raw_out=False, scratch=(), bytes_moved=None, large=False):
    def spec(i):
        if i in raw:
            return pl.BlockSpec(memory_space=pltpu.HBM)
        return pl.BlockSpec(memory_space=pltpu.SMEM if i in smem else pltpu.VMEM)

    return pl.pallas_call(
        kernel,
        out_shape=outs,
        in_specs=[spec(i) for i in range(n_in)],
        out_specs=[
            pl.BlockSpec(memory_space=pltpu.HBM if raw_out else pltpu.VMEM) for _ in outs
        ],
        scratch_shapes=list(scratch),
        cost_estimate=bytes_moved
        and pl.CostEstimate(flops=0, transcendentals=0, bytes_accessed=bytes_moved),
        compiler_params=pltpu.CompilerParams(vmem_limit_bytes=VMEM_LARGE if large else VMEM_SMALL),
    )


def shape(*dims):
    return jax.ShapeDtypeStruct(dims, F32)


def place_of(rows_ref, odd, j):
    side = jnp.where(odd == 1, j // IFB, 1 - j // IFB)
    return rows_ref[0, side, j % IFB]


def load_blocks(blocks_hbm, high_ref, low_ref, chunk_ref, sems):
    chunks = [
        pltpu.make_async_copy(
            blocks_hbm.at[:, :, pl.ds(CHUNK * t, CHUNK)], chunk_ref.at[t], sems.at[t]
        )
        for t in range(B * B // CHUNK)
    ]
    for copy in chunks:
        copy.start()
    filler = jnp.zeros((NB * KPAD - NB * (KNZ + 1), B * B), BF16)
    high_ref[NB * (KNZ + 1) :, :] = filler
    low_ref[NB * (KNZ + 1) :, :] = filler
    for t, copy in enumerate(chunks):
        copy.wait()
        padded = jnp.concatenate([chunk_ref[t], jnp.zeros((1, NB, CHUNK), F32)], axis=0)
        wh, wl = split(padded.reshape(NB * (KNZ + 1), CHUNK))
        cut = slice(CHUNK * t, CHUNK * (t + 1))
        high_ref[: NB * (KNZ + 1), cut] = wh
        low_ref[: NB * (KNZ + 1), cut] = wl


def assemble(rows_ref, columns_ref, wh_ref, wl_ref, after_ref, high_ref, low_ref):
    odd = lax.axis_index("sub") % 2
    column = columns_ref[...]
    place = jnp.where(
        (column < NB + IFB) == (odd == 1), column % IFB + NB, column % IFB + NB + IFB
    )
    for j in range(NB):
        place = jnp.where(column == place_of(rows_ref, odd, j), j, place)
    slot = lax.broadcasted_iota(jnp.int32, (KNZ, NB * KPAD), 0)
    entry = lax.broadcasted_iota(jnp.int32, (KNZ, NB * KPAD), 1)
    widen = jnp.where(entry // NB == slot, 1.0, 0.0).astype(BF16)
    wide = lax.dot_general(place.astype(F32).astype(BF16), widen, NN, preferred_element_type=F32)
    r = lax.broadcasted_iota(jnp.int32, (NE * NB, NB * KPAD), 0)
    q = lax.broadcasted_iota(jnp.int32, (NE * NB, NB * KPAD), 1)
    hit = (jnp.concatenate([wide] * NE, axis=0) == (r // NB).astype(F32)) & (r % NB == q % NB)
    onehot = jnp.where(hit, 1.0, 0.0).astype(BF16)
    first = lax.broadcasted_iota(jnp.int32, (NB, 128), 1) < B
    for t in range(B * B // CHUNK):
        cut = slice(CHUNK * t, CHUNK * (t + 1))
        dense = lax.dot_general(
            onehot, wh_ref[:, cut], NN, preferred_element_type=F32
        ) + lax.dot_general(onehot, wl_ref[:, cut], NN, preferred_element_type=F32)
        for m in range(NE // 2):
            for h in range(CHUNK // 128):
                lane = slice(128 * h, 128 * (h + 1))
                left = dense[16 * m : 16 * m + 8, lane]
                right = dense[16 * m + 8 : 16 * m + 16, lane]
                tile = jnp.concatenate(
                    [
                        jnp.where(first, left, pltpu.roll(right, B, 1)),
                        jnp.where(first, pltpu.roll(left, B, 1), right),
                    ],
                    axis=0,
                )
                th, tl = split(tile)
                at = NB * CHUNK // B * t + 16 * h
                high_ref[at : at + 16, 128 * m : 128 * (m + 1)] = th
                low_ref[at : at + 16, 128 * m : 128 * (m + 1)] = tl


def turn(high_ref, low_ref, high_t_ref, low_t_ref):
    high_t_ref[...] = high_ref[...].T
    low_t_ref[...] = low_ref[...].T


def sides(rows_ref, owner_ref, right_ref, scale_ref, after_ref, *rest, parts):
    basis_refs = rest[:parts]
    resid_ref, side_a_ref, side_b_ref, blk_ref = rest[parts:]
    odd = lax.axis_index("sub") % 2
    mine = lax.axis_index("rhs")
    cases = right_ref.shape[0]
    per = NCL // parts
    scale = jnp.broadcast_to(scale_ref[...], (8, OWN))
    unknown = lax.broadcasted_iota(jnp.int32, (FRAME, OWN), 0) + frame_start()
    coarse = jnp.zeros((FRAME, OWN), F32)
    for k in range(parts):
        for t in range(per):
            owner = owner_ref[0, ((mine + k) % parts) * per + t]
            coarse = coarse + jnp.where(unknown == owner, basis_refs[k][t : t + 1, :], 0.0)
    right = right_ref[...]
    fine = right * scale[0:1]
    live = cases + FRAME
    for n in range(NB):
        cut = slice(B * n, B * (n + 1))
        blk_ref[n, 0:cases, :] = fine[:, cut]
        blk_ref[n, cases:live, :] = coarse[:, cut]
        blk_ref[n, live : live + 8, :] = scale[:, cut]
        blk_ref[n, live + 8 :, :] = right[:, cut]
    for j in range(0, NB, 2):
        pair = jnp.concatenate(
            [blk_ref[place_of(rows_ref, odd, j)], blk_ref[place_of(rows_ref, odd, j + 1)]], axis=1
        )
        target = side_a_ref if j < IFB else side_b_ref
        at = B * (j % IFB)
        target[:, at : at + 2 * B] = pair[: live + 8]
        resid_ref[:, B * j : B * (j + 2)] = pair[live + 8 :]


def frame_start():
    return STEP * lax.axis_index("sub") - 6


def turned(rows, upper):
    up = pltpu.roll(rows, STEP, 0)
    down = pltpu.roll(rows, rows.shape[0] - STEP, 0)
    return jnp.where(upper, up, down)


def arrived(rows, upper):
    cases = rows.shape[0] - FRAME
    return jnp.concatenate([rows[:cases], turned(rows[cases:], upper)], axis=0)


def first_apply(
    a_ref, b_ref, ga_ref, gb_ref, high_ref, low_ref, high_t, low_t, strain_ref, send_a_ref, send_b_ref
):
    live = strain_ref.shape[0]
    odd = lax.axis_index("sub") % 2 == 1
    field = jnp.concatenate(
        [
            a_ref[:live, :],
            b_ref[:live, :],
            arrived(ga_ref[:live, :], jnp.logical_not(odd)),
            arrived(inside() * gb_ref[:live, :], odd),
        ],
        axis=1,
    )
    strain = times(field, high_t[...], low_t[...], NN)
    strain_ref[...] = strain
    back = times(strain, high_ref[...], low_ref[...], NN)
    send_a_ref[:live, :] = field[:, :EDGE] + back[:, :EDGE]
    send_a_ref[live:, :] = back[:, OWN : OWN + EDGE]
    send_b_ref[:live, :] = field[:, EDGE:OWN] + back[:, EDGE:OWN]
    send_b_ref[live:, :] = back[:, OWN + EDGE :]


def to_lanes(block, wide_ref):
    width = wide_ref.shape[1]
    wide_ref[...] = jnp.zeros_like(wide_ref)
    wide_ref[:, :FRAME] = block
    return pltpu.roll(wide_ref[...], (frame_start() + width) % width, 1)


def row_sums(value):
    return exact(jnp.ones((8, value.shape[1]), F32), value, NT)[0:1]


def first_sums(resid_ref, a_ref, b_ref, strain_ref, frame_ref, scalar_ref, wide_ref, *, ncoarse):
    live = strain_ref.shape[0]
    cases = live - FRAME
    own = jnp.concatenate([a_ref[:live, :], b_ref[:live, :]], axis=1)
    paired = jnp.concatenate([own, strain_ref[...]], axis=1)
    gram = exact(paired[cases:], paired, NT)
    resid = resid_ref[...]
    lead = paired[:cases]
    second = places(cases, ncoarse)[0]
    frame_ref[...] = jnp.zeros_like(frame_ref)
    frame_ref[:, 0:cases] = exact(own[cases:], resid, NT)
    frame_ref[:, cases : cases + ncoarse] = to_lanes(gram[:, cases:], wide_ref)[:, :ncoarse]
    frame_ref[:, second : second + cases] = gram[:, :cases]
    scalar_ref[...] = jnp.zeros_like(scalar_ref)
    scalar_ref[0:1, :] = row_sums(resid * own[:cases])
    scalar_ref[1:2, :] = row_sums(lead * lead)


def second_apply(
    a_ref,
    b_ref,
    ga_ref,
    gb_ref,
    own_a_ref,
    own_b_ref,
    got_a_ref,
    got_b_ref,
    high_t,
    low_t,
    frame_ref,
    scalar_ref,
    strain_ref,
    image_ref,
    scaled_ref,
    pay_ref,
    wide_ref,
    tall_ref,
    *,
    ncoarse,
):
    live = strain_ref.shape[0]
    cases = live - FRAME
    odd = lax.axis_index("sub") % 2 == 1
    even = jnp.logical_not(odd)
    inner = inside()
    image = jnp.concatenate(
        [
            own_a_ref[:live, :] + arrived(got_a_ref[live:, :], even),
            own_b_ref[:live, :] + inner * arrived(got_b_ref[live:, :], odd),
            own_a_ref[live:, :] + arrived(got_a_ref[:live, :], even),
            own_b_ref[live:, :] + arrived(got_b_ref[:live, :], odd),
        ],
        axis=1,
    )
    end = slice(live, live + 1)
    scale = jnp.concatenate(
        [a_ref[end, :], b_ref[end, :], ga_ref[end, :], inner * gb_ref[end, :]], axis=1
    )
    field = scale * image
    strain = times(field, high_t[...], low_t[...], NN)
    own = field[:, :OWN]
    first = image[:, :OWN]
    strain_ref[...] = strain
    image_ref[...] = first
    scaled_ref[...] = own
    paired = jnp.concatenate([own, strain], axis=1)
    gram = exact(paired[cases:], paired, NT)
    cross = exact(first[cases:], own, NT)
    lead = paired[:cases]
    width = cases + ncoarse
    tall_ref[...] = jnp.zeros_like(tall_ref)
    tall_ref[:FRAME, :] = frame_ref[...]
    second = places(cases, ncoarse)[0]
    for block, at, far in (
        (cross, width, width + cases),
        (gram, second + width, second + cases),
    ):
        tall_ref[:FRAME, at : at + cases] = block[:, :cases]
        tall_ref[:FRAME, far : far + ncoarse] = to_lanes(block[:, cases:], wide_ref)[:, :ncoarse]
    pay_ref[...] = pltpu.roll(tall_ref[...], (frame_start() + ncoarse) % ncoarse, 0)
    at = second + width + cases
    pay_ref[0:8, at : at + cases] = scalar_ref[...]
    pay_ref[2:3, at : at + cases] = row_sums(own[:cases] * first[:cases])
    pay_ref[3:4, at : at + cases] = row_sums(lead * lead)


def second_image(scaled_ref, strain_ref, high_ref, low_ref, own_ref, send_a_ref, send_b_ref):
    back = times(strain_ref[...], high_ref[...], low_ref[...], NN)
    own_ref[...] = scaled_ref[...] + back[:, :OWN]
    send_a_ref[...] = back[:, OWN : OWN + EDGE]
    send_b_ref[...] = back[:, OWN + EDGE :]


def window(value, start, count):
    rows = value.shape[0] + 32
    longer = jnp.concatenate([value, jnp.zeros((32, value.shape[1]), F32)], axis=0)
    return pltpu.roll(longer, (rows - start) % rows, 0)[:count]


def widened(own, got_a, got_b, even):
    gap = WIDE - FRAME

    def placed(rows, upper):
        none = jnp.zeros((gap, rows.shape[1]), F32)
        low = jnp.concatenate([rows, none], axis=0)
        return jnp.where(upper, pltpu.roll(low, 2 * STEP, 0), low)

    none = jnp.zeros((gap, own.shape[1]), F32)
    middle = pltpu.roll(jnp.concatenate([own, none], axis=0), STEP, 0)
    return middle + jnp.concatenate(
        [placed(got_a, even), placed(got_b, jnp.logical_not(even))], axis=1
    )


def settle(
    rows_ref,
    resid_ref,
    a_ref,
    b_ref,
    image_ref,
    scaled_ref,
    own_ref,
    got_a_ref,
    got_b_ref,
    all_ref,
    blk_ref,
):
    odd = lax.axis_index("sub") % 2
    live = own_ref.shape[0]
    cases = live - FRAME
    own = own_ref[...]
    got_a = got_a_ref[...]
    got_b = inside() * got_b_ref[...]
    image2 = own[:cases] + jnp.concatenate([got_a[:cases], got_b[:cases]], axis=1)
    coarse2 = widened(own[cases:], got_a[cases:], got_b[cases:], odd == 0)
    start = jnp.concatenate([a_ref[:live, :], b_ref[:live, :]], axis=1)
    scaled = scaled_ref[...]
    image = image_ref[...]
    at = 0
    for value in (
        resid_ref[...],
        start[:cases],
        scaled[:cases],
        image[:cases],
        image2,
        start[cases:],
        scaled[cases:],
        image[cases:],
        coarse2,
    ):
        end = at + value.shape[0]
        for j in range(NB):
            blk_ref[place_of(rows_ref, odd, j), at:end, :] = value[:, B * j : B * (j + 1)]
        at = end
    for m in range(0, NB, 2):
        all_ref[:, B * m : B * (m + 2)] = jnp.concatenate([blk_ref[m], blk_ref[m + 1]], axis=1)


def finish(inverse_ref, all_ref, *rest, ncoarse, n_pay):
    pays = rest[:n_pay]
    field_hbm, resid2_hbm, field_ref, resid2_ref, sems = rest[n_pay:]
    cases = field_ref.shape[0]
    width = cases + ncoarse
    pay = pays[0][...]
    for other in pays[1:]:
        pay = pay + other[...]

    def total(value):
        return jnp.sum(value, axis=0, keepdims=True)

    lead, full = places(cases, ncoarse)
    one, two = pay[:, :lead], pay[:, lead:]
    tile = slice(0, 128)
    u0, g12 = one[:, tile], two[:, tile]
    g14 = pltpu.roll(one, lead - width, 1)[:, tile]
    g34 = pltpu.roll(two, full - lead - width, 1)[:, tile]
    scalars = pltpu.roll(two[0:8], full - lead - width - cases, 1)[:, tile]
    r0d, g11, g13, g33 = (scalars[k : k + 1] for k in range(4))
    inverse = inverse_ref[...]
    y0 = near(inverse, u0)

    def picked(left, at, y):
        def none(rows):
            return [jnp.zeros((rows, 128), F32)] if rows else []

        rest = left.shape[1] - at - ncoarse
        return near(left, jnp.concatenate(none(at) + [y] + none(rest), axis=0))

    y22 = picked(one, cases, y0)
    y24 = picked(one, width + cases, y0)
    y44 = picked(two, cases, y0)
    rz0 = r0d + total(u0 * y0)
    pq0 = g11 + total(y0 * (2.0 * g12 + y22))
    alpha = rz0 / pq0
    u1 = u0 - alpha * (g12 + y22)
    y1 = near(inverse, u1)
    cross = g13 + total(y0 * g14)
    rz1 = (
        r0d
        - 2.0 * alpha * (g11 + total(y0 * g12))
        + alpha * alpha * (cross + total(y0 * (g14 + y24)))
        + total(u1 * y1)
    )
    beta = rz1 / rz0
    ahead = 1.0 + beta
    coarse = y1 + beta * y0
    c22 = picked(one, cases, y1) + beta * y22
    pq1 = (
        ahead * (ahead * g11 + 2.0 * total(coarse * g12) - 2.0 * alpha * cross)
        + total(coarse * (c22 - 2.0 * alpha * (g14 + y24)))
        + alpha * alpha * (g33 + total(y0 * (2.0 * g34 + y44)))
    )
    alpha1 = rz1 / pq1
    lower = alpha1 * alpha
    upper = alpha + alpha1 * ahead
    first = alpha * y0 + alpha1 * coarse
    second = -lower * y0
    begin = frame_start()
    first16 = window(first, begin, FRAME)
    weights = jnp.concatenate([first16, window(second, begin, FRAME)], axis=0)[:, :cases]
    weights2 = jnp.concatenate([first16, window(second, begin - STEP, WIDE)], axis=0)[:, :cases]
    row = lax.broadcasted_iota(jnp.int32, (8, 256), 0)
    half = lax.broadcasted_iota(jnp.int32, (8, 256), 1) // 128
    pair = jnp.concatenate([upper, lower, jnp.zeros((6, 128), F32)], axis=0)[:, :cases]
    columns = exact(pair, jnp.where(row == half, 1.0, 0.0), TN)
    upper = jnp.concatenate([columns[:, :128]] * (OWN // 128), axis=1)
    lower = jnp.concatenate([columns[:, 128:]] * (OWN // 128), axis=1)
    resid, fine, scaled, image, image2 = (
        all_ref[k * cases : (k + 1) * cases, :] for k in range(5)
    )
    at = 5 * cases
    field_ref[...] = upper * fine - lower * scaled + near(weights, all_ref[at : at + 2 * FRAME, :], TN)
    copies = [pltpu.make_async_copy(field_ref, field_hbm, sems.at[0])]
    copies[0].start()
    at += 2 * FRAME
    resid2_ref[...] = (
        resid
        - upper * image
        + lower * image2
        - near(weights2, all_ref[at : at + FRAME + WIDE, :], TN)
    )
    copies.append(pltpu.make_async_copy(resid2_ref, resid2_hbm, sems.at[1]))
    copies[1].start()
    for copy in copies:
        copy.wait()


def places(cases, ncoarse):
    both = cases + ncoarse
    lead = lanes_for(2 * both)
    return lead, lead + lanes_for(2 * cases + both)


def lanes_for(width):
    return -(-width // 128) * 128


def swap(x, steps, count):
    return [lax.ppermute(x, "sub", [(i, i ^ k) for i in range(count)]) for k in steps]


def rounds_of(count):
    rounds = []
    base = 1
    while base < count:
        turn = 1 if base > 1 else 0
        if base * 4 <= count:
            rounds.append((base, 2 * base + turn, 3 * base + turn))
            base *= 4
        else:
            rounds.append((base,))
            base *= 2
    return rounds


def across(a, b, count, parts):
    low = lax.ppermute(a, "sub", [(i, i ^ 1) for i in range(count)])
    inner = [(i, i + 1) for i in range(1, count - 1, 2)]
    pairs = [(i * parts + x, j * parts + x) for i, j in inner for x in range(parts)]
    ends = [(i * parts + x, i * parts + x + 1) for i in (0, count - 1) for x in range(0, parts - 1, 2)]
    pairs += ends
    return low, lax.ppermute(b, ("sub", "rhs"), pairs + [(j, i) for i, j in pairs])


def inside():
    place = lax.axis_index("sub")
    return jnp.where((place == 0) | (place == lax.axis_size("sub") - 1), 0.0, 1.0)


def body(
    right_side,
    stiffness_blocks,
    block_columns,
    interface_rows,
    corner_owner,
    corner_basis,
    jacobi_scale,
    coarse_inverse,
):
    cases = right_side.shape[0]
    ncoarse = coarse_inverse.shape[0]
    count = lax.axis_size("sub")
    parts = lax.axis_size("rhs")
    live = cases + FRAME
    rounds = rounds_of(count)
    run = functools.partial(call, large=ncoarse > 128)

    bases = [corner_basis] + [
        lax.ppermute(corner_basis, "rhs", [((i + k) % parts, i) for i in range(parts)])
        for k in range(1, parts)
    ]
    packed = jax.ShapeDtypeStruct((NB * KPAD, B * B), BF16)
    wh, wl = call(
        load_blocks,
        [packed, packed],
        1,
        raw=(0,),
        scratch=[
            pltpu.VMEM((B * B // CHUNK, KNZ, NB, CHUNK), F32),
            pltpu.SemaphoreType.DMA((B * B // CHUNK,)),
        ],
        bytes_moved=16 * 1024 * 1024,
        large=True,
    )(jnp.transpose(stiffness_blocks, (1, 0, 2)))
    resid, side_a, side_b = run(
        functools.partial(sides, parts=parts),
        [shape(cases, OWN), shape(live + 8, EDGE), shape(live + 8, EDGE)],
        5 + parts,
        smem=(0, 1),
        scratch=[pltpu.VMEM((NB, live + 8 + cases, B), F32)],
    )(interface_rows, corner_owner, right_side, jacobi_scale.reshape(1, OWN), wh, *bases)
    dense = jax.ShapeDtypeStruct((ROWS, EXT), BF16)
    high, low = run(assemble, [dense, dense], 5, smem=(0,))(
        interface_rows, block_columns, wh, wl, side_a
    )
    turned_g = jax.ShapeDtypeStruct((EXT, ROWS), BF16)
    high_t, low_t = run(turn, [turned_g, turned_g], 2)(high, low)
    ghost_a, ghost_b = across(side_a, side_b, count, parts)
    ends = (side_a, side_b, ghost_a, ghost_b)

    lanes = places(cases, ncoarse)[1]
    wide = pltpu.VMEM((FRAME, lanes_for(ncoarse)), F32)
    strain, own_a, own_b = run(
        first_apply, [shape(live, ROWS), shape(2 * live, EDGE), shape(2 * live, EDGE)], 8
    )(*ends, high, low, high_t, low_t)
    got_a, got_b = across(own_a, own_b, count, parts)
    frame, scalars = run(
        functools.partial(first_sums, ncoarse=ncoarse),
        [shape(FRAME, lanes), shape(8, cases)],
        4,
        scratch=[wide],
    )(resid, side_a, side_b, strain)
    strain, image, scaled, pay = run(
        functools.partial(second_apply, ncoarse=ncoarse),
        [shape(live, ROWS), shape(live, OWN), shape(live, OWN), shape(ncoarse, lanes)],
        12,
        scratch=[wide, pltpu.VMEM((ncoarse, lanes), F32)],
    )(*ends, own_a, own_b, got_a, got_b, high_t, low_t, frame, scalars)
    for steps in rounds[:-1]:
        pay = sum(swap(pay, steps, count), pay)
    pays = [pay] + swap(pay, rounds[-1], count)
    own, back_a, back_b = run(
        second_image, [shape(live, OWN), shape(live, EDGE), shape(live, EDGE)], 4
    )(scaled, strain, high, low)
    got_a, got_b = across(back_a, back_b, count, parts)
    height = 5 * cases + 3 * FRAME + WIDE
    (everything,) = run(
        settle,
        [shape(height, OWN)],
        9,
        smem=(0,),
        scratch=[pltpu.VMEM((NB, height, B), F32)],
    )(interface_rows, resid, side_a, side_b, image, scaled, own, got_a, got_b)
    return tuple(
        run(
            functools.partial(finish, ncoarse=ncoarse, n_pay=len(pays)),
            [shape(cases, OWN)] * 2,
            2 + len(pays),
            raw_out=True,
            scratch=[
                pltpu.VMEM((cases, OWN), F32),
                pltpu.VMEM((cases, OWN), F32),
                pltpu.SemaphoreType.DMA((2,)),
            ],
        )(coarse_inverse, everything, *pays)
    )


def solution(mesh):
    placed = (
        P("rhs", "sub"),
        P("sub", None, None),
        P("sub", None),
        P("sub", None, None),
        P("sub", None),
        P("rhs", "sub"),
        P("sub"),
        P(),
    )
    return jax.shard_map(
        body,
        mesh=mesh,
        in_specs=placed,
        out_specs=(P("rhs", "sub"), P("rhs", "sub")),
        check_vma=False,
    )
```

```python
import functools

import jax
import jax.numpy as jnp
from jax import lax
from jax.experimental import pallas as pl
from jax.experimental.pallas import tpu as pltpu
from jax.sharding import PartitionSpec as P

B = 64
KNZ = 27
IFB = 4
NCL = 8
NB = 2 * IFB
NE = NB + 2 * IFB
EDGE = IFB * B
OWN = NB * B
EXT = NE * B
ROWS = NB * B
KPAD = 32
F32 = jnp.float32
BF16 = jnp.bfloat16
HIGHEST = lax.Precision.HIGHEST
NT = (((1,), (1,)), ((), ()))
NN = (((1,), (0,)), ((), ()))
VMEM_SMALL = 16 * 1024 * 1024
VMEM_LARGE = 48 * 1024 * 1024
CHUNK = 512
STEP = 2
FRAME = 16
WIDE = 24
TN = (((0,), (0,)), ((), ()))


def split(x):
    high = x.astype(BF16)
    return high, (x - high.astype(F32)).astype(BF16)


def times(x, high, low, dims):
    count = x.shape[0]
    xh, xl = split(x)
    both = lax.dot_general(
        jnp.concatenate([xh, xl], axis=0), high, dims, preferred_element_type=F32
    )
    return both[:count] + both[count:] + lax.dot_general(xh, low, dims, preferred_element_type=F32)


def exact(x, y, dims=NN):
    return lax.dot_general(x, y, dims, precision=HIGHEST, preferred_element_type=F32)


def near(x, y, dims=NN):
    xh, xl = split(x)
    yh, yl = split(y)
    (left,), (right,) = dims[0]
    return lax.dot_general(
        jnp.concatenate([xh, xh, xl], axis=left),
        jnp.concatenate([yh, yl, yh], axis=right),
        dims,
        preferred_element_type=F32,
    )


def call(kernel, outs, n_in, smem=(), raw=(), raw_out=False, scratch=(), bytes_moved=None, large=False):
    def spec(i):
        if i in raw:
            return pl.BlockSpec(memory_space=pltpu.HBM)
        return pl.BlockSpec(memory_space=pltpu.SMEM if i in smem else pltpu.VMEM)

    return pl.pallas_call(
        kernel,
        out_shape=outs,
        in_specs=[spec(i) for i in range(n_in)],
        out_specs=[
            pl.BlockSpec(memory_space=pltpu.HBM if raw_out else pltpu.VMEM) for _ in outs
        ],
        scratch_shapes=list(scratch),
        cost_estimate=bytes_moved
        and pl.CostEstimate(flops=0, transcendentals=0, bytes_accessed=bytes_moved),
        compiler_params=pltpu.CompilerParams(vmem_limit_bytes=VMEM_LARGE if large else VMEM_SMALL),
    )


def shape(*dims):
    return jax.ShapeDtypeStruct(dims, F32)


def place_of(rows_ref, odd, j):
    side = jnp.where(odd == 1, j // IFB, 1 - j // IFB)
    return rows_ref[0, side, j % IFB]


def load_blocks(blocks_hbm, high_ref, low_ref, chunk_ref, sems):
    chunks = [
        pltpu.make_async_copy(
            blocks_hbm.at[:, :, pl.ds(CHUNK * t, CHUNK)], chunk_ref.at[t], sems.at[t]
        )
        for t in range(B * B // CHUNK)
    ]
    for copy in chunks:
        copy.start()
    filler = jnp.zeros((NB * KPAD - NB * (KNZ + 1), B * B), BF16)
    high_ref[NB * (KNZ + 1) :, :] = filler
    low_ref[NB * (KNZ + 1) :, :] = filler
    for t, copy in enumerate(chunks):
        copy.wait()
        padded = jnp.concatenate([chunk_ref[t], jnp.zeros((1, NB, CHUNK), F32)], axis=0)
        wh, wl = split(padded.reshape(NB * (KNZ + 1), CHUNK))
        cut = slice(CHUNK * t, CHUNK * (t + 1))
        high_ref[: NB * (KNZ + 1), cut] = wh
        low_ref[: NB * (KNZ + 1), cut] = wl


def assemble(rows_ref, columns_ref, wh_ref, wl_ref, after_ref, high_ref, low_ref):
    odd = lax.axis_index("sub") % 2
    column = columns_ref[...]
    place = jnp.where(
        (column < NB + IFB) == (odd == 1), column % IFB + NB, column % IFB + NB + IFB
    )
    for j in range(NB):
        place = jnp.where(column == place_of(rows_ref, odd, j), j, place)
    slot = lax.broadcasted_iota(jnp.int32, (KNZ, NB * KPAD), 0)
    entry = lax.broadcasted_iota(jnp.int32, (KNZ, NB * KPAD), 1)
    widen = jnp.where(entry // NB == slot, 1.0, 0.0).astype(BF16)
    wide = lax.dot_general(place.astype(F32).astype(BF16), widen, NN, preferred_element_type=F32)
    r = lax.broadcasted_iota(jnp.int32, (NE * NB, NB * KPAD), 0)
    q = lax.broadcasted_iota(jnp.int32, (NE * NB, NB * KPAD), 1)
    hit = (jnp.concatenate([wide] * NE, axis=0) == (r // NB).astype(F32)) & (r % NB == q % NB)
    onehot = jnp.where(hit, 1.0, 0.0).astype(BF16)
    first = lax.broadcasted_iota(jnp.int32, (NB, 128), 1) < B
    for t in range(B * B // CHUNK):
        cut = slice(CHUNK * t, CHUNK * (t + 1))
        dense = lax.dot_general(
            onehot, wh_ref[:, cut], NN, preferred_element_type=F32
        ) + lax.dot_general(onehot, wl_ref[:, cut], NN, preferred_element_type=F32)
        for m in range(NE // 2):
            for h in range(CHUNK // 128):
                lane = slice(128 * h, 128 * (h + 1))
                left = dense[16 * m : 16 * m + 8, lane]
                right = dense[16 * m + 8 : 16 * m + 16, lane]
                tile = jnp.concatenate(
                    [
                        jnp.where(first, left, pltpu.roll(right, B, 1)),
                        jnp.where(first, pltpu.roll(left, B, 1), right),
                    ],
                    axis=0,
                )
                th, tl = split(tile)
                at = NB * CHUNK // B * t + 16 * h
                high_ref[at : at + 16, 128 * m : 128 * (m + 1)] = th
                low_ref[at : at + 16, 128 * m : 128 * (m + 1)] = tl


def turn(high_ref, low_ref, high_t_ref, low_t_ref):
    high_t_ref[...] = high_ref[...].T
    low_t_ref[...] = low_ref[...].T


def sides(rows_ref, owner_ref, right_ref, scale_ref, after_ref, *rest, parts):
    basis_refs = rest[:parts]
    resid_ref, side_a_ref, side_b_ref, blk_ref = rest[parts:]
    odd = lax.axis_index("sub") % 2
    mine = lax.axis_index("rhs")
    cases = right_ref.shape[0]
    per = NCL // parts
    scale = jnp.broadcast_to(scale_ref[...], (8, OWN))
    unknown = lax.broadcasted_iota(jnp.int32, (FRAME, OWN), 0) + frame_start()
    coarse = jnp.zeros((FRAME, OWN), F32)
    for k in range(parts):
        for t in range(per):
            owner = owner_ref[0, ((mine + k) % parts) * per + t]
            coarse = coarse + jnp.where(unknown == owner, basis_refs[k][t : t + 1, :], 0.0)
    right = right_ref[...]
    fine = right * scale[0:1]
    live = cases + FRAME
    for n in range(NB):
        cut = slice(B * n, B * (n + 1))
        blk_ref[n, 0:cases, :] = fine[:, cut]
        blk_ref[n, cases:live, :] = coarse[:, cut]
        blk_ref[n, live : live + 8, :] = scale[:, cut]
        blk_ref[n, live + 8 :, :] = right[:, cut]
    for j in range(0, NB, 2):
        pair = jnp.concatenate(
            [blk_ref[place_of(rows_ref, odd, j)], blk_ref[place_of(rows_ref, odd, j + 1)]], axis=1
        )
        target = side_a_ref if j < IFB else side_b_ref
        at = B * (j % IFB)
        target[:, at : at + 2 * B] = pair[: live + 8]
        resid_ref[:, B * j : B * (j + 2)] = pair[live + 8 :]


def frame_start():
    return STEP * lax.axis_index("sub") - 6


def turned(rows, upper):
    up = pltpu.roll(rows, STEP, 0)
    down = pltpu.roll(rows, rows.shape[0] - STEP, 0)
    return jnp.where(upper, up, down)


def arrived(rows, upper):
    cases = rows.shape[0] - FRAME
    return jnp.concatenate([rows[:cases], turned(rows[cases:], upper)], axis=0)


def first_apply(
    a_ref, b_ref, ga_ref, gb_ref, high_ref, low_ref, high_t, low_t, strain_ref, send_a_ref, send_b_ref
):
    live = strain_ref.shape[0]
    odd = lax.axis_index("sub") % 2 == 1
    field = jnp.concatenate(
        [
            a_ref[:live, :],
            b_ref[:live, :],
            arrived(ga_ref[:live, :], jnp.logical_not(odd)),
            arrived(inside() * gb_ref[:live, :], odd),
        ],
        axis=1,
    )
    strain = times(field, high_t[...], low_t[...], NN)
    strain_ref[...] = strain
    back = times(strain, high_ref[...], low_ref[...], NN)
    send_a_ref[:live, :] = field[:, :EDGE] + back[:, :EDGE]
    send_a_ref[live:, :] = back[:, OWN : OWN + EDGE]
    send_b_ref[:live, :] = field[:, EDGE:OWN] + back[:, EDGE:OWN]
    send_b_ref[live:, :] = back[:, OWN + EDGE :]


def to_lanes(block, wide_ref):
    width = wide_ref.shape[1]
    wide_ref[...] = jnp.zeros_like(wide_ref)
    wide_ref[:, :FRAME] = block
    return pltpu.roll(wide_ref[...], (frame_start() + width) % width, 1)


def row_sums(value):
    return exact(jnp.ones((8, value.shape[1]), F32), value, NT)[0:1]


def first_sums(resid_ref, a_ref, b_ref, strain_ref, frame_ref, scalar_ref, wide_ref, *, ncoarse):
    live = strain_ref.shape[0]
    cases = live - FRAME
    own = jnp.concatenate([a_ref[:live, :], b_ref[:live, :]], axis=1)
    paired = jnp.concatenate([own, strain_ref[...]], axis=1)
    gram = exact(paired[cases:], paired, NT)
    resid = resid_ref[...]
    lead = paired[:cases]
    second = places(cases, ncoarse)[0]
    frame_ref[...] = jnp.zeros_like(frame_ref)
    frame_ref[:, 0:cases] = exact(own[cases:], resid, NT)
    frame_ref[:, cases : cases + ncoarse] = to_lanes(gram[:, cases:], wide_ref)[:, :ncoarse]
    frame_ref[:, second : second + cases] = gram[:, :cases]
    scalar_ref[...] = jnp.zeros_like(scalar_ref)
    scalar_ref[0:1, :] = row_sums(resid * own[:cases])
    scalar_ref[1:2, :] = row_sums(lead * lead)


def second_apply(
    a_ref,
    b_ref,
    ga_ref,
    gb_ref,
    own_a_ref,
    own_b_ref,
    got_a_ref,
    got_b_ref,
    high_t,
    low_t,
    frame_ref,
    scalar_ref,
    strain_ref,
    image_ref,
    scaled_ref,
    pay_ref,
    wide_ref,
    tall_ref,
    *,
    ncoarse,
):
    live = strain_ref.shape[0]
    cases = live - FRAME
    odd = lax.axis_index("sub") % 2 == 1
    even = jnp.logical_not(odd)
    inner = inside()
    image = jnp.concatenate(
        [
            own_a_ref[:live, :] + arrived(got_a_ref[live:, :], even),
            own_b_ref[:live, :] + inner * arrived(got_b_ref[live:, :], odd),
            own_a_ref[live:, :] + arrived(got_a_ref[:live, :], even),
            own_b_ref[live:, :] + arrived(got_b_ref[:live, :], odd),
        ],
        axis=1,
    )
    end = slice(live, live + 1)
    scale = jnp.concatenate(
        [a_ref[end, :], b_ref[end, :], ga_ref[end, :], inner * gb_ref[end, :]], axis=1
    )
    field = scale * image
    strain = times(field, high_t[...], low_t[...], NN)
    own = field[:, :OWN]
    first = image[:, :OWN]
    strain_ref[...] = strain
    image_ref[...] = first
    scaled_ref[...] = own
    paired = jnp.concatenate([own, strain], axis=1)
    gram = exact(paired[cases:], paired, NT)
    cross = exact(first[cases:], own, NT)
    lead = paired[:cases]
    width = cases + ncoarse
    tall_ref[...] = jnp.zeros_like(tall_ref)
    tall_ref[:FRAME, :] = frame_ref[...]
    second = places(cases, ncoarse)[0]
    for block, at, far in (
        (cross, width, width + cases),
        (gram, second + width, second + cases),
    ):
        tall_ref[:FRAME, at : at + cases] = block[:, :cases]
        tall_ref[:FRAME, far : far + ncoarse] = to_lanes(block[:, cases:], wide_ref)[:, :ncoarse]
    pay_ref[...] = pltpu.roll(tall_ref[...], (frame_start() + ncoarse) % ncoarse, 0)
    at = second + width + cases
    pay_ref[0:8, at : at + cases] = scalar_ref[...]
    pay_ref[2:3, at : at + cases] = row_sums(own[:cases] * first[:cases])
    pay_ref[3:4, at : at + cases] = row_sums(lead * lead)


def second_image(scaled_ref, strain_ref, high_ref, low_ref, own_ref, send_a_ref, send_b_ref):
    back = times(strain_ref[...], high_ref[...], low_ref[...], NN)
    own_ref[...] = scaled_ref[...] + back[:, :OWN]
    send_a_ref[...] = back[:, OWN : OWN + EDGE]
    send_b_ref[...] = back[:, OWN + EDGE :]


def window(value, start, count):
    rows = value.shape[0] + 32
    longer = jnp.concatenate([value, jnp.zeros((32, value.shape[1]), F32)], axis=0)
    return pltpu.roll(longer, (rows - start) % rows, 0)[:count]


def widened(own, got_a, got_b, even):
    gap = WIDE - FRAME

    def placed(rows, upper):
        none = jnp.zeros((gap, rows.shape[1]), F32)
        low = jnp.concatenate([rows, none], axis=0)
        return jnp.where(upper, pltpu.roll(low, 2 * STEP, 0), low)

    none = jnp.zeros((gap, own.shape[1]), F32)
    middle = pltpu.roll(jnp.concatenate([own, none], axis=0), STEP, 0)
    return middle + jnp.concatenate(
        [placed(got_a, even), placed(got_b, jnp.logical_not(even))], axis=1
    )


def settle(
    rows_ref,
    resid_ref,
    a_ref,
    b_ref,
    image_ref,
    scaled_ref,
    own_ref,
    got_a_ref,
    got_b_ref,
    all_ref,
    blk_ref,
):
    odd = lax.axis_index("sub") % 2
    live = own_ref.shape[0]
    cases = live - FRAME
    own = own_ref[...]
    got_a = got_a_ref[...]
    got_b = inside() * got_b_ref[...]
    image2 = own[:cases] + jnp.concatenate([got_a[:cases], got_b[:cases]], axis=1)
    coarse2 = widened(own[cases:], got_a[cases:], got_b[cases:], odd == 0)
    start = jnp.concatenate([a_ref[:live, :], b_ref[:live, :]], axis=1)
    scaled = scaled_ref[...]
    image = image_ref[...]
    at = 0
    for value in (
        resid_ref[...],
        start[:cases],
        scaled[:cases],
        image[:cases],
        image2,
        start[cases:],
        scaled[cases:],
        image[cases:],
        coarse2,
    ):
        end = at + value.shape[0]
        for j in range(NB):
            blk_ref[place_of(rows_ref, odd, j), at:end, :] = value[:, B * j : B * (j + 1)]
        at = end
    for m in range(0, NB, 2):
        all_ref[:, B * m : B * (m + 2)] = jnp.concatenate([blk_ref[m], blk_ref[m + 1]], axis=1)


def finish(inverse_ref, all_ref, *rest, ncoarse, n_pay):
    pays = rest[:n_pay]
    field_hbm, resid2_hbm, field_ref, resid2_ref, sems = rest[n_pay:]
    cases = field_ref.shape[0]
    width = cases + ncoarse
    pay = pays[0][...]
    for other in pays[1:]:
        pay = pay + other[...]

    def total(value):
        return jnp.sum(value, axis=0, keepdims=True)

    lead, full = places(cases, ncoarse)
    one, two = pay[:, :lead], pay[:, lead:]
    tile = slice(0, 128)
    u0, g12 = one[:, tile], two[:, tile]
    g14 = pltpu.roll(one, lead - width, 1)[:, tile]
    g34 = pltpu.roll(two, full - lead - width, 1)[:, tile]
    scalars = pltpu.roll(two[0:8], full - lead - width - cases, 1)[:, tile]
    r0d, g11, g13, g33 = (scalars[k : k + 1] for k in range(4))
    inverse = inverse_ref[...]
    y0 = near(inverse, u0)

    def picked(left, at, y):
        def none(rows):
            return [jnp.zeros((rows, 128), F32)] if rows else []

        rest = left.shape[1] - at - ncoarse
        return near(left, jnp.concatenate(none(at) + [y] + none(rest), axis=0))

    y22 = picked(one, cases, y0)
    y24 = picked(one, width + cases, y0)
    y44 = picked(two, cases, y0)
    rz0 = r0d + total(u0 * y0)
    pq0 = g11 + total(y0 * (2.0 * g12 + y22))
    alpha = rz0 / pq0
    u1 = u0 - alpha * (g12 + y22)
    y1 = near(inverse, u1)
    cross = g13 + total(y0 * g14)
    rz1 = (
        r0d
        - 2.0 * alpha * (g11 + total(y0 * g12))
        + alpha * alpha * (cross + total(y0 * (g14 + y24)))
        + total(u1 * y1)
    )
    beta = rz1 / rz0
    ahead = 1.0 + beta
    coarse = y1 + beta * y0
    c22 = picked(one, cases, y1) + beta * y22
    pq1 = (
        ahead * (ahead * g11 + 2.0 * total(coarse * g12) - 2.0 * alpha * cross)
        + total(coarse * (c22 - 2.0 * alpha * (g14 + y24)))
        + alpha * alpha * (g33 + total(y0 * (2.0 * g34 + y44)))
    )
    alpha1 = rz1 / pq1
    lower = alpha1 * alpha
    upper = alpha + alpha1 * ahead
    first = alpha * y0 + alpha1 * coarse
    second = -lower * y0
    begin = frame_start()
    first16 = window(first, begin, FRAME)
    weights = jnp.concatenate([first16, window(second, begin, FRAME)], axis=0)[:, :cases]
    weights2 = jnp.concatenate([first16, window(second, begin - STEP, WIDE)], axis=0)[:, :cases]
    row = lax.broadcasted_iota(jnp.int32, (8, 256), 0)
    half = lax.broadcasted_iota(jnp.int32, (8, 256), 1) // 128
    pair = jnp.concatenate([upper, lower, jnp.zeros((6, 128), F32)], axis=0)[:, :cases]
    columns = exact(pair, jnp.where(row == half, 1.0, 0.0), TN)
    upper = jnp.concatenate([columns[:, :128]] * (OWN // 128), axis=1)
    lower = jnp.concatenate([columns[:, 128:]] * (OWN // 128), axis=1)
    resid, fine, scaled, image, image2 = (
        all_ref[k * cases : (k + 1) * cases, :] for k in range(5)
    )
    at = 5 * cases
    field_ref[...] = upper * fine - lower * scaled + near(weights, all_ref[at : at + 2 * FRAME, :], TN)
    copies = [pltpu.make_async_copy(field_ref, field_hbm, sems.at[0])]
    copies[0].start()
    at += 2 * FRAME
    resid2_ref[...] = (
        resid
        - upper * image
        + lower * image2
        - near(weights2, all_ref[at : at + FRAME + WIDE, :], TN)
    )
    copies.append(pltpu.make_async_copy(resid2_ref, resid2_hbm, sems.at[1]))
    copies[1].start()
    for copy in copies:
        copy.wait()


def places(cases, ncoarse):
    both = cases + ncoarse
    lead = lanes_for(2 * both)
    return lead, lead + lanes_for(2 * cases + both)


def lanes_for(width):
    return -(-width // 128) * 128


def swap(x, steps, count):
    return [lax.ppermute(x, "sub", [(i, i ^ k) for i in range(count)]) for k in steps]


def rounds_of(count):
    rounds = []
    base = 1
    while base < count:
        if base * 4 <= count:
            rounds.append((base, 2 * base + 1, 3 * base + 1) if base > 1 else (1, 3, 2))
            base *= 4
        else:
            rounds.append((base,))
            base *= 2
    return rounds


def across(a, b, count, parts):
    low = lax.ppermute(a, "sub", [(i, i ^ 1) for i in range(count)])
    inner = [(i, i + 1) for i in range(1, count - 1, 2)]
    pairs = [(i * parts + x, j * parts + x) for i, j in inner for x in range(parts)]
    ends = [(i * parts + x, i * parts + x + 1) for i in (0, count - 1) for x in range(0, parts - 1, 2)]
    pairs += ends
    return low, lax.ppermute(b, ("sub", "rhs"), pairs + [(j, i) for i, j in pairs])


def inside():
    place = lax.axis_index("sub")
    return jnp.where((place == 0) | (place == lax.axis_size("sub") - 1), 0.0, 1.0)


def body(
    right_side,
    stiffness_blocks,
    block_columns,
    interface_rows,
    corner_owner,
    corner_basis,
    jacobi_scale,
    coarse_inverse,
):
    cases = right_side.shape[0]
    ncoarse = coarse_inverse.shape[0]
    count = lax.axis_size("sub")
    parts = lax.axis_size("rhs")
    live = cases + FRAME
    rounds = rounds_of(count)
    run = functools.partial(call, large=ncoarse > 128)

    bases = [corner_basis] + [
        lax.ppermute(corner_basis, "rhs", [((i + k) % parts, i) for i in range(parts)])
        for k in range(1, parts)
    ]
    packed = jax.ShapeDtypeStruct((NB * KPAD, B * B), BF16)
    wh, wl = call(
        load_blocks,
        [packed, packed],
        1,
        raw=(0,),
        scratch=[
            pltpu.VMEM((B * B // CHUNK, KNZ, NB, CHUNK), F32),
            pltpu.SemaphoreType.DMA((B * B // CHUNK,)),
        ],
        bytes_moved=16 * 1024 * 1024,
        large=True,
    )(jnp.transpose(stiffness_blocks, (1, 0, 2)))
    resid, side_a, side_b = run(
        functools.partial(sides, parts=parts),
        [shape(cases, OWN), shape(live + 8, EDGE), shape(live + 8, EDGE)],
        5 + parts,
        smem=(0, 1),
        scratch=[pltpu.VMEM((NB, live + 8 + cases, B), F32)],
    )(interface_rows, corner_owner, right_side, jacobi_scale.reshape(1, OWN), wh, *bases)
    dense = jax.ShapeDtypeStruct((ROWS, EXT), BF16)
    high, low = run(assemble, [dense, dense], 5, smem=(0,))(
        interface_rows, block_columns, wh, wl, side_a
    )
    turned_g = jax.ShapeDtypeStruct((EXT, ROWS), BF16)
    high_t, low_t = run(turn, [turned_g, turned_g], 2)(high, low)
    ghost_a, ghost_b = across(side_a, side_b, count, parts)
    ends = (side_a, side_b, ghost_a, ghost_b)

    lanes = places(cases, ncoarse)[1]
    wide = pltpu.VMEM((FRAME, lanes_for(ncoarse)), F32)
    strain, own_a, own_b = run(
        first_apply, [shape(live, ROWS), shape(2 * live, EDGE), shape(2 * live, EDGE)], 8
    )(*ends, high, low, high_t, low_t)
    got_a, got_b = across(own_a, own_b, count, parts)
    frame, scalars = run(
        functools.partial(first_sums, ncoarse=ncoarse),
        [shape(FRAME, lanes), shape(8, cases)],
        4,
        scratch=[wide],
    )(resid, side_a, side_b, strain)
    strain, image, scaled, pay = run(
        functools.partial(second_apply, ncoarse=ncoarse),
        [shape(live, ROWS), shape(live, OWN), shape(live, OWN), shape(ncoarse, lanes)],
        12,
        scratch=[wide, pltpu.VMEM((ncoarse, lanes), F32)],
    )(*ends, own_a, own_b, got_a, got_b, high_t, low_t, frame, scalars)
    for steps in rounds[:-1]:
        pay = sum(swap(pay, steps, count), pay)
    pays = [pay] + swap(pay, rounds[-1], count)
    own, back_a, back_b = run(
        second_image, [shape(live, OWN), shape(live, EDGE), shape(live, EDGE)], 4
    )(scaled, strain, high, low)
    got_a, got_b = across(back_a, back_b, count, parts)
    height = 5 * cases + 3 * FRAME + WIDE
    (everything,) = run(
        settle,
        [shape(height, OWN)],
        9,
        smem=(0,),
        scratch=[pltpu.VMEM((NB, height, B), F32)],
    )(interface_rows, resid, side_a, side_b, image, scaled, own, got_a, got_b)
    return tuple(
        run(
            functools.partial(finish, ncoarse=ncoarse, n_pay=len(pays)),
            [shape(cases, OWN)] * 2,
            2 + len(pays),
            raw_out=True,
            scratch=[
                pltpu.VMEM((cases, OWN), F32),
                pltpu.VMEM((cases, OWN), F32),
                pltpu.SemaphoreType.DMA((2,)),
            ],
        )(coarse_inverse, everything, *pays)
    )


def solution(mesh):
    placed = (
        P("rhs", "sub"),
        P("sub", None, None),
        P("sub", None),
        P("sub", None, None),
        P("sub", None),
        P("rhs", "sub"),
        P("sub"),
        P(),
    )
    return jax.shard_map(
        body,
        mesh=mesh,
        in_specs=placed,
        out_specs=(P("rhs", "sub"), P("rhs", "sub")),
        check_vma=False,
    )
```

```python
import functools

import jax
import jax.numpy as jnp
from jax import lax
from jax.experimental import pallas as pl
from jax.experimental.pallas import tpu as pltpu
from jax.sharding import PartitionSpec as P

B = 64
KNZ = 27
IFB = 4
NCL = 8
NB = 2 * IFB
NE = NB + 2 * IFB
EDGE = IFB * B
OWN = NB * B
EXT = NE * B
ROWS = NB * B
KPAD = 32
F32 = jnp.float32
BF16 = jnp.bfloat16
HIGHEST = lax.Precision.HIGHEST
NT = (((1,), (1,)), ((), ()))
NN = (((1,), (0,)), ((), ()))
VMEM_SMALL = 16 * 1024 * 1024
VMEM_LARGE = 48 * 1024 * 1024
CHUNK = 512
STEP = 2
FRAME = 16
WIDE = 24
TN = (((0,), (0,)), ((), ()))


def split(x):
    high = x.astype(BF16)
    return high, (x - high.astype(F32)).astype(BF16)


def times(x, high, low, dims):
    count = x.shape[0]
    xh, xl = split(x)
    both = lax.dot_general(
        jnp.concatenate([xh, xl], axis=0), high, dims, preferred_element_type=F32
    )
    return both[:count] + both[count:] + lax.dot_general(xh, low, dims, preferred_element_type=F32)


def exact(x, y, dims=NN):
    return lax.dot_general(x, y, dims, precision=HIGHEST, preferred_element_type=F32)


def near(x, y, dims=NN):
    xh, xl = split(x)
    yh, yl = split(y)
    (left,), (right,) = dims[0]
    return lax.dot_general(
        jnp.concatenate([xh, xh, xl], axis=left),
        jnp.concatenate([yh, yl, yh], axis=right),
        dims,
        preferred_element_type=F32,
    )


def call(kernel, outs, n_in, smem=(), raw=(), raw_out=False, scratch=(), bytes_moved=None, large=False):
    def spec(i):
        if i in raw:
            return pl.BlockSpec(memory_space=pltpu.HBM)
        return pl.BlockSpec(memory_space=pltpu.SMEM if i in smem else pltpu.VMEM)

    return pl.pallas_call(
        kernel,
        out_shape=outs,
        in_specs=[spec(i) for i in range(n_in)],
        out_specs=[
            pl.BlockSpec(memory_space=pltpu.HBM if raw_out else pltpu.VMEM) for _ in outs
        ],
        scratch_shapes=list(scratch),
        cost_estimate=bytes_moved
        and pl.CostEstimate(flops=0, transcendentals=0, bytes_accessed=bytes_moved),
        compiler_params=pltpu.CompilerParams(vmem_limit_bytes=VMEM_LARGE if large else VMEM_SMALL),
    )


def shape(*dims):
    return jax.ShapeDtypeStruct(dims, F32)


def place_of(rows_ref, odd, j):
    side = jnp.where(odd == 1, j // IFB, 1 - j // IFB)
    return rows_ref[0, side, j % IFB]


def load_blocks(blocks_hbm, high_ref, low_ref, chunk_ref, sems):
    chunks = [
        pltpu.make_async_copy(
            blocks_hbm.at[:, :, pl.ds(CHUNK * t, CHUNK)], chunk_ref.at[t], sems.at[t]
        )
        for t in range(B * B // CHUNK)
    ]
    for copy in chunks:
        copy.start()
    filler = jnp.zeros((NB * KPAD - NB * (KNZ + 1), B * B), BF16)
    high_ref[NB * (KNZ + 1) :, :] = filler
    low_ref[NB * (KNZ + 1) :, :] = filler
    for t, copy in enumerate(chunks):
        copy.wait()
        padded = jnp.concatenate([chunk_ref[t], jnp.zeros((1, NB, CHUNK), F32)], axis=0)
        wh, wl = split(padded.reshape(NB * (KNZ + 1), CHUNK))
        cut = slice(CHUNK * t, CHUNK * (t + 1))
        high_ref[: NB * (KNZ + 1), cut] = wh
        low_ref[: NB * (KNZ + 1), cut] = wl


def assemble(rows_ref, columns_ref, wh_ref, wl_ref, after_ref, high_ref, low_ref):
    odd = lax.axis_index("sub") % 2
    column = columns_ref[...]
    place = jnp.where(
        (column < NB + IFB) == (odd == 1), column % IFB + NB, column % IFB + NB + IFB
    )
    for j in range(NB):
        place = jnp.where(column == place_of(rows_ref, odd, j), j, place)
    slot = lax.broadcasted_iota(jnp.int32, (KNZ, NB * KPAD), 0)
    entry = lax.broadcasted_iota(jnp.int32, (KNZ, NB * KPAD), 1)
    widen = jnp.where(entry // NB == slot, 1.0, 0.0).astype(BF16)
    wide = lax.dot_general(place.astype(F32).astype(BF16), widen, NN, preferred_element_type=F32)
    r = lax.broadcasted_iota(jnp.int32, (NE * NB, NB * KPAD), 0)
    q = lax.broadcasted_iota(jnp.int32, (NE * NB, NB * KPAD), 1)
    hit = (jnp.concatenate([wide] * NE, axis=0) == (r // NB).astype(F32)) & (r % NB == q % NB)
    onehot = jnp.where(hit, 1.0, 0.0).astype(BF16)
    first = lax.broadcasted_iota(jnp.int32, (NB, 128), 1) < B
    for t in range(B * B // CHUNK):
        cut = slice(CHUNK * t, CHUNK * (t + 1))
        dense = lax.dot_general(
            onehot, wh_ref[:, cut], NN, preferred_element_type=F32
        ) + lax.dot_general(onehot, wl_ref[:, cut], NN, preferred_element_type=F32)
        for m in range(NE // 2):
            for h in range(CHUNK // 128):
                lane = slice(128 * h, 128 * (h + 1))
                left = dense[16 * m : 16 * m + 8, lane]
                right = dense[16 * m + 8 : 16 * m + 16, lane]
                tile = jnp.concatenate(
                    [
                        jnp.where(first, left, pltpu.roll(right, B, 1)),
                        jnp.where(first, pltpu.roll(left, B, 1), right),
                    ],
                    axis=0,
                )
                th, tl = split(tile)
                at = NB * CHUNK // B * t + 16 * h
                high_ref[at : at + 16, 128 * m : 128 * (m + 1)] = th
                low_ref[at : at + 16, 128 * m : 128 * (m + 1)] = tl


def turn(high_ref, low_ref, high_t_ref, low_t_ref):
    high_t_ref[...] = high_ref[...].T
    low_t_ref[...] = low_ref[...].T


def sides(rows_ref, owner_ref, right_ref, scale_ref, after_ref, *rest, parts):
    basis_refs = rest[:parts]
    resid_ref, side_a_ref, side_b_ref, blk_ref = rest[parts:]
    odd = lax.axis_index("sub") % 2
    mine = lax.axis_index("rhs")
    cases = right_ref.shape[0]
    per = NCL // parts
    scale = jnp.broadcast_to(scale_ref[...], (8, OWN))
    unknown = lax.broadcasted_iota(jnp.int32, (FRAME, OWN), 0) + frame_start()
    coarse = jnp.zeros((FRAME, OWN), F32)
    for k in range(parts):
        for t in range(per):
            owner = owner_ref[0, ((mine + k) % parts) * per + t]
            coarse = coarse + jnp.where(unknown == owner, basis_refs[k][t : t + 1, :], 0.0)
    right = right_ref[...]
    live = cases + FRAME
    for n in range(NB):
        cut = slice(B * n, B * (n + 1))
        blk_ref[n, 0:cases, :] = right[:, cut]
        blk_ref[n, cases:live, :] = coarse[:, cut]
        blk_ref[n, live:, :] = scale[:, cut]
    for j in range(0, NB, 2):
        pair = jnp.concatenate(
            [blk_ref[place_of(rows_ref, odd, j)], blk_ref[place_of(rows_ref, odd, j + 1)]], axis=1
        )
        target = side_a_ref if j < IFB else side_b_ref
        at = B * (j % IFB)
        target[:cases, at : at + 2 * B] = pair[:cases] * pair[live : live + 1]
        target[cases:, at : at + 2 * B] = pair[cases:]
        resid_ref[:, B * j : B * (j + 2)] = pair[:cases]


def frame_start():
    return STEP * lax.axis_index("sub") - 6


def turned(rows, upper):
    up = pltpu.roll(rows, STEP, 0)
    down = pltpu.roll(rows, rows.shape[0] - STEP, 0)
    return jnp.where(upper, up, down)


def arrived(rows, upper):
    cases = rows.shape[0] - FRAME
    return jnp.concatenate([rows[:cases], turned(rows[cases:], upper)], axis=0)


def first_apply(
    a_ref, b_ref, ga_ref, gb_ref, high_ref, low_ref, high_t, low_t, strain_ref, send_a_ref, send_b_ref
):
    live = strain_ref.shape[0]
    odd = lax.axis_index("sub") % 2 == 1
    field = jnp.concatenate(
        [
            a_ref[:live, :],
            b_ref[:live, :],
            arrived(ga_ref[:live, :], jnp.logical_not(odd)),
            arrived(inside() * gb_ref[:live, :], odd),
        ],
        axis=1,
    )
    strain = times(field, high_t[...], low_t[...], NN)
    strain_ref[...] = strain
    back = times(strain, high_ref[...], low_ref[...], NN)
    send_a_ref[:live, :] = field[:, :EDGE] + back[:, :EDGE]
    send_a_ref[live:, :] = back[:, OWN : OWN + EDGE]
    send_b_ref[:live, :] = field[:, EDGE:OWN] + back[:, EDGE:OWN]
    send_b_ref[live:, :] = back[:, OWN + EDGE :]


def to_lanes(block, wide_ref):
    width = wide_ref.shape[1]
    wide_ref[...] = jnp.zeros_like(wide_ref)
    wide_ref[:, :FRAME] = block
    return pltpu.roll(wide_ref[...], (frame_start() + width) % width, 1)


def row_sums(value):
    return exact(jnp.ones((8, value.shape[1]), F32), value, NT)[0:1]


def first_sums(resid_ref, a_ref, b_ref, strain_ref, frame_ref, scalar_ref, wide_ref, *, ncoarse):
    live = strain_ref.shape[0]
    cases = live - FRAME
    own = jnp.concatenate([a_ref[:live, :], b_ref[:live, :]], axis=1)
    paired = jnp.concatenate([own, strain_ref[...]], axis=1)
    gram = exact(paired[cases:], paired, NT)
    resid = resid_ref[...]
    lead = paired[:cases]
    second = places(cases, ncoarse)[0]
    frame_ref[...] = jnp.zeros_like(frame_ref)
    frame_ref[:, 0:cases] = exact(own[cases:], resid, NT)
    frame_ref[:, cases : cases + ncoarse] = to_lanes(gram[:, cases:], wide_ref)[:, :ncoarse]
    frame_ref[:, second : second + cases] = gram[:, :cases]
    scalar_ref[...] = jnp.zeros_like(scalar_ref)
    scalar_ref[0:1, :] = row_sums(resid * own[:cases])
    scalar_ref[1:2, :] = row_sums(lead * lead)


def second_apply(
    a_ref,
    b_ref,
    ga_ref,
    gb_ref,
    own_a_ref,
    own_b_ref,
    got_a_ref,
    got_b_ref,
    high_t,
    low_t,
    frame_ref,
    scalar_ref,
    strain_ref,
    image_ref,
    scaled_ref,
    pay_ref,
    wide_ref,
    tall_ref,
    *,
    ncoarse,
):
    live = strain_ref.shape[0]
    cases = live - FRAME
    odd = lax.axis_index("sub") % 2 == 1
    even = jnp.logical_not(odd)
    inner = inside()
    image = jnp.concatenate(
        [
            own_a_ref[:live, :] + arrived(got_a_ref[live:, :], even),
            own_b_ref[:live, :] + inner * arrived(got_b_ref[live:, :], odd),
            own_a_ref[live:, :] + arrived(got_a_ref[:live, :], even),
            own_b_ref[live:, :] + arrived(got_b_ref[:live, :], odd),
        ],
        axis=1,
    )
    end = slice(live, live + 1)
    scale = jnp.concatenate(
        [a_ref[end, :], b_ref[end, :], ga_ref[end, :], inner * gb_ref[end, :]], axis=1
    )
    field = scale * image
    strain = times(field, high_t[...], low_t[...], NN)
    own = field[:, :OWN]
    first = image[:, :OWN]
    strain_ref[...] = strain
    image_ref[...] = first
    scaled_ref[...] = own
    paired = jnp.concatenate([own, strain], axis=1)
    blank = jnp.zeros((FRAME, ROWS), F32)
    left = jnp.concatenate(
        [paired[cases:], jnp.concatenate([first[cases:], blank], axis=1)], axis=0
    )
    both = near(left, paired, NT)
    gram, cross = both[:FRAME], both[FRAME:]
    lead = paired[:cases]
    width = cases + ncoarse
    tall_ref[...] = jnp.zeros_like(tall_ref)
    tall_ref[:FRAME, :] = frame_ref[...]
    second = places(cases, ncoarse)[0]
    for block, at, far in (
        (cross, width, width + cases),
        (gram, second + width, second + cases),
    ):
        tall_ref[:FRAME, at : at + cases] = block[:, :cases]
        tall_ref[:FRAME, far : far + ncoarse] = to_lanes(block[:, cases:], wide_ref)[:, :ncoarse]
    pay_ref[...] = pltpu.roll(tall_ref[...], (frame_start() + ncoarse) % ncoarse, 0)
    at = second + width + cases
    pay_ref[0:8, at : at + cases] = scalar_ref[...]
    pay_ref[2:3, at : at + cases] = row_sums(own[:cases] * first[:cases])
    pay_ref[3:4, at : at + cases] = row_sums(lead * lead)


def second_image(scaled_ref, strain_ref, high_ref, low_ref, own_ref, send_a_ref, send_b_ref):
    back = times(strain_ref[...], high_ref[...], low_ref[...], NN)
    own_ref[...] = scaled_ref[...] + back[:, :OWN]
    send_a_ref[...] = back[:, OWN : OWN + EDGE]
    send_b_ref[...] = back[:, OWN + EDGE :]


def window(value, start, count):
    rows = value.shape[0] + 32
    longer = jnp.concatenate([value, jnp.zeros((32, value.shape[1]), F32)], axis=0)
    return pltpu.roll(longer, (rows - start) % rows, 0)[:count]


def widened(own, got_a, got_b, even):
    gap = WIDE - FRAME

    def placed(rows, upper):
        none = jnp.zeros((gap, rows.shape[1]), F32)
        low = jnp.concatenate([rows, none], axis=0)
        return jnp.where(upper, pltpu.roll(low, 2 * STEP, 0), low)

    none = jnp.zeros((gap, own.shape[1]), F32)
    middle = pltpu.roll(jnp.concatenate([own, none], axis=0), STEP, 0)
    return middle + jnp.concatenate(
        [placed(got_a, even), placed(got_b, jnp.logical_not(even))], axis=1
    )


def settle(
    rows_ref,
    resid_ref,
    a_ref,
    b_ref,
    image_ref,
    scaled_ref,
    own_ref,
    got_a_ref,
    got_b_ref,
    all_ref,
    blk_ref,
):
    odd = lax.axis_index("sub") % 2
    live = own_ref.shape[0]
    cases = live - FRAME
    own = own_ref[...]
    got_a = got_a_ref[...]
    got_b = inside() * got_b_ref[...]
    image2 = own[:cases] + jnp.concatenate([got_a[:cases], got_b[:cases]], axis=1)
    coarse2 = widened(own[cases:], got_a[cases:], got_b[cases:], odd == 0)
    start = jnp.concatenate([a_ref[:live, :], b_ref[:live, :]], axis=1)
    scaled = scaled_ref[...]
    image = image_ref[...]
    at = 0
    for value in (
        resid_ref[...],
        start[:cases],
        scaled[:cases],
        image[:cases],
        image2,
        start[cases:],
        scaled[cases:],
        image[cases:],
        coarse2,
    ):
        end = at + value.shape[0]
        for j in range(NB):
            blk_ref[place_of(rows_ref, odd, j), at:end, :] = value[:, B * j : B * (j + 1)]
        at = end
    for m in range(0, NB, 2):
        all_ref[:, B * m : B * (m + 2)] = jnp.concatenate([blk_ref[m], blk_ref[m + 1]], axis=1)


def finish(inverse_ref, all_ref, *rest, ncoarse, n_pay):
    pays = rest[:n_pay]
    field_hbm, resid2_hbm, field_ref, resid2_ref, sems = rest[n_pay:]
    cases = field_ref.shape[0]
    width = cases + ncoarse
    pay = pays[0][...]
    for other in pays[1:]:
        pay = pay + other[...]

    def total(value):
        return jnp.sum(value, axis=0, keepdims=True)

    lead, full = places(cases, ncoarse)
    one, two = pay[:, :lead], pay[:, lead:]
    tile = slice(0, 128)
    u0, g12 = one[:, tile], two[:, tile]
    g14 = pltpu.roll(one, lead - width, 1)[:, tile]
    g34 = pltpu.roll(two, full - lead - width, 1)[:, tile]
    scalars = pltpu.roll(two[0:8], full - lead - width - cases, 1)[:, tile]
    r0d, g11, g13, g33 = (scalars[k : k + 1] for k in range(4))
    inverse = inverse_ref[...]
    y0 = near(inverse, u0)

    def picked(left, at, y):
        def none(rows):
            return [jnp.zeros((rows, 128), F32)] if rows else []

        rest = left.shape[1] - at - ncoarse
        return near(left, jnp.concatenate(none(at) + [y] + none(rest), axis=0))

    y22 = picked(one, cases, y0)
    y24 = picked(one, width + cases, y0)
    y44 = picked(two, cases, y0)
    rz0 = r0d + total(u0 * y0)
    pq0 = g11 + total(y0 * (2.0 * g12 + y22))
    alpha = rz0 / pq0
    u1 = u0 - alpha * (g12 + y22)
    y1 = near(inverse, u1)
    cross = g13 + total(y0 * g14)
    rz1 = (
        r0d
        - 2.0 * alpha * (g11 + total(y0 * g12))
        + alpha * alpha * (cross + total(y0 * (g14 + y24)))
        + total(u1 * y1)
    )
    beta = rz1 / rz0
    ahead = 1.0 + beta
    coarse = y1 + beta * y0
    c22 = picked(one, cases, y1) + beta * y22
    pq1 = (
        ahead * (ahead * g11 + 2.0 * total(coarse * g12) - 2.0 * alpha * cross)
        + total(coarse * (c22 - 2.0 * alpha * (g14 + y24)))
        + alpha * alpha * (g33 + total(y0 * (2.0 * g34 + y44)))
    )
    alpha1 = rz1 / pq1
    lower = alpha1 * alpha
    upper = alpha + alpha1 * ahead
    first = alpha * y0 + alpha1 * coarse
    second = -lower * y0
    begin = frame_start()
    first16 = window(first, begin, FRAME)
    weights = jnp.concatenate([first16, window(second, begin, FRAME)], axis=0)[:, :cases]
    weights2 = jnp.concatenate([first16, window(second, begin - STEP, WIDE)], axis=0)[:, :cases]
    row = lax.broadcasted_iota(jnp.int32, (8, 256), 0)
    half = lax.broadcasted_iota(jnp.int32, (8, 256), 1) // 128
    pair = jnp.concatenate([upper, lower, jnp.zeros((6, 128), F32)], axis=0)[:, :cases]
    columns = exact(pair, jnp.where(row == half, 1.0, 0.0), TN)
    upper = jnp.concatenate([columns[:, :128]] * (OWN // 128), axis=1)
    lower = jnp.concatenate([columns[:, 128:]] * (OWN // 128), axis=1)
    resid, fine, scaled, image, image2 = (
        all_ref[k * cases : (k + 1) * cases, :] for k in range(5)
    )
    at = 5 * cases
    field_ref[...] = upper * fine - lower * scaled + near(weights, all_ref[at : at + 2 * FRAME, :], TN)
    copies = [pltpu.make_async_copy(field_ref, field_hbm, sems.at[0])]
    copies[0].start()
    at += 2 * FRAME
    resid2_ref[...] = (
        resid
        - upper * image
        + lower * image2
        - near(weights2, all_ref[at : at + FRAME + WIDE, :], TN)
    )
    copies.append(pltpu.make_async_copy(resid2_ref, resid2_hbm, sems.at[1]))
    copies[1].start()
    for copy in copies:
        copy.wait()


def places(cases, ncoarse):
    both = cases + ncoarse
    lead = lanes_for(2 * both)
    return lead, lead + lanes_for(2 * cases + both)


def lanes_for(width):
    return -(-width // 128) * 128


def swap(x, steps, count):
    return [lax.ppermute(x, "sub", [(i, i ^ k) for i in range(count)]) for k in steps]


def rounds_of(count):
    rounds = []
    base = 1
    while base < count:
        turn = 1 if base > 1 else 0
        if base * 4 <= count:
            rounds.append((base, 2 * base + turn, 3 * base + turn))
            base *= 4
        else:
            rounds.append((base,))
            base *= 2
    return rounds


def across(a, b, count, parts):
    low = lax.ppermute(a, "sub", [(i, i ^ 1) for i in range(count)])
    inner = [(i, i + 1) for i in range(1, count - 1, 2)]
    pairs = [(i * parts + x, j * parts + x) for i, j in inner for x in range(parts)]
    ends = [(i * parts + x, i * parts + x + 1) for i in (0, count - 1) for x in range(0, parts - 1, 2)]
    pairs += ends
    return low, lax.ppermute(b, ("sub", "rhs"), pairs + [(j, i) for i, j in pairs])


def inside():
    place = lax.axis_index("sub")
    return jnp.where((place == 0) | (place == lax.axis_size("sub") - 1), 0.0, 1.0)


def body(
    right_side,
    stiffness_blocks,
    block_columns,
    interface_rows,
    corner_owner,
    corner_basis,
    jacobi_scale,
    coarse_inverse,
):
    cases = right_side.shape[0]
    ncoarse = coarse_inverse.shape[0]
    count = lax.axis_size("sub")
    parts = lax.axis_size("rhs")
    live = cases + FRAME
    rounds = rounds_of(count)
    run = functools.partial(call, large=ncoarse > 128)

    bases = [corner_basis] + [
        lax.ppermute(corner_basis, "rhs", [((i + k) % parts, i) for i in range(parts)])
        for k in range(1, parts)
    ]
    packed = jax.ShapeDtypeStruct((NB * KPAD, B * B), BF16)
    wh, wl = call(
        load_blocks,
        [packed, packed],
        1,
        raw=(0,),
        scratch=[
            pltpu.VMEM((B * B // CHUNK, KNZ, NB, CHUNK), F32),
            pltpu.SemaphoreType.DMA((B * B // CHUNK,)),
        ],
        bytes_moved=16 * 1024 * 1024,
        large=True,
    )(jnp.transpose(stiffness_blocks, (1, 0, 2)))
    resid, side_a, side_b = run(
        functools.partial(sides, parts=parts),
        [shape(cases, OWN), shape(live + 8, EDGE), shape(live + 8, EDGE)],
        5 + parts,
        smem=(0, 1),
        scratch=[pltpu.VMEM((NB, live + 8, B), F32)],
    )(interface_rows, corner_owner, right_side, jacobi_scale.reshape(1, OWN), wh, *bases)
    dense = jax.ShapeDtypeStruct((ROWS, EXT), BF16)
    high, low = run(assemble, [dense, dense], 5, smem=(0,))(
        interface_rows, block_columns, wh, wl, side_a
    )
    turned_g = jax.ShapeDtypeStruct((EXT, ROWS), BF16)
    high_t, low_t = run(turn, [turned_g, turned_g], 2)(high, low)
    ghost_a, ghost_b = across(side_a, side_b, count, parts)
    ends = (side_a, side_b, ghost_a, ghost_b)

    lanes = places(cases, ncoarse)[1]
    wide = pltpu.VMEM((FRAME, lanes_for(ncoarse)), F32)
    strain, own_a, own_b = run(
        first_apply, [shape(live, ROWS), shape(2 * live, EDGE), shape(2 * live, EDGE)], 8
    )(*ends, high, low, high_t, low_t)
    got_a, got_b = across(own_a, own_b, count, parts)
    frame, scalars = run(
        functools.partial(first_sums, ncoarse=ncoarse),
        [shape(FRAME, lanes), shape(8, cases)],
        4,
        scratch=[wide],
    )(resid, side_a, side_b, strain)
    strain, image, scaled, pay = run(
        functools.partial(second_apply, ncoarse=ncoarse),
        [shape(live, ROWS), shape(live, OWN), shape(live, OWN), shape(ncoarse, lanes)],
        12,
        scratch=[wide, pltpu.VMEM((ncoarse, lanes), F32)],
    )(*ends, own_a, own_b, got_a, got_b, high_t, low_t, frame, scalars)
    for steps in rounds[:-1]:
        pay = sum(swap(pay, steps, count), pay)
    pays = [pay] + swap(pay, rounds[-1], count)
    own, back_a, back_b = run(
        second_image, [shape(live, OWN), shape(live, EDGE), shape(live, EDGE)], 4
    )(scaled, strain, high, low)
    got_a, got_b = across(back_a, back_b, count, parts)
    height = 5 * cases + 3 * FRAME + WIDE
    (everything,) = run(
        settle,
        [shape(height, OWN)],
        9,
        smem=(0,),
        scratch=[pltpu.VMEM((NB, height, B), F32)],
    )(interface_rows, resid, side_a, side_b, image, scaled, own, got_a, got_b)
    return tuple(
        run(
            functools.partial(finish, ncoarse=ncoarse, n_pay=len(pays)),
            [shape(cases, OWN)] * 2,
            2 + len(pays),
            raw_out=True,
            scratch=[
                pltpu.VMEM((cases, OWN), F32),
                pltpu.VMEM((cases, OWN), F32),
                pltpu.SemaphoreType.DMA((2,)),
            ],
        )(coarse_inverse, everything, *pays)
    )


def solution(mesh):
    placed = (
        P("rhs", "sub"),
        P("sub", None, None),
        P("sub", None),
        P("sub", None, None),
        P("sub", None),
        P("rhs", "sub"),
        P("sub"),
        P(),
    )
    return jax.shard_map(
        body,
        mesh=mesh,
        in_specs=placed,
        out_specs=(P("rhs", "sub"), P("rhs", "sub")),
        check_vma=False,
    )
```

```python
import functools

import jax
import jax.numpy as jnp
from jax import lax
from jax.experimental import pallas as pl
from jax.experimental.pallas import tpu as pltpu
from jax.sharding import PartitionSpec as P

B = 64
KNZ = 27
IFB = 4
NCL = 8
NB = 2 * IFB
NE = NB + 2 * IFB
EDGE = IFB * B
OWN = NB * B
EXT = NE * B
ROWS = NB * B
KPAD = 32
F32 = jnp.float32
BF16 = jnp.bfloat16
HIGHEST = lax.Precision.HIGHEST
NT = (((1,), (1,)), ((), ()))
NN = (((1,), (0,)), ((), ()))
VMEM_SMALL = 16 * 1024 * 1024
VMEM_LARGE = 48 * 1024 * 1024
CHUNK = 512
STEP = 2
FRAME = 16
WIDE = 24
TN = (((0,), (0,)), ((), ()))


def split(x):
    high = x.astype(BF16)
    return high, (x - high.astype(F32)).astype(BF16)


def times(x, high, low, dims):
    count = x.shape[0]
    xh, xl = split(x)
    both = lax.dot_general(
        jnp.concatenate([xh, xl], axis=0), high, dims, preferred_element_type=F32
    )
    return both[:count] + both[count:] + lax.dot_general(xh, low, dims, preferred_element_type=F32)


def exact(x, y, dims=NN):
    return lax.dot_general(x, y, dims, precision=HIGHEST, preferred_element_type=F32)


def near(x, y, dims=NN):
    xh, xl = split(x)
    yh, yl = split(y)
    (left,), (right,) = dims[0]
    return lax.dot_general(
        jnp.concatenate([xh, xh, xl], axis=left),
        jnp.concatenate([yh, yl, yh], axis=right),
        dims,
        preferred_element_type=F32,
    )


def call(kernel, outs, n_in, smem=(), raw=(), raw_out=False, scratch=(), bytes_moved=None, large=False):
    def spec(i):
        if i in raw:
            return pl.BlockSpec(memory_space=pltpu.HBM)
        return pl.BlockSpec(memory_space=pltpu.SMEM if i in smem else pltpu.VMEM)

    return pl.pallas_call(
        kernel,
        out_shape=outs,
        in_specs=[spec(i) for i in range(n_in)],
        out_specs=[
            pl.BlockSpec(memory_space=pltpu.HBM if raw_out else pltpu.VMEM) for _ in outs
        ],
        scratch_shapes=list(scratch),
        cost_estimate=bytes_moved
        and pl.CostEstimate(flops=0, transcendentals=0, bytes_accessed=bytes_moved),
        compiler_params=pltpu.CompilerParams(vmem_limit_bytes=VMEM_LARGE if large else VMEM_SMALL),
    )


def shape(*dims):
    return jax.ShapeDtypeStruct(dims, F32)


def place_of(rows_ref, odd, j):
    side = jnp.where(odd == 1, j // IFB, 1 - j // IFB)
    return rows_ref[0, side, j % IFB]


def load_blocks(blocks_hbm, high_ref, low_ref, chunk_ref, sems):
    chunks = [
        pltpu.make_async_copy(
            blocks_hbm.at[:, :, pl.ds(CHUNK * t, CHUNK)], chunk_ref.at[t], sems.at[t]
        )
        for t in range(B * B // CHUNK)
    ]
    for copy in chunks:
        copy.start()
    filler = jnp.zeros((NB * KPAD - NB * (KNZ + 1), B * B), BF16)
    high_ref[NB * (KNZ + 1) :, :] = filler
    low_ref[NB * (KNZ + 1) :, :] = filler
    for t, copy in enumerate(chunks):
        copy.wait()
        padded = jnp.concatenate([chunk_ref[t], jnp.zeros((1, NB, CHUNK), F32)], axis=0)
        wh, wl = split(padded.reshape(NB * (KNZ + 1), CHUNK))
        cut = slice(CHUNK * t, CHUNK * (t + 1))
        high_ref[: NB * (KNZ + 1), cut] = wh
        low_ref[: NB * (KNZ + 1), cut] = wl


def assemble(rows_ref, columns_ref, wh_ref, wl_ref, after_ref, high_ref, low_ref):
    odd = lax.axis_index("sub") % 2
    column = columns_ref[...]
    place = jnp.where(
        (column < NB + IFB) == (odd == 1), column % IFB + NB, column % IFB + NB + IFB
    )
    for j in range(NB):
        place = jnp.where(column == place_of(rows_ref, odd, j), j, place)
    slot = lax.broadcasted_iota(jnp.int32, (KNZ, NB * KPAD), 0)
    entry = lax.broadcasted_iota(jnp.int32, (KNZ, NB * KPAD), 1)
    widen = jnp.where(entry // NB == slot, 1.0, 0.0).astype(BF16)
    wide = lax.dot_general(place.astype(F32).astype(BF16), widen, NN, preferred_element_type=F32)
    r = lax.broadcasted_iota(jnp.int32, (NE * NB, NB * KPAD), 0)
    q = lax.broadcasted_iota(jnp.int32, (NE * NB, NB * KPAD), 1)
    hit = (jnp.concatenate([wide] * NE, axis=0) == (r // NB).astype(F32)) & (r % NB == q % NB)
    onehot = jnp.where(hit, 1.0, 0.0).astype(BF16)
    first = lax.broadcasted_iota(jnp.int32, (NB, 128), 1) < B
    for t in range(B * B // CHUNK):
        cut = slice(CHUNK * t, CHUNK * (t + 1))
        dense = lax.dot_general(
            onehot, wh_ref[:, cut], NN, preferred_element_type=F32
        ) + lax.dot_general(onehot, wl_ref[:, cut], NN, preferred_element_type=F32)
        for m in range(NE // 2):
            for h in range(CHUNK // 128):
                lane = slice(128 * h, 128 * (h + 1))
                left = dense[16 * m : 16 * m + 8, lane]
                right = dense[16 * m + 8 : 16 * m + 16, lane]
                tile = jnp.concatenate(
                    [
                        jnp.where(first, left, pltpu.roll(right, B, 1)),
                        jnp.where(first, pltpu.roll(left, B, 1), right),
                    ],
                    axis=0,
                )
                th, tl = split(tile)
                at = NB * CHUNK // B * t + 16 * h
                high_ref[at : at + 16, 128 * m : 128 * (m + 1)] = th
                low_ref[at : at + 16, 128 * m : 128 * (m + 1)] = tl


def turn(high_ref, low_ref, high_t_ref, low_t_ref):
    high_t_ref[...] = high_ref[...].T
    low_t_ref[...] = low_ref[...].T


def sides(rows_ref, owner_ref, right_ref, scale_ref, after_ref, *rest, parts):
    basis_refs = rest[:parts]
    resid_ref, side_a_ref, side_b_ref, blk_ref = rest[parts:]
    odd = lax.axis_index("sub") % 2
    mine = lax.axis_index("rhs")
    cases = right_ref.shape[0]
    per = NCL // parts
    scale = jnp.broadcast_to(scale_ref[...], (8, OWN))
    unknown = lax.broadcasted_iota(jnp.int32, (FRAME, OWN), 0) + frame_start()
    coarse = jnp.zeros((FRAME, OWN), F32)
    for k in range(parts):
        for t in range(per):
            owner = owner_ref[0, ((mine + k) % parts) * per + t]
            coarse = coarse + jnp.where(unknown == owner, basis_refs[k][t : t + 1, :], 0.0)
    right = right_ref[...]
    live = cases + FRAME
    for n in range(NB):
        cut = slice(B * n, B * (n + 1))
        blk_ref[n, 0:cases, :] = right[:, cut]
        blk_ref[n, cases:live, :] = coarse[:, cut]
        blk_ref[n, live:, :] = scale[:, cut]
    for j in range(0, NB, 2):
        pair = jnp.concatenate(
            [blk_ref[place_of(rows_ref, odd, j)], blk_ref[place_of(rows_ref, odd, j + 1)]], axis=1
        )
        target = side_a_ref if j < IFB else side_b_ref
        at = B * (j % IFB)
        target[:cases, at : at + 2 * B] = pair[:cases] * pair[live : live + 1]
        target[cases:, at : at + 2 * B] = pair[cases:]
        resid_ref[:, B * j : B * (j + 2)] = pair[:cases]


def frame_start():
    return STEP * lax.axis_index("sub") - 6


def turned(rows, upper):
    up = pltpu.roll(rows, STEP, 0)
    down = pltpu.roll(rows, rows.shape[0] - STEP, 0)
    return jnp.where(upper, up, down)


def arrived(rows, upper):
    cases = rows.shape[0] - FRAME
    return jnp.concatenate([rows[:cases], turned(rows[cases:], upper)], axis=0)


def first_apply(
    a_ref, b_ref, ga_ref, gb_ref, high_ref, low_ref, high_t, low_t, strain_ref, send_a_ref, send_b_ref
):
    live = strain_ref.shape[0]
    odd = lax.axis_index("sub") % 2 == 1
    field = jnp.concatenate(
        [
            a_ref[:live, :],
            b_ref[:live, :],
            arrived(ga_ref[:live, :], jnp.logical_not(odd)),
            arrived(inside() * gb_ref[:live, :], odd),
        ],
        axis=1,
    )
    strain = times(field, high_t[...], low_t[...], NN)
    strain_ref[...] = strain
    back = times(strain, high_ref[...], low_ref[...], NN)
    send_a_ref[:live, :] = field[:, :EDGE] + back[:, :EDGE]
    send_a_ref[live:, :] = back[:, OWN : OWN + EDGE]
    send_b_ref[:live, :] = field[:, EDGE:OWN] + back[:, EDGE:OWN]
    send_b_ref[live:, :] = back[:, OWN + EDGE :]


def to_lanes(block, wide_ref):
    width = wide_ref.shape[1]
    wide_ref[...] = jnp.zeros_like(wide_ref)
    wide_ref[:, :FRAME] = block
    return pltpu.roll(wide_ref[...], (frame_start() + width) % width, 1)


def row_sums(value):
    return exact(jnp.ones((8, value.shape[1]), F32), value, NT)[0:1]


def first_sums(resid_ref, a_ref, b_ref, strain_ref, frame_ref, scalar_ref, wide_ref, *, ncoarse):
    live = strain_ref.shape[0]
    cases = live - FRAME
    own = jnp.concatenate([a_ref[:live, :], b_ref[:live, :]], axis=1)
    paired = jnp.concatenate([own, strain_ref[...]], axis=1)
    gram = exact(paired[cases:], paired, NT)
    resid = resid_ref[...]
    lead = paired[:cases]
    second = places(cases, ncoarse)[0]
    frame_ref[...] = jnp.zeros_like(frame_ref)
    frame_ref[:, 0:cases] = exact(own[cases:], resid, NT)
    frame_ref[:, cases : cases + ncoarse] = to_lanes(gram[:, cases:], wide_ref)[:, :ncoarse]
    frame_ref[:, second : second + cases] = gram[:, :cases]
    scalar_ref[...] = jnp.zeros_like(scalar_ref)
    scalar_ref[0:1, :] = row_sums(resid * own[:cases])
    scalar_ref[1:2, :] = row_sums(lead * lead)


def second_apply(
    a_ref,
    b_ref,
    ga_ref,
    gb_ref,
    own_a_ref,
    own_b_ref,
    got_a_ref,
    got_b_ref,
    high_t,
    low_t,
    frame_ref,
    scalar_ref,
    strain_ref,
    image_ref,
    scaled_ref,
    pay_ref,
    wide_ref,
    tall_ref,
    *,
    ncoarse,
):
    live = strain_ref.shape[0]
    cases = live - FRAME
    odd = lax.axis_index("sub") % 2 == 1
    even = jnp.logical_not(odd)
    inner = inside()
    image = jnp.concatenate(
        [
            own_a_ref[:live, :] + arrived(got_a_ref[live:, :], even),
            own_b_ref[:live, :] + inner * arrived(got_b_ref[live:, :], odd),
            own_a_ref[live:, :] + arrived(got_a_ref[:live, :], even),
            own_b_ref[live:, :] + arrived(got_b_ref[:live, :], odd),
        ],
        axis=1,
    )
    end = slice(live, live + 1)
    scale = jnp.concatenate(
        [a_ref[end, :], b_ref[end, :], ga_ref[end, :], inner * gb_ref[end, :]], axis=1
    )
    field = scale * image
    strain = times(field, high_t[...], low_t[...], NN)
    own = field[:, :OWN]
    first = image[:, :OWN]
    strain_ref[...] = strain
    image_ref[...] = first
    scaled_ref[...] = own
    paired = jnp.concatenate([own, strain], axis=1)
    blank = jnp.zeros((FRAME, ROWS), F32)
    left = jnp.concatenate(
        [paired[cases:], jnp.concatenate([first[cases:], blank], axis=1)], axis=0
    )
    both = near(left, paired, NT)
    gram, cross = both[:FRAME], both[FRAME:]
    lead = paired[:cases]
    width = cases + ncoarse
    tall_ref[...] = jnp.zeros_like(tall_ref)
    tall_ref[:FRAME, :] = frame_ref[...]
    second = places(cases, ncoarse)[0]
    for block, at, far in (
        (cross, width, width + cases),
        (gram, second + width, second + cases),
    ):
        tall_ref[:FRAME, at : at + cases] = block[:, :cases]
        tall_ref[:FRAME, far : far + ncoarse] = to_lanes(block[:, cases:], wide_ref)[:, :ncoarse]
    pay_ref[...] = pltpu.roll(tall_ref[...], (frame_start() + ncoarse) % ncoarse, 0)
    at = second + width + cases
    pay_ref[0:8, at : at + cases] = scalar_ref[...]
    pay_ref[2:3, at : at + cases] = row_sums(own[:cases] * first[:cases])
    pay_ref[3:4, at : at + cases] = row_sums(lead * lead)


def second_image(scaled_ref, strain_ref, high_ref, low_ref, own_ref, send_a_ref, send_b_ref):
    back = times(strain_ref[...], high_ref[...], low_ref[...], NN)
    own_ref[...] = scaled_ref[...] + back[:, :OWN]
    send_a_ref[...] = back[:, OWN : OWN + EDGE]
    send_b_ref[...] = back[:, OWN + EDGE :]


def window(value, start, count):
    rows = value.shape[0] + 32
    longer = jnp.concatenate([value, jnp.zeros((32, value.shape[1]), F32)], axis=0)
    return pltpu.roll(longer, (rows - start) % rows, 0)[:count]


def widened(own, got_a, got_b, even):
    gap = WIDE - FRAME

    def placed(rows, upper):
        none = jnp.zeros((gap, rows.shape[1]), F32)
        low = jnp.concatenate([rows, none], axis=0)
        return jnp.where(upper, pltpu.roll(low, 2 * STEP, 0), low)

    none = jnp.zeros((gap, own.shape[1]), F32)
    middle = pltpu.roll(jnp.concatenate([own, none], axis=0), STEP, 0)
    return middle + jnp.concatenate(
        [placed(got_a, even), placed(got_b, jnp.logical_not(even))], axis=1
    )


def settle(
    rows_ref,
    resid_ref,
    a_ref,
    b_ref,
    image_ref,
    scaled_ref,
    own_ref,
    got_a_ref,
    got_b_ref,
    all_ref,
    blk_ref,
):
    odd = lax.axis_index("sub") % 2
    live = own_ref.shape[0]
    cases = live - FRAME
    own = own_ref[...]
    got_a = got_a_ref[...]
    got_b = inside() * got_b_ref[...]
    image2 = own[:cases] + jnp.concatenate([got_a[:cases], got_b[:cases]], axis=1)
    coarse2 = widened(own[cases:], got_a[cases:], got_b[cases:], odd == 0)
    start = jnp.concatenate([a_ref[:live, :], b_ref[:live, :]], axis=1)
    scaled = scaled_ref[...]
    image = image_ref[...]
    at = 0
    for value in (
        resid_ref[...],
        start[:cases],
        scaled[:cases],
        image[:cases],
        image2,
        start[cases:],
        scaled[cases:],
        image[cases:],
        coarse2,
    ):
        end = at + value.shape[0]
        for j in range(NB):
            blk_ref[place_of(rows_ref, odd, j), at:end, :] = value[:, B * j : B * (j + 1)]
        at = end
    for m in range(0, NB, 2):
        all_ref[:, B * m : B * (m + 2)] = jnp.concatenate([blk_ref[m], blk_ref[m + 1]], axis=1)


def finish(inverse_ref, all_ref, *rest, ncoarse, n_pay):
    pays = rest[:n_pay]
    field_hbm, resid2_hbm, field_ref, resid2_ref, sems = rest[n_pay:]
    cases = field_ref.shape[0]
    width = cases + ncoarse
    pay = pays[0][...]
    for other in pays[1:]:
        pay = pay + other[...]

    def total(value):
        return jnp.sum(value, axis=0, keepdims=True)

    lead, full = places(cases, ncoarse)
    one, two = pay[:, :lead], pay[:, lead:]
    tile = slice(0, 128)
    u0, g12 = one[:, tile], two[:, tile]
    g14 = pltpu.roll(one, lead - width, 1)[:, tile]
    g34 = pltpu.roll(two, full - lead - width, 1)[:, tile]
    scalars = pltpu.roll(two[0:8], full - lead - width - cases, 1)[:, tile]
    r0d, g11, g13, g33 = (scalars[k : k + 1] for k in range(4))
    inverse = inverse_ref[...]
    y0 = near(inverse, u0)

    def picked(left, at, y):
        def none(rows):
            return [jnp.zeros((rows, 128), F32)] if rows else []

        rest = left.shape[1] - at - ncoarse
        return near(left, jnp.concatenate(none(at) + [y] + none(rest), axis=0))

    y22 = picked(one, cases, y0)
    y24 = picked(one, width + cases, y0)
    y44 = picked(two, cases, y0)
    rz0 = r0d + total(u0 * y0)
    pq0 = g11 + total(y0 * (2.0 * g12 + y22))
    alpha = rz0 / pq0
    u1 = u0 - alpha * (g12 + y22)
    y1 = near(inverse, u1)
    cross = g13 + total(y0 * g14)
    rz1 = (
        r0d
        - 2.0 * alpha * (g11 + total(y0 * g12))
        + alpha * alpha * (cross + total(y0 * (g14 + y24)))
        + total(u1 * y1)
    )
    beta = rz1 / rz0
    ahead = 1.0 + beta
    coarse = y1 + beta * y0
    c22 = picked(one, cases, y1) + beta * y22
    pq1 = (
        ahead * (ahead * g11 + 2.0 * total(coarse * g12) - 2.0 * alpha * cross)
        + total(coarse * (c22 - 2.0 * alpha * (g14 + y24)))
        + alpha * alpha * (g33 + total(y0 * (2.0 * g34 + y44)))
    )
    alpha1 = rz1 / pq1
    lower = alpha1 * alpha
    upper = alpha + alpha1 * ahead
    first = alpha * y0 + alpha1 * coarse
    second = -lower * y0
    begin = frame_start()
    first16 = window(first, begin, FRAME)
    weights = jnp.concatenate([first16, window(second, begin, FRAME)], axis=0)[:, :cases]
    weights2 = jnp.concatenate([first16, window(second, begin - STEP, WIDE)], axis=0)[:, :cases]
    row = lax.broadcasted_iota(jnp.int32, (8, 256), 0)
    half = lax.broadcasted_iota(jnp.int32, (8, 256), 1) // 128
    pair = jnp.concatenate([upper, lower, jnp.zeros((6, 128), F32)], axis=0)[:, :cases]
    columns = exact(pair, jnp.where(row == half, 1.0, 0.0), TN)
    upper = jnp.concatenate([columns[:, :128]] * (OWN // 128), axis=1)
    lower = jnp.concatenate([columns[:, 128:]] * (OWN // 128), axis=1)
    resid, fine, scaled, image, image2 = (
        all_ref[k * cases : (k + 1) * cases, :] for k in range(5)
    )
    at = 5 * cases
    field_ref[...] = upper * fine - lower * scaled + near(weights, all_ref[at : at + 2 * FRAME, :], TN)
    copies = [pltpu.make_async_copy(field_ref, field_hbm, sems.at[0])]
    copies[0].start()
    at += 2 * FRAME
    resid2_ref[...] = (
        resid
        - upper * image
        + lower * image2
        - near(weights2, all_ref[at : at + FRAME + WIDE, :], TN)
    )
    copies.append(pltpu.make_async_copy(resid2_ref, resid2_hbm, sems.at[1]))
    copies[1].start()
    for copy in copies:
        copy.wait()


def places(cases, ncoarse):
    both = cases + ncoarse
    lead = lanes_for(2 * both)
    return lead, lead + lanes_for(2 * cases + both)


def lanes_for(width):
    return -(-width // 128) * 128


def swap(x, steps, count):
    return [lax.ppermute(x, "sub", [(i, i ^ k) for i in range(count)]) for k in steps]


def rounds_of(count):
    rounds = []
    base = 1
    while base < count:
        if base * 4 <= count:
            rounds.append((base + 1, 2 * base + 1, 3 * base + 1) if base > 1 else (1, 3, 2))
            base *= 4
        else:
            rounds.append((base,))
            base *= 2
    return rounds


def across(a, b, count, parts):
    low = lax.ppermute(a, "sub", [(i, i ^ 1) for i in range(count)])
    inner = [(i, i + 1) for i in range(1, count - 1, 2)]
    pairs = [(i * parts + x, j * parts + x) for i, j in inner for x in range(parts)]
    ends = [(i * parts + x, i * parts + x + 1) for i in (0, count - 1) for x in range(0, parts - 1, 2)]
    pairs += ends
    return low, lax.ppermute(b, ("sub", "rhs"), pairs + [(j, i) for i, j in pairs])


def inside():
    place = lax.axis_index("sub")
    return jnp.where((place == 0) | (place == lax.axis_size("sub") - 1), 0.0, 1.0)


def body(
    right_side,
    stiffness_blocks,
    block_columns,
    interface_rows,
    corner_owner,
    corner_basis,
    jacobi_scale,
    coarse_inverse,
):
    cases = right_side.shape[0]
    ncoarse = coarse_inverse.shape[0]
    count = lax.axis_size("sub")
    parts = lax.axis_size("rhs")
    live = cases + FRAME
    rounds = rounds_of(count)
    run = functools.partial(call, large=ncoarse > 128)

    bases = [corner_basis] + [
        lax.ppermute(corner_basis, "rhs", [((i + k) % parts, i) for i in range(parts)])
        for k in range(1, parts)
    ]
    packed = jax.ShapeDtypeStruct((NB * KPAD, B * B), BF16)
    wh, wl = call(
        load_blocks,
        [packed, packed],
        1,
        raw=(0,),
        scratch=[
            pltpu.VMEM((B * B // CHUNK, KNZ, NB, CHUNK), F32),
            pltpu.SemaphoreType.DMA((B * B // CHUNK,)),
        ],
        bytes_moved=16 * 1024 * 1024,
        large=True,
    )(jnp.transpose(stiffness_blocks, (1, 0, 2)))
    resid, side_a, side_b = run(
        functools.partial(sides, parts=parts),
        [shape(cases, OWN), shape(live + 8, EDGE), shape(live + 8, EDGE)],
        5 + parts,
        smem=(0, 1),
        scratch=[pltpu.VMEM((NB, live + 8, B), F32)],
    )(interface_rows, corner_owner, right_side, jacobi_scale.reshape(1, OWN), wh, *bases)
    dense = jax.ShapeDtypeStruct((ROWS, EXT), BF16)
    high, low = run(assemble, [dense, dense], 5, smem=(0,))(
        interface_rows, block_columns, wh, wl, side_a
    )
    turned_g = jax.ShapeDtypeStruct((EXT, ROWS), BF16)
    high_t, low_t = run(turn, [turned_g, turned_g], 2)(high, low)
    ghost_a, ghost_b = across(side_a, side_b, count, parts)
    ends = (side_a, side_b, ghost_a, ghost_b)

    lanes = places(cases, ncoarse)[1]
    wide = pltpu.VMEM((FRAME, lanes_for(ncoarse)), F32)
    strain, own_a, own_b = run(
        first_apply, [shape(live, ROWS), shape(2 * live, EDGE), shape(2 * live, EDGE)], 8
    )(*ends, high, low, high_t, low_t)
    got_a, got_b = across(own_a, own_b, count, parts)
    frame, scalars = run(
        functools.partial(first_sums, ncoarse=ncoarse),
        [shape(FRAME, lanes), shape(8, cases)],
        4,
        scratch=[wide],
    )(resid, side_a, side_b, strain)
    strain, image, scaled, pay = run(
        functools.partial(second_apply, ncoarse=ncoarse),
        [shape(live, ROWS), shape(live, OWN), shape(live, OWN), shape(ncoarse, lanes)],
        12,
        scratch=[wide, pltpu.VMEM((ncoarse, lanes), F32)],
    )(*ends, own_a, own_b, got_a, got_b, high_t, low_t, frame, scalars)
    for steps in rounds[:-1]:
        pay = sum(swap(pay, steps, count), pay)
    pays = [pay] + swap(pay, rounds[-1], count)
    own, back_a, back_b = run(
        second_image, [shape(live, OWN), shape(live, EDGE), shape(live, EDGE)], 4
    )(scaled, strain, high, low)
    got_a, got_b = across(back_a, back_b, count, parts)
    height = 5 * cases + 3 * FRAME + WIDE
    (everything,) = run(
        settle,
        [shape(height, OWN)],
        9,
        smem=(0,),
        scratch=[pltpu.VMEM((NB, height, B), F32)],
    )(interface_rows, resid, side_a, side_b, image, scaled, own, got_a, got_b)
    return tuple(
        run(
            functools.partial(finish, ncoarse=ncoarse, n_pay=len(pays)),
            [shape(cases, OWN)] * 2,
            2 + len(pays),
            raw_out=True,
            scratch=[
                pltpu.VMEM((cases, OWN), F32),
                pltpu.VMEM((cases, OWN), F32),
                pltpu.SemaphoreType.DMA((2,)),
            ],
        )(coarse_inverse, everything, *pays)
    )


def solution(mesh):
    placed = (
        P("rhs", "sub"),
        P("sub", None, None),
        P("sub", None),
        P("sub", None, None),
        P("sub", None),
        P("rhs", "sub"),
        P("sub"),
        P(),
    )
    return jax.shard_map(
        body,
        mesh=mesh,
        in_specs=placed,
        out_specs=(P("rhs", "sub"), P("rhs", "sub")),
        check_vma=False,
    )
```
